256 devices in a mesh: space: 32 (over x, z), rep: 8 (over y, core).
Axes of the slice: x: 4, y: 4, z: 8, core: 2. Of those that a mesh axis runs over, the one named last changes fastest.
Arguments:
- stem_input: bfloat16 [8, 128, 512, 256], P('rep', 'space'), may hold values from -6 to 6
- stem_preact: bfloat16 [8, 64, 256, 256], P('rep', 'space'), may hold values from -6 to 6
- deep_cotangent: bfloat16 [8, 64, 256, 1024], P('rep', None, 'space'), may hold values from -6 to 6
- tissue_tiles: int32 [8], P('rep'), may hold values from 1 to 64
- conv_weight: bfloat16 [3, 3, 256, 256], replicated, may hold values from -0.125 to 0.125
- expand_weight: bfloat16 [256, 1024], replicated, may hold values from -0.1875 to 0.1875
Outputs:
- grad_input: bfloat16 [8, 128, 512, 256], P('rep', 'space')
- grad_conv: float32 [3, 3, 256, 256], replicated
- grad_expand: float32 [256, 1024], replicated
The draws below stay inside these ranges and needn't reach their ends.
All inputs are finite; a program needn't handle non-finite values.
Results may differ from the reference program's by a relative error of at most 0.001.
The reference program's roundings to bfloat16 on the way (of `weighted`, `active`, `grad_hidden` and `grad_pre`) count: a program that leaves them out, or rounds other values in their place, can miss the bound.
Values may be sent and summed in bfloat16 or wider, within the bound.
No kernel may reach another device: no remote copies, remote signals or barrier semaphores. Data moves between devices by JAX's collectives and lax.ppermute only.
A program may use at most 128 MiB of HBM per device.

```python
import jax
import jax.numpy as jnp
from jax import lax

C = 256
CD = 1024
TILES = 64
COLS = 512
SAMPLES = 8
H0 = 128
H1 = 64
OUT_COLS = 256
N_REP = 8


def place_ends(entries, own_key, smallest, top_value):
    longest = entries.shape.index(max(entries.shape))
    spots = []
    for shift in (0, 1):
        where = [jax.random.randint(jax.random.fold_in(own_key, axis), (), 0, length) for axis, length in enumerate(entries.shape)]
        where[longest] = (where[longest] + shift) % entries.shape[longest]
        spots.append(tuple(where))
    return entries.at[spots[0]].set(smallest).at[spots[1]].set(top_value)


def with_spikes(entries, own_key, source, target, parts, factor):
    owner, partner = [(jnp.arange(entries.shape[axis_at]) // (entries.shape[axis_at] // parts)).reshape([-1 if axis == axis_at else 1 for axis in range(entries.ndim)]) for axis_at in (source, target)]
    chosen = jax.random.permutation(own_key, parts)[partner]
    strong = (owner == chosen) | (owner == (partner + parts // 2) % parts)
    return jnp.where(strong, factor * entries, entries)


def levels(rng, extent, shards, least, high):
    def one(axis_at, shards_of):
        heights = jax.random.uniform(jax.random.fold_in(jax.random.fold_in(rng, 6), axis_at), (shards_of,), jnp.float32, least / len(shards), high / len(shards))
        return jnp.repeat(jnp.exp(heights), extent[axis_at] // shards_of).reshape((-1,) + (1,) * (len(extent) - axis_at - 1))

    factor_of = one(*shards[0])
    for cut in shards[1:]:
        factor_of = factor_of * one(*cut)
    return factor_of


def normal_values(stream_key, dims, width, reach, cuts=(), dtype=jnp.bfloat16):
    drawn = jax.random.normal(stream_key, dims, jnp.float32) * width
    if len(cuts) > 0:
        drawn = levels(stream_key, dims, cuts, -0.22, 0.18) * drawn
    return jnp.clip(drawn, min=-reach, max=reach).astype(dtype)


def noise_with(stream_key, shape, spread, most, split, heavy, dtype=jnp.bfloat16):
    drawn = spread * jax.random.normal(stream_key, shape, jnp.float32)
    if split:
        drawn = drawn * levels(stream_key, shape, split, -0.22, 0.18)
    return jnp.clip(with_spikes(drawn, jax.random.fold_in(stream_key, 3), *heavy), -most, most).astype(dtype)


def setup_inputs(seed: int = 0) -> dict:
    keys = jax.random.split(jax.random.key(seed), 7)
    stem_input = normal_values(keys[0], (SAMPLES, H0, COLS, C), 1.0, 6.0, ((0, 8), (1, 32)))
    stem_preact = noise_with(keys[1], (SAMPLES, H1, OUT_COLS, C), 1.0, 6.0, ((0, 8), (1, 32)), (1, 3, 32, 2.75))
    deep_cotangent = noise_with(keys[2], (SAMPLES, H1, OUT_COLS, CD), 1.0, 6.0, ((0, 8), (2, 32)), (2, 3, 32, 2.75))
    tissue_tiles = place_ends(jax.random.randint(keys[3], (SAMPLES,), 1, TILES + 1), jax.random.fold_in(keys[3], 1), 1, TILES).astype(jnp.int32)
    conv_weight = normal_values(keys[4], (3, 3, C, C), (9 * C) ** -0.5, 0.125)
    expand_weight = normal_values(keys[5], (C, CD), CD ** -0.5, 0.1875)
    return dict(stem_input=stem_input, stem_preact=stem_preact, deep_cotangent=deep_cotangent, tissue_tiles=tissue_tiles, conv_weight=conv_weight, expand_weight=expand_weight)


def weight_taps(above, strip_rows, cotangent):
    samples_here, half_rows, width_out, channels_out = cotangent.shape
    zero_row = jnp.zeros_like(strip_rows[:, :1])
    padded = jnp.concatenate([above, strip_rows, zero_row], axis=1)
    zero_col = jnp.zeros_like(padded[:, :, :1])
    padded = jnp.concatenate([zero_col, padded, zero_col], axis=2)
    padded = padded.reshape(samples_here, half_rows + 1, 2, width_out + 1, 2, strip_rows.shape[3])
    blocks = []
    for row_tap in range(3):
        for col_tap in range(3):
            window = padded[:, row_tap // 2:row_tap // 2 + half_rows, row_tap % 2, col_tap // 2:col_tap // 2 + width_out, col_tap % 2, :]
            blocks.append(lax.dot_general(window, cotangent, (((0, 1, 2), (0, 1, 2)), ((), ())), preferred_element_type=jnp.float32))
    return jnp.stack(blocks, axis=1)

def input_grad(extended, conv_weight):
    samples_here, ext_rows, width_out, channels_out = extended.shape
    half_rows = ext_rows - 1
    tap_terms = lax.dot_general(extended, conv_weight, (((3,), (3,)), ((), ())), preferred_element_type=jnp.float32)
    accumulated = jnp.zeros((samples_here, half_rows + 1, 2, width_out + 1, 2, conv_weight.shape[2]), jnp.float32)
    for row_tap in range(3):
        if row_tap < 2:
            row_target, row_source, row_parity = (slice(0, half_rows + 1), slice(0, half_rows + 1), row_tap)
        else:
            row_target, row_source, row_parity = (slice(1, half_rows + 1), slice(0, half_rows), 0)
        for col_tap in range(3):
            if col_tap < 2:
                col_target, col_source, col_parity = (slice(0, width_out), slice(0, width_out), col_tap)
            else:
                col_target, col_source, col_parity = (slice(1, width_out + 1), slice(0, width_out), 0)
            accumulated = accumulated.at[:, row_target, row_parity, col_target, col_parity, :].add(tap_terms[:, row_source, col_source, row_tap, col_tap, :])
    accumulated = accumulated.reshape(samples_here, 2 * half_rows + 2, 2 * width_out + 2, conv_weight.shape[2])
    return accumulated[:, 1:2 * half_rows + 1, 1:2 * width_out + 1, :].astype(jnp.bfloat16)

def group_grads(stem_input, stem_preact, deep_cotangent, tissue_tiles, conv_weight, expand_weight):
    tile_share = tissue_tiles.astype(jnp.float32) / TILES
    weighted = (deep_cotangent.astype(jnp.float32) * tile_share[:, None, None, None]).astype(jnp.bfloat16)
    active = jnp.maximum(stem_preact, jnp.zeros_like(stem_preact))
    grad_hidden = lax.dot_general(weighted, expand_weight, (((3,), (1,)), ((), ())), preferred_element_type=jnp.float32).astype(jnp.bfloat16)
    grad_pre = jnp.where(stem_preact > 0, grad_hidden, jnp.zeros_like(grad_hidden))
    part_expand = lax.dot_general(active, weighted, (((0, 1, 2), (0, 1, 2)), ((), ())), preferred_element_type=jnp.float32)
    above = jnp.zeros_like(stem_input[:, :1])
    part_conv = weight_taps(above, stem_input, grad_pre)
    extended = jnp.concatenate([grad_pre, jnp.zeros_like(grad_pre[:, :1])], axis=1)
    grad_input = input_grad(extended, conv_weight)
    return (grad_input, part_conv, part_expand)

def reference(stem_input, stem_preact, deep_cotangent, tissue_tiles, conv_weight, expand_weight):
    groups = N_REP

    def regroup(stacked):
        return stacked.reshape((groups, stacked.shape[0] // groups) + stacked.shape[1:])

    def advance(running, members):
        conv_total, expand_total = running
        grad_part, part_conv, part_expand = group_grads(members[0], members[1], members[2], members[3], conv_weight, expand_weight)
        return ((conv_total + part_conv, expand_total + part_expand), grad_part)
    initial = (jnp.zeros((C, 9, C), jnp.float32), jnp.zeros((C, CD), jnp.float32))
    running, grad_parts = lax.scan(advance, initial, (regroup(stem_input), regroup(stem_preact), regroup(deep_cotangent), regroup(tissue_tiles)))
    grad_scale = float(SAMPLES * H1 * OUT_COLS) ** (-0.5)
    grad_input = grad_parts.reshape(stem_input.shape)
    grad_conv = (running[0] * grad_scale).reshape(C, 3, 3, C).transpose(1, 2, 0, 3)
    grad_expand = running[1] * grad_scale
    return (grad_input, grad_conv, grad_expand)
```

```python
import functools

import jax
import jax.numpy as jnp
from jax import lax
from jax.experimental import pallas as pl
from jax.experimental.pallas import tpu as pltpu
from jax.sharding import Mesh
from jax.sharding import PartitionSpec as P

TILES = 64
LANES = 128
SIZES = {"x": 4, "z": 8, "y": 4, "core": 2}
SPACE = ("x", "z")
REP = ("y", "core")
VMEM_BYTES = 48 * 1024 * 1024


def whole(*_):
    return pl.BlockSpec(memory_space=pltpu.VMEM)


def shifted(x, by):
    length = SIZES["x"] * SIZES["z"]
    pairs = [(i, i + by) for i in range(length) if 0 <= i + by < length]
    return lax.ppermute(x, SPACE, pairs)


def prepare_kernel(above_ref, x_ref, out_ref, wide):
    half = out_ref.shape[2]
    first = lax.broadcasted_iota(jnp.int32, (LANES, half), 1) == 0
    for row in range(5):
        source = above_ref[0] if row == 0 else x_ref[row - 1]
        for part in range(source.shape[1] // LANES):
            lanes = slice(part * LANES, (part + 1) * LANES)
            wide[...] = source[:, lanes].astype(jnp.float32)
            even = wide[pl.ds(0, half, stride=2), :].T
            odd = wide[pl.ds(1, half, stride=2), :].T
            late = jnp.where(first, 0.0, pltpu.roll(odd, 1, 1))
            out_ref[3 * row, lanes, :] = late.astype(jnp.bfloat16)
            out_ref[3 * row + 1, lanes, :] = even.astype(jnp.bfloat16)
            out_ref[3 * row + 2, lanes, :] = odd.astype(jnp.bfloat16)


def prepare(above, x):
    rows, cols, channels = x.shape
    return pl.pallas_call(
        prepare_kernel,
        out_shape=jax.ShapeDtypeStruct((15, channels, cols // 2), jnp.bfloat16),
        in_specs=[whole()] * 2,
        out_specs=whole(),
        scratch_shapes=[pltpu.VMEM((cols, LANES), jnp.float32)],
        compiler_params=pltpu.CompilerParams(vmem_limit_bytes=VMEM_BYTES),
        cost_estimate=pl.CostEstimate(flops=10**7, bytes_accessed=3 * 10**6, transcendentals=0),
        name="prepare",
    )(above, x)


def taps_kernel(blocks_ref, grad_ref, out_ref):
    for row_tap in range(3):
        for col_tap in range(3):
            total = None
            for i in range(2):
                term = jnp.dot(
                    blocks_ref[3 * (2 * i + row_tap) + col_tap],
                    grad_ref[i],
                    preferred_element_type=jnp.float32,
                )
                total = term if total is None else total + term
            out_ref[3 * row_tap + col_tap] = total


def taps(blocks, grad):
    channels = blocks.shape[1]
    return pl.pallas_call(
        taps_kernel,
        out_shape=jax.ShapeDtypeStruct((9, channels, grad.shape[2]), jnp.float32),
        in_specs=[whole()] * 2,
        out_specs=whole(),
        compiler_params=pltpu.CompilerParams(vmem_limit_bytes=VMEM_BYTES),
        cost_estimate=pl.CostEstimate(flops=604 * 10**6, bytes_accessed=5 * 10**6, transcendentals=0),
        name="taps",
    )(blocks, grad)


def input_kernel(grad_ref, below_ref, weight_ref, out_ref, wide):
    half = grad_ref.shape[1]
    last = lax.broadcasted_iota(jnp.int32, grad_ref.shape[1:], 0) == half - 1

    def early(g):
        moved = pltpu.roll(g.astype(jnp.float32), half - 1, 0)
        return jnp.where(last, 0.0, moved).astype(jnp.bfloat16)

    grads = [grad_ref[0], grad_ref[1], below_ref[0]]
    moved = [early(g) for g in grads]

    def times(g, row_tap, col_tap):
        return lax.dot_general(
            g,
            weight_ref[row_tap, col_tap],
            (((1,), (1,)), ((), ())),
            preferred_element_type=jnp.float32,
        )

    for row in range(4):
        i = row // 2
        terms = [(i, 1)] if row % 2 == 0 else [(i, 2), (i + 1, 0)]
        even = sum(times(grads[n], p, 1) for n, p in terms)
        odd = sum(times(grads[n], p, 2) + times(moved[n], p, 0) for n, p in terms)
        for part in range(even.shape[1] // LANES):
            lanes = slice(part * LANES, (part + 1) * LANES)
            wide[pl.ds(0, half, stride=2), :] = even[:, lanes]
            wide[pl.ds(1, half, stride=2), :] = odd[:, lanes]
            out_ref[row, :, lanes] = wide[...].astype(jnp.bfloat16)


def input_grad(grad, below, weight):
    rows, half, channels = grad.shape
    return pl.pallas_call(
        input_kernel,
        out_shape=jax.ShapeDtypeStruct((2 * rows, 2 * half, weight.shape[2]), jnp.bfloat16),
        in_specs=[whole()] * 3,
        out_specs=whole(),
        scratch_shapes=[pltpu.VMEM((2 * half, LANES), jnp.float32)],
        compiler_params=pltpu.CompilerParams(vmem_limit_bytes=VMEM_BYTES),
        cost_estimate=pl.CostEstimate(flops=604 * 10**6, bytes_accessed=3 * 10**6, transcendentals=0),
        name="input_grad",
    )(grad, below, weight)


def exchange(x, axis):
    return lax.all_to_all(x, axis, split_axis=0, concat_axis=0, tiled=True)


def place(axis, by=0):
    return (lax.axis_index(axis).astype(jnp.uint32) + jnp.uint32(by % SIZES[axis])) & jnp.uint32(SIZES[axis] - 1)


def pick(parts, index):
    zero = jnp.uint32(0)
    return lax.dynamic_slice(parts, (index, zero, zero), (1,) + parts.shape[1:])[0]


def put(parts, piece, index):
    zero = jnp.uint32(0)
    return lax.dynamic_update_slice(parts, piece[None], (index, zero, zero))


def rotated(x, axis, by):
    size = SIZES[axis]
    return lax.ppermute(x, axis, [(i, (i + by) % size) for i in range(size)])


def scatter_sum(x, axis):
    size = SIZES[axis]
    parts = exchange(x.reshape(size, x.shape[0] // size, x.shape[1]), axis)
    return jnp.sum(parts, axis=0)


def gather(x, axis):
    size = SIZES[axis]
    parts = exchange(jnp.broadcast_to(x[None], (size,) + x.shape), axis)
    return parts.reshape(size * x.shape[0], x.shape[1])


def scatter_sum_by_permutes(x, axis):
    size = SIZES[axis]
    parts = x.reshape(size, x.shape[0] // size, x.shape[1])
    arrived = [rotated(pick(parts, place(axis, by)), axis, by) for by in range(1, size)]
    return sum(arrived, pick(parts, place(axis)))


def gather_by_permutes(x, axis):
    size = SIZES[axis]
    out = jnp.zeros((size,) + x.shape, x.dtype)
    for by in range(size):
        piece = x if by == 0 else rotated(x, axis, by)
        out = put(out, piece, place(axis, -by))
    return out.reshape(size * x.shape[0], x.shape[1])


def core_sum(x):
    return scatter_sum_by_permutes(x, "core")


def core_gather(x):
    first = lax.axis_index("core") == 0
    got = lax.ppermute(x, "core", [(0, 1), (1, 0)])
    return jnp.where(first, x, got), jnp.where(first, got, x)


def total_sums(groups, orders, scale):
    parts = []
    for x, order in zip(groups, orders):
        x = core_sum(x)
        for axis in order:
            x = scatter_sum_by_permutes(x, axis)
        parts.append(x)
    lengths = [p.shape[0] for p in parts]
    rows = sum(lengths)
    padded = -(-rows // 64) * 64
    joined = jnp.concatenate(parts + [jnp.zeros((padded - rows, parts[0].shape[1]), jnp.float32)])
    joined = gather(scatter_sum(joined, "z") * scale, "z")
    out, start = [], 0
    for length, order in zip(lengths, orders):
        x = joined[start : start + length]
        start += length
        for axis in reversed(order):
            x = gather_by_permutes(x, axis)
        out.append(core_gather(x))
    return out


def body(stem_input, stem_preact, deep_cotangent, tissue_tiles, conv_weight, expand_weight):
    _, out_rows, out_cols, channels = stem_preact.shape
    _, all_rows, band, deep = deep_cotangent.shape
    devices = SIZES["x"] * SIZES["z"]
    preact = stem_preact[0]
    x = stem_input[0]
    tile_share = tissue_tiles.astype(jnp.float32) / TILES
    weighted = (deep_cotangent[0].astype(jnp.float32) * tile_share[:, None, None]).astype(jnp.bfloat16)
    weighted = weighted.reshape(all_rows * band, deep)
    hidden = lax.dot_general(
        weighted, expand_weight, (((1,), (1,)), ((), ())), preferred_element_type=jnp.float32
    ).astype(jnp.bfloat16)
    hidden = exchange(hidden.reshape(devices, out_rows * band, channels), SPACE)
    hidden = hidden.reshape(devices, out_rows, band, channels).transpose(1, 0, 2, 3)
    hidden = hidden.reshape(out_rows, out_cols, channels)
    grad = jnp.where(preact > 0, hidden, jnp.zeros_like(hidden))
    active = jnp.maximum(preact, jnp.zeros_like(preact))
    active = active.reshape(out_rows, devices, band, channels).transpose(1, 0, 2, 3)
    active = exchange(active.reshape(devices, out_rows * band, channels), SPACE)
    active = active.reshape(all_rows * band, channels)
    part_expand = lax.dot_general(
        active, weighted, (((0,), (0,)), ((), ())), preferred_element_type=jnp.float32
    )
    above = shifted(x[-1:], 1)
    below = shifted(grad[:1], -1)
    part_conv = taps(prepare(above, x), grad)
    grad_input = input_grad(grad, below, conv_weight)

    samples_all = stem_input.shape[0] * SIZES["y"] * SIZES["core"]
    scale = float(samples_all * all_rows * out_cols) ** (-0.5)
    columns = deep // channels
    expand_rows = jnp.concatenate(
        [part_expand[:, n * channels : (n + 1) * channels] for n in range(columns)]
    )
    first = part_conv[:6].reshape(6 * channels, channels)
    second = jnp.concatenate([part_conv[6:].reshape(3 * channels, channels), expand_rows])
    (first, second) = total_sums([first, second], [("y", "x"), ("x", "y")], scale)
    first, second = jnp.concatenate(first), jnp.concatenate(second)
    grad_conv = jnp.concatenate([first, second[: 3 * channels]]).reshape(3, 3, channels, channels)
    pieces = second[3 * channels :].reshape(columns, channels, channels)
    grad_expand = jnp.concatenate([pieces[n] for n in range(columns)], axis=1)
    return (grad_input[None], grad_conv, grad_expand)


def solution(mesh):
    fine = Mesh(
        mesh.devices.reshape(SIZES["x"], SIZES["z"], SIZES["y"], SIZES["core"]),
        ("x", "z", "y", "core"),
    )
    return jax.shard_map(
        body,
        mesh=fine,
        in_specs=(
            P(REP, SPACE, None, None),
            P(REP, SPACE, None, None),
            P(REP, None, SPACE, None),
            P(REP),
            P(),
            P(),
        ),
        out_specs=(P(REP, SPACE, None, None), P(), P()),
        check_vma=False,
    )
```

```python
import functools

import jax
import jax.numpy as jnp
from jax import lax
from jax.experimental import pallas as pl
from jax.experimental.pallas import tpu as pltpu
from jax.sharding import Mesh
from jax.sharding import PartitionSpec as P

TILES = 64
LANES = 128
SIZES = {"x": 4, "z": 8, "y": 4, "core": 2}
SPACE = ("x", "z")
REP = ("y", "core")
VMEM_BYTES = 48 * 1024 * 1024


def whole(*_):
    return pl.BlockSpec(memory_space=pltpu.VMEM)


def scalars():
    return pl.BlockSpec(memory_space=pltpu.SMEM)


def params():
    return pltpu.CompilerParams(vmem_limit_bytes=VMEM_BYTES)


def shifted(x, by):
    length = SIZES["x"] * SIZES["z"]
    pairs = [(i, i + by) for i in range(length) if 0 <= i + by < length]
    return lax.ppermute(x, SPACE, pairs)


def prepare_kernel(share_ref, x_ref, cotangent_ref, out_ref, weighted_ref, wide):
    half = out_ref.shape[2]
    first = lax.broadcasted_iota(jnp.int32, (LANES, half), 1) == 0
    for row in range(x_ref.shape[0]):
        for part in range(x_ref.shape[2] // LANES):
            lanes = slice(part * LANES, (part + 1) * LANES)
            wide[...] = x_ref[row, :, lanes].astype(jnp.float32)
            even = wide[pl.ds(0, half, stride=2), :].T
            odd = wide[pl.ds(1, half, stride=2), :].T
            late = jnp.where(first, 0.0, pltpu.roll(odd, 1, 1))
            out_ref[3 * row, lanes, :] = late.astype(jnp.bfloat16)
            out_ref[3 * row + 1, lanes, :] = even.astype(jnp.bfloat16)
            out_ref[3 * row + 2, lanes, :] = odd.astype(jnp.bfloat16)
    weighted_ref[...] = (cotangent_ref[...].astype(jnp.float32) * share_ref[0]).astype(jnp.bfloat16)


def prepare(share, x, cotangent):
    rows, cols, channels = x.shape
    return pl.pallas_call(
        prepare_kernel,
        out_shape=(
            jax.ShapeDtypeStruct((3 * rows, channels, cols // 2), jnp.bfloat16),
            jax.ShapeDtypeStruct(cotangent.shape, jnp.bfloat16),
        ),
        in_specs=[scalars(), whole(), whole()],
        out_specs=(whole(), whole()),
        scratch_shapes=[pltpu.VMEM((cols, LANES), jnp.float32)],
        compiler_params=params(),
        cost_estimate=pl.CostEstimate(flops=10**7, bytes_accessed=5 * 10**6, transcendentals=0),
        name="prepare",
    )(share, x, cotangent)


def half_taps(blocks_ref, grads, row_tap, col_tap, start):
    total = None
    for i, grad in enumerate(grads):
        row = 2 * i + row_tap - 1
        if 0 <= row < blocks_ref.shape[0] // 3:
            term = jnp.dot(
                blocks_ref[3 * row + col_tap, pl.ds(start, LANES), :],
                grad,
                preferred_element_type=jnp.float32,
            )
            total = term if total is None else total + term
    return total


def inner_kernel(core_ref, blocks_ref, grad_ref, own_ref, other_ref):
    grads = [grad_ref[0], grad_ref[1]]
    for out_ref, owner in ((other_ref, 1 - core_ref[0]), (own_ref, core_ref[0])):
        start = pl.multiple_of(owner * LANES, LANES)
        for row_tap in (1, 2):
            for col_tap in range(3):
                at = (3 * (row_tap - 1) + col_tap) * LANES
                out_ref[at : at + LANES, :] = half_taps(blocks_ref, grads, row_tap, col_tap, start)


def outer_kernel(core_ref, blocks_ref, grad_ref, below_ref, active_ref, weighted_ref, own_ref, other_ref, turned):
    channels = grad_ref.shape[2]
    grads = [grad_ref[0], grad_ref[1], below_ref[0]]
    turned[...] = active_ref[...].T
    for out_ref, owner in ((other_ref, 1 - core_ref[0]), (own_ref, core_ref[0])):
        start = pl.multiple_of(owner * LANES, LANES)
        for col_tap in range(3):
            at = col_tap * LANES
            out_ref[at : at + LANES, :] = half_taps(blocks_ref, grads, 0, col_tap, start)
        for n in range(weighted_ref.shape[1] // channels):
            at = (3 + n) * LANES
            out_ref[at : at + LANES, :] = jnp.dot(
                turned[pl.ds(start, LANES), :],
                weighted_ref[:, n * channels : (n + 1) * channels],
                preferred_element_type=jnp.float32,
            )


def halves(kernel, rows, core, *arrays, scratch=()):
    shape = jax.ShapeDtypeStruct((rows, 2 * LANES), jnp.float32)
    return pl.pallas_call(
        kernel,
        out_shape=(shape, shape),
        in_specs=[scalars()] + [whole()] * len(arrays),
        out_specs=(whole(), whole()),
        scratch_shapes=scratch,
        compiler_params=params(),
        cost_estimate=pl.CostEstimate(flops=400 * 10**6, bytes_accessed=4 * 10**6, transcendentals=0),
        name="halves",
    )(core, *arrays)


def input_kernel(grad_ref, below_ref, weight_ref, out_ref, wide):
    half = grad_ref.shape[1]
    last = lax.broadcasted_iota(jnp.int32, grad_ref.shape[1:], 0) == half - 1

    def early(g):
        moved = pltpu.roll(g.astype(jnp.float32), half - 1, 0)
        return jnp.where(last, 0.0, moved).astype(jnp.bfloat16)

    grads = [grad_ref[0], grad_ref[1], below_ref[0]]
    moved = [early(g) for g in grads]

    def times(g, row_tap, col_tap):
        return lax.dot_general(
            g,
            weight_ref[row_tap, col_tap],
            (((1,), (1,)), ((), ())),
            preferred_element_type=jnp.float32,
        )

    for row in range(4):
        i = row // 2
        terms = [(i, 1)] if row % 2 == 0 else [(i, 2), (i + 1, 0)]
        even = sum(times(grads[n], p, 1) for n, p in terms)
        odd = sum(times(grads[n], p, 2) + times(moved[n], p, 0) for n, p in terms)
        for part in range(even.shape[1] // LANES):
            lanes = slice(part * LANES, (part + 1) * LANES)
            wide[pl.ds(0, half, stride=2), :] = even[:, lanes]
            wide[pl.ds(1, half, stride=2), :] = odd[:, lanes]
            out_ref[row, :, lanes] = wide[...].astype(jnp.bfloat16)


def input_grad(grad, below, weight):
    rows, half, channels = grad.shape
    return pl.pallas_call(
        input_kernel,
        out_shape=jax.ShapeDtypeStruct((2 * rows, 2 * half, weight.shape[2]), jnp.bfloat16),
        in_specs=[whole()] * 3,
        out_specs=whole(),
        scratch_shapes=[pltpu.VMEM((2 * half, LANES), jnp.float32)],
        compiler_params=params(),
        cost_estimate=pl.CostEstimate(flops=604 * 10**6, bytes_accessed=3 * 10**6, transcendentals=0),
        name="input_grad",
    )(grad, below, weight)


def exchange(x, axis):
    return lax.all_to_all(x, axis, split_axis=0, concat_axis=0, tiled=True)


def place(axis, by=0):
    return (lax.axis_index(axis).astype(jnp.uint32) + jnp.uint32(by % SIZES[axis])) & jnp.uint32(SIZES[axis] - 1)


def pick(parts, index):
    zero = jnp.uint32(0)
    return lax.dynamic_slice(parts, (index, zero, zero), (1,) + parts.shape[1:])[0]


def put(parts, piece, index):
    zero = jnp.uint32(0)
    return lax.dynamic_update_slice(parts, piece[None], (index, zero, zero))


def rotated(x, axis, by):
    size = SIZES[axis]
    return lax.ppermute(x, axis, [(i, (i + by) % size) for i in range(size)])


def scatter_sum(x, axis):
    size = SIZES[axis]
    parts = x.reshape(size, x.shape[0] // size, x.shape[1])
    arrived = [rotated(pick(parts, place(axis, by)), axis, by) for by in range(1, size)]
    return sum(arrived, pick(parts, place(axis)))


def gather_pieces(x, axis):
    return [x] + [rotated(x, axis, by) for by in range(1, SIZES[axis])]


def gather(x, axis):
    out = jnp.zeros((SIZES[axis],) + x.shape, x.dtype)
    for by, piece in enumerate(gather_pieces(x, axis)):
        out = put(out, piece, place(axis, -by))
    return out.reshape(-1, x.shape[1])


def swapped(x, axis, bit):
    return lax.ppermute(x, axis, [(i, i ^ bit) for i in range(SIZES[axis])])


def sum_along_z(pair, scale):
    rows = max(p.shape[0] for p in pair)
    both = jnp.stack([jnp.pad(p, ((0, rows - p.shape[0]), (0, 0))) for p in pair])
    bit = place("z") & jnp.uint32(1)
    part = pick(both, bit) + swapped(pick(both, jnp.uint32(1) - bit), "z", 1)
    part = part + swapped(part, "z", 2)
    part = (part + swapped(part, "z", 4)) * scale
    got = swapped(part, "z", 1)
    even = bit == 0
    out = (jnp.where(even, part, got), jnp.where(even, got, part))
    return [o[: p.shape[0]] for o, p in zip(out, pair)]


def assemble_kernel(where_ref, *refs):
    groups, (conv_ref, expand_ref), scratch = (refs[:8], refs[8:16]), refs[16:18], refs[18:]
    channels = conv_ref.shape[2]
    core = where_ref[0]
    for n, (pieces, whole_ref) in enumerate(zip(groups, scratch)):
        for by in range(4):
            rows = pieces[by].shape[0]
            at = pl.multiple_of(((where_ref[1 + n] + 4 - by) & 3) * rows, 8)
            whole_ref[core, pl.ds(at, rows), :] = pieces[by][...]
            whole_ref[1 - core, pl.ds(at, rows), :] = pieces[4 + by][...]
    for half in range(2):
        lanes = slice(half * LANES, (half + 1) * LANES)
        for tap in range(6):
            conv_ref[3 + tap, lanes, :] = scratch[0][half, tap * LANES : (tap + 1) * LANES, :]
        for tap in range(3):
            conv_ref[tap, lanes, :] = scratch[1][half, tap * LANES : (tap + 1) * LANES, :]
        for n in range(expand_ref.shape[1] // channels):
            at = (3 + n) * LANES
            expand_ref[lanes, n * channels : (n + 1) * channels] = scratch[1][half, at : at + LANES, :]


def assemble(where, groups, channels, deep):
    refs = [piece for group in groups for piece in group]
    return pl.pallas_call(
        assemble_kernel,
        out_shape=(
            jax.ShapeDtypeStruct((9, channels, channels), jnp.float32),
            jax.ShapeDtypeStruct((channels, deep), jnp.float32),
        ),
        in_specs=[scalars()] + [whole()] * len(refs),
        out_specs=(whole(), whole()),
        scratch_shapes=[pltpu.VMEM((2, 4 * group[0].shape[0], channels), jnp.float32) for group in groups],
        compiler_params=params(),
        cost_estimate=pl.CostEstimate(flops=0, bytes_accessed=7 * 10**6, transcendentals=0),
        name="assemble",
    )(where, *refs)


def body(stem_input, stem_preact, deep_cotangent, tissue_tiles, conv_weight, expand_weight):
    _, out_rows, out_cols, channels = stem_preact.shape
    _, all_rows, band, deep = deep_cotangent.shape
    devices = SIZES["x"] * SIZES["z"]
    preact = stem_preact[0]
    cotangent = deep_cotangent[0].reshape(all_rows * band, deep)
    share = tissue_tiles.astype(jnp.float32) / TILES
    core = lax.axis_index("core").astype(jnp.int32)
    where = jnp.stack([core, lax.axis_index("y"), lax.axis_index("x")]).astype(jnp.int32)

    hidden = lax.dot_general(
        (cotangent.astype(jnp.float32) * share[:, None]).astype(jnp.bfloat16),
        expand_weight,
        (((1,), (1,)), ((), ())),
        preferred_element_type=jnp.float32,
    ).astype(jnp.bfloat16)
    active = jnp.maximum(preact, jnp.zeros_like(preact))
    active = active.reshape(out_rows, devices, band, channels).transpose(1, 0, 2, 3)
    chunk = out_rows * band
    sent = jnp.concatenate(
        [hidden.reshape(devices, chunk, channels), active.reshape(devices, chunk, channels)], axis=1
    )
    blocks, weighted = prepare(share, stem_input[0], cotangent)
    arrived = exchange(sent, SPACE)
    hidden = arrived[:, :chunk].reshape(devices, out_rows, band, channels).transpose(1, 0, 2, 3)
    hidden = hidden.reshape(out_rows, out_cols, channels)
    active = arrived[:, chunk:].reshape(all_rows * band, channels)
    grad = jnp.where(preact > 0, hidden, jnp.zeros_like(hidden))
    below = shifted(grad[:1], -1)

    own_inner, other_inner = halves(inner_kernel, 6 * LANES, where[:1], blocks, grad)
    own_outer, other_outer = halves(
        outer_kernel,
        3 * LANES + deep // 2,
        where[:1],
        blocks,
        grad,
        below,
        active,
        weighted,
        scratch=[pltpu.VMEM((channels, all_rows * band), jnp.bfloat16)],
    )
    grad_input = input_grad(grad, below, conv_weight)

    samples_all = stem_input.shape[0] * SIZES["y"] * SIZES["core"]
    scale = float(samples_all * all_rows * out_cols) ** (-0.5)
    inner = own_inner + swapped(other_inner, "core", 1)
    outer = own_outer + swapped(other_outer, "core", 1)
    inner = scatter_sum(scatter_sum(inner, "y"), "x")
    outer = scatter_sum(scatter_sum(outer, "x"), "y")
    inner, outer = sum_along_z([inner, outer], scale)
    inner = gather_pieces(gather(inner, "x"), "y")
    outer = gather_pieces(gather(outer, "y"), "x")
    groups = [pieces + [swapped(piece, "core", 1) for piece in pieces] for pieces in (inner, outer)]
    grad_conv, grad_expand = assemble(where, groups, channels, deep)
    return (grad_input[None], grad_conv.reshape(3, 3, channels, channels), grad_expand)


def solution(mesh):
    fine = Mesh(
        mesh.devices.reshape(SIZES["x"], SIZES["z"], SIZES["y"], SIZES["core"]),
        ("x", "z", "y", "core"),
    )
    return jax.shard_map(
        body,
        mesh=fine,
        in_specs=(
            P(REP, SPACE, None, None),
            P(REP, SPACE, None, None),
            P(REP, None, SPACE, None),
            P(REP),
            P(),
            P(),
        ),
        out_specs=(P(REP, SPACE, None, None), P(), P()),
        check_vma=False,
    )
```

```python
import functools

import jax
import jax.numpy as jnp
from jax import lax
from jax.experimental import pallas as pl
from jax.experimental.pallas import tpu as pltpu
from jax.sharding import Mesh
from jax.sharding import PartitionSpec as P

TILES = 64
LANES = 128
SIZES = {"x": 4, "z": 8, "y": 4, "core": 2}
SPACE = ("x", "z")
REP = ("y", "core")
VMEM_BYTES = 48 * 1024 * 1024


def whole(*_):
    return pl.BlockSpec(memory_space=pltpu.VMEM)


def scalars():
    return pl.BlockSpec(memory_space=pltpu.SMEM)


def params():
    return pltpu.CompilerParams(vmem_limit_bytes=VMEM_BYTES)


def shifted(x, by):
    length = SIZES["x"] * SIZES["z"]
    pairs = [(i, i + by) for i in range(length) if 0 <= i + by < length]
    return lax.ppermute(x, SPACE, pairs)


def prepare_kernel(share_ref, above_ref, x_ref, cotangent_ref, out_ref, weighted_ref, wide):
    half = out_ref.shape[2]
    first = lax.broadcasted_iota(jnp.int32, (LANES, half), 1) == 0
    for row in range(x_ref.shape[0] + 1):
        source = above_ref.at[0] if row == 0 else x_ref.at[row - 1]
        for part in range(x_ref.shape[2] // LANES):
            lanes = slice(part * LANES, (part + 1) * LANES)
            wide[...] = source[:, lanes].astype(jnp.float32)
            even = wide[pl.ds(0, half, stride=2), :].T
            odd = wide[pl.ds(1, half, stride=2), :].T
            late = jnp.where(first, 0.0, pltpu.roll(odd, 1, 1))
            out_ref[3 * row, lanes, :] = late.astype(jnp.bfloat16)
            out_ref[3 * row + 1, lanes, :] = even.astype(jnp.bfloat16)
            out_ref[3 * row + 2, lanes, :] = odd.astype(jnp.bfloat16)
    weighted_ref[...] = (cotangent_ref[...].astype(jnp.float32) * share_ref[0]).astype(jnp.bfloat16)


def prepare(share, above, x, cotangent):
    rows, cols, channels = x.shape
    return pl.pallas_call(
        prepare_kernel,
        out_shape=(
            jax.ShapeDtypeStruct((3 * rows + 3, channels, cols // 2), jnp.bfloat16),
            jax.ShapeDtypeStruct(cotangent.shape, jnp.bfloat16),
        ),
        in_specs=[scalars(), whole(), whole(), whole()],
        out_specs=(whole(), whole()),
        scratch_shapes=[pltpu.VMEM((cols, LANES), jnp.float32)],
        compiler_params=params(),
        cost_estimate=pl.CostEstimate(flops=10**7, bytes_accessed=5 * 10**6, transcendentals=0),
        name="prepare",
    )(share, above, x, cotangent)


def half_taps(blocks_ref, grad_ref, row_tap, col_tap, start):
    total = None
    for i in range(2):
        term = jnp.dot(
            blocks_ref[3 * (2 * i + row_tap) + col_tap, pl.ds(start, LANES), :],
            grad_ref[i],
            preferred_element_type=jnp.float32,
        )
        total = term if total is None else total + term
    return total


def inner_kernel(core_ref, blocks_ref, grad_ref, own_ref, other_ref):
    for out_ref, owner in ((other_ref, 1 - core_ref[0]), (own_ref, core_ref[0])):
        start = pl.multiple_of(owner * LANES, LANES)
        for row_tap in (1, 2):
            for col_tap in range(3):
                at = (3 * (row_tap - 1) + col_tap) * LANES
                out_ref[at : at + LANES, :] = half_taps(blocks_ref, grad_ref, row_tap, col_tap, start)


def outer_kernel(core_ref, blocks_ref, grad_ref, active_ref, weighted_ref, own_ref, other_ref, turned):
    channels = grad_ref.shape[2]
    turned[...] = active_ref[...].T
    for out_ref, owner in ((other_ref, 1 - core_ref[0]), (own_ref, core_ref[0])):
        start = pl.multiple_of(owner * LANES, LANES)
        for col_tap in range(3):
            at = col_tap * LANES
            out_ref[at : at + LANES, :] = half_taps(blocks_ref, grad_ref, 0, col_tap, start)
        for n in range(weighted_ref.shape[1] // channels):
            at = (3 + n) * LANES
            out_ref[at : at + LANES, :] = jnp.dot(
                turned[pl.ds(start, LANES), :],
                weighted_ref[:, n * channels : (n + 1) * channels],
                preferred_element_type=jnp.float32,
            )


def halves(kernel, rows, core, *arrays, scratch=()):
    shape = jax.ShapeDtypeStruct((rows, 2 * LANES), jnp.float32)
    return pl.pallas_call(
        kernel,
        out_shape=(shape, shape),
        in_specs=[scalars()] + [whole()] * len(arrays),
        out_specs=(whole(), whole()),
        scratch_shapes=scratch,
        compiler_params=params(),
        cost_estimate=pl.CostEstimate(flops=400 * 10**6, bytes_accessed=4 * 10**6, transcendentals=0),
        name="halves",
    )(core, *arrays)


def input_kernel(grad_ref, below_ref, weight_ref, out_ref, wide):
    half = grad_ref.shape[1]
    last = lax.broadcasted_iota(jnp.int32, grad_ref.shape[1:], 0) == half - 1

    def early(g):
        moved = pltpu.roll(g.astype(jnp.float32), half - 1, 0)
        return jnp.where(last, 0.0, moved).astype(jnp.bfloat16)

    grads = [grad_ref[0], grad_ref[1], below_ref[0]]
    moved = [early(g) for g in grads]

    def times(g, row_tap, col_tap):
        return lax.dot_general(
            g,
            weight_ref[row_tap, col_tap],
            (((1,), (1,)), ((), ())),
            preferred_element_type=jnp.float32,
        )

    for row in range(4):
        i = row // 2
        terms = [(i, 1)] if row % 2 == 0 else [(i, 2), (i + 1, 0)]
        even = sum(times(grads[n], p, 1) for n, p in terms)
        odd = sum(times(grads[n], p, 2) + times(moved[n], p, 0) for n, p in terms)
        for part in range(even.shape[1] // LANES):
            lanes = slice(part * LANES, (part + 1) * LANES)
            wide[pl.ds(0, half, stride=2), :] = even[:, lanes]
            wide[pl.ds(1, half, stride=2), :] = odd[:, lanes]
            out_ref[row, :, lanes] = wide[...].astype(jnp.bfloat16)


def input_grad(grad, below, weight):
    rows, half, channels = grad.shape
    return pl.pallas_call(
        input_kernel,
        out_shape=jax.ShapeDtypeStruct((2 * rows, 2 * half, weight.shape[2]), jnp.bfloat16),
        in_specs=[whole()] * 3,
        out_specs=whole(),
        scratch_shapes=[pltpu.VMEM((2 * half, LANES), jnp.float32)],
        compiler_params=params(),
        cost_estimate=pl.CostEstimate(flops=604 * 10**6, bytes_accessed=3 * 10**6, transcendentals=0),
        name="input_grad",
    )(grad, below, weight)


def exchange(x, axis):
    return lax.all_to_all(x, axis, split_axis=0, concat_axis=0, tiled=True)


def place(axis, by=0):
    return (lax.axis_index(axis).astype(jnp.uint32) + jnp.uint32(by % SIZES[axis])) & jnp.uint32(SIZES[axis] - 1)


def pick(parts, index):
    zero = jnp.uint32(0)
    return lax.dynamic_slice(parts, (index, zero, zero), (1,) + parts.shape[1:])[0]


def put(parts, piece, index):
    zero = jnp.uint32(0)
    return lax.dynamic_update_slice(parts, piece[None], (index, zero, zero))


def rotated(x, axis, by):
    size = SIZES[axis]
    return lax.ppermute(x, axis, [(i, (i + by) % size) for i in range(size)])


def split(x):
    return x.reshape(4, x.shape[0] // 4, x.shape[1])


def swapped(x, axis, bit):
    return lax.ppermute(x, axis, [(i, i ^ bit) for i in range(SIZES[axis])])


def turned(x, by):
    pairs = []
    for i in range(SIZES["x"]):
        for k in range(SIZES["z"]):
            for j in range(SIZES["y"]):
                to = (i, (j + by) % 4) if k % 2 else ((i + by) % 4, j)
                pairs.append(((i * SIZES["z"] + k) * 4 + j, (to[0] * SIZES["z"] + k) * 4 + to[1]))
    return lax.ppermute(x, ("x", "z", "y"), pairs)


def turned_place(by=0):
    odd = (place("z") & jnp.uint32(1)) == 1
    return jnp.where(odd, place("y", by), place("x", by))


barrier = lax.optimization_barrier
STEPS = (1, 2, 3)


def total_sums(inner, outer, scale, beside):
    inner, outer = split(inner), split(outer)
    inner, parts = barrier((inner, [pick(outer, place("x", by)) for by in STEPS]))
    inner = exchange(inner, "y")
    moved = [rotated(p, "x", by) for p, by in zip(parts, STEPS)]
    inner, moved, beside = barrier((inner, moved, beside))
    inner = jnp.sum(inner, axis=0)
    outer = sum(moved, pick(outer, place("x")))

    rows = outer.shape[0] - inner.shape[0]
    both = jnp.stack([jnp.pad(inner, ((0, rows), (0, 0))), outer])
    bit = place("z") & jnp.uint32(1)
    part = pick(both, bit) + swapped(pick(both, jnp.uint32(1) - bit), "z", 1)

    parts = split(part)
    moved = barrier([pick(parts, turned_place(by)) for by in STEPS])
    moved = [turned(p, by) for p, by in zip(moved, STEPS)]
    part = sum(moved, pick(parts, turned_place()))

    two, four, six = [rotated(part, "z", by) for by in (2, 4, 6)]
    part = ((part + four) + (two + six)) * scale

    whole_part = jnp.zeros((4,) + part.shape, part.dtype)
    for by in range(4):
        whole_part = put(whole_part, turned(part, by) if by else part, turned_place(-by))
    part = whole_part.reshape(-1, part.shape[1])
    got = swapped(part, "z", 1)
    inner = jnp.where(bit == 0, part, got)[: part.shape[0] - rows]
    outer = jnp.where(bit == 0, got, part)
    inner, outer = barrier((inner, outer))
    copies = barrier(jnp.broadcast_to(inner, (4,) + inner.shape))
    copies, moved = barrier((exchange(copies, "y"), [rotated(outer, "x", by) for by in STEPS]))
    return [copies.reshape(-1, part.shape[1])], [outer] + moved, beside


def assemble_kernel(where_ref, *refs):
    inner, pieces, (conv_ref, expand_ref, joined) = refs[:2], refs[2:10], refs[10:]
    channels = conv_ref.shape[2]
    core = where_ref[0]
    for by in range(4):
        rows = pieces[by].shape[0]
        at = pl.multiple_of(((where_ref[1] + 4 - by) & 3) * rows, 8)
        joined[core, pl.ds(at, rows), :] = pieces[by][...]
        joined[1 - core, pl.ds(at, rows), :] = pieces[4 + by][...]
    for tap in range(6):
        rows = slice(tap * LANES, (tap + 1) * LANES)
        conv_ref[3 + tap, pl.ds(pl.multiple_of(core * LANES, LANES), LANES), :] = inner[0][rows, :]
        conv_ref[3 + tap, pl.ds(pl.multiple_of((1 - core) * LANES, LANES), LANES), :] = inner[1][rows, :]
    for half in range(2):
        lanes = slice(half * LANES, (half + 1) * LANES)
        for tap in range(3):
            conv_ref[tap, lanes, :] = joined[half, tap * LANES : (tap + 1) * LANES, :]
        for n in range(expand_ref.shape[1] // channels):
            at = (3 + n) * LANES
            expand_ref[lanes, n * channels : (n + 1) * channels] = joined[half, at : at + LANES, :]


def assemble(where, groups, channels, deep):
    refs = [piece for group in groups for piece in group]
    return pl.pallas_call(
        assemble_kernel,
        out_shape=(
            jax.ShapeDtypeStruct((9, channels, channels), jnp.float32),
            jax.ShapeDtypeStruct((channels, deep), jnp.float32),
        ),
        in_specs=[scalars()] + [whole()] * len(refs),
        out_specs=(whole(), whole()),
        scratch_shapes=[pltpu.VMEM((2, 4 * groups[1][0].shape[0], channels), jnp.float32)],
        compiler_params=params(),
        cost_estimate=pl.CostEstimate(flops=0, bytes_accessed=7 * 10**6, transcendentals=0),
        name="assemble",
    )(where, *refs)


def body(stem_input, stem_preact, deep_cotangent, tissue_tiles, conv_weight, expand_weight):
    _, out_rows, out_cols, channels = stem_preact.shape
    _, all_rows, band, deep = deep_cotangent.shape
    devices = SIZES["x"] * SIZES["z"]
    preact = stem_preact[0]
    cotangent = deep_cotangent[0].reshape(all_rows * band, deep)
    share = tissue_tiles.astype(jnp.float32) / TILES
    core = lax.axis_index("core").astype(jnp.int32)
    where = jnp.stack([core, lax.axis_index("x")]).astype(jnp.int32)

    hidden = lax.dot_general(
        (cotangent.astype(jnp.float32) * share[:, None]).astype(jnp.bfloat16),
        expand_weight,
        (((1,), (1,)), ((), ())),
        preferred_element_type=jnp.float32,
    ).astype(jnp.bfloat16)
    active = jnp.maximum(preact, jnp.zeros_like(preact))
    active = active.reshape(out_rows, devices, band, channels).transpose(1, 0, 2, 3)
    chunk = out_rows * band
    sent = jnp.concatenate(
        [hidden.reshape(devices, chunk, channels), active.reshape(devices, chunk, channels)], axis=1
    )
    above = shifted(stem_input[0, -1:], 1)
    blocks, weighted = prepare(share, above, stem_input[0], cotangent)
    arrived = exchange(sent, SPACE)
    hidden = arrived[:, :chunk].reshape(devices, out_rows, band, channels).transpose(1, 0, 2, 3)
    hidden = hidden.reshape(out_rows, out_cols, channels)
    active = arrived[:, chunk:].reshape(all_rows * band, channels)
    grad = jnp.where(preact > 0, hidden, jnp.zeros_like(hidden))
    below = shifted(grad[:1], -1)

    own_inner, other_inner = halves(inner_kernel, 6 * LANES, where[:1], blocks, grad)
    own_outer, other_outer = halves(
        outer_kernel,
        3 * LANES + deep // 2,
        where[:1],
        blocks,
        grad,
        active,
        weighted,
        scratch=[pltpu.VMEM((channels, all_rows * band), jnp.bfloat16)],
    )
    grad_input = input_grad(grad, below, conv_weight)

    samples_all = stem_input.shape[0] * SIZES["y"] * SIZES["core"]
    scale = float(samples_all * all_rows * out_cols) ** (-0.5)
    inner = own_inner + swapped(other_inner, "core", 1)
    outer = own_outer + swapped(other_outer, "core", 1)
    inner, outer, grad_input = total_sums(inner, outer, scale, grad_input)
    groups = [pieces + [swapped(piece, "core", 1) for piece in pieces] for pieces in (inner, outer)]
    grad_conv, grad_expand = assemble(where, groups, channels, deep)
    return (grad_input[None], grad_conv.reshape(3, 3, channels, channels), grad_expand)


def solution(mesh):
    fine = Mesh(
        mesh.devices.reshape(SIZES["x"], SIZES["z"], SIZES["y"], SIZES["core"]),
        ("x", "z", "y", "core"),
    )
    return jax.shard_map(
        body,
        mesh=fine,
        in_specs=(
            P(REP, SPACE, None, None),
            P(REP, SPACE, None, None),
            P(REP, None, SPACE, None),
            P(REP),
            P(),
            P(),
        ),
        out_specs=(P(REP, SPACE, None, None), P(), P()),
        check_vma=False,
    )
```

```python
import functools

import jax
import jax.numpy as jnp
from jax import lax
from jax.experimental import pallas as pl
from jax.experimental.pallas import tpu as pltpu
from jax.sharding import Mesh
from jax.sharding import PartitionSpec as P

TILES = 64
LANES = 128
SIZES = {"x": 4, "z": 8, "y": 4, "core": 2}
SPACE = ("x", "z")
REP = ("y", "core")


def whole():
    return pl.BlockSpec(memory_space=pltpu.VMEM)


def far():
    return pl.BlockSpec(memory_space=pl.ANY)


def room(x):
    return pltpu.VMEM(x.shape, x.dtype)


def scalars():
    return pl.BlockSpec(memory_space=pltpu.SMEM)


def params(mib=24):
    return pltpu.CompilerParams(vmem_limit_bytes=mib * 1024 * 1024)


def shifted(x, by):
    length = SIZES["x"] * SIZES["z"]
    pairs = [(i, i + by) for i in range(length) if 0 <= i + by < length]
    return lax.ppermute(x, SPACE, pairs)


def send_kernel(
    share_ref, cotangent_hbm, weight_hbm, preact_hbm, sent_hbm, weighted_hbm,
    cotangent_ref, weight_ref, preact_ref, weighted_ref, sent_ref, sems,
):
    pairs = ((preact_hbm, preact_ref), (weight_hbm, weight_ref), (cotangent_hbm, cotangent_ref))
    copies = [pltpu.make_async_copy(a, b, sems.at[n]) for n, (a, b) in enumerate(pairs)]
    for copy in copies:
        copy.start()
    devices, chunk, channels = sent_ref.shape
    chunk = chunk // 2
    rows, cols = preact_ref.shape[:2]
    band = cols // devices
    copies[0].wait()
    for i in range(rows):
        active = jnp.maximum(preact_ref[i].astype(jnp.float32), 0.0).reshape(devices, band, channels)
        sent_ref[:, chunk + i * band : chunk + (i + 1) * band, :] = active.astype(jnp.bfloat16)
    copies[1].wait()
    copies[2].wait()
    weighted = (cotangent_ref[...].astype(jnp.float32) * share_ref[0]).astype(jnp.bfloat16)
    weighted_ref[...] = weighted
    back = pltpu.make_async_copy(weighted_ref, weighted_hbm, sems.at[3])
    back.start()
    hidden = lax.dot_general(
        weighted, weight_ref[...], (((1,), (1,)), ((), ())), preferred_element_type=jnp.float32
    )
    sent_ref[:, :chunk, :] = hidden.reshape(devices, chunk, channels).astype(jnp.bfloat16)
    out = pltpu.make_async_copy(sent_ref, sent_hbm, sems.at[4])
    out.start()
    back.wait()
    out.wait()


def build_sent(share, cotangent, weight, preact, devices):
    rows, cols, channels = preact.shape
    sent = jax.ShapeDtypeStruct((devices, 2 * rows * cols // devices, channels), jnp.bfloat16)
    return pl.pallas_call(
        send_kernel,
        out_shape=(
            sent,
            jax.ShapeDtypeStruct(cotangent.shape, jnp.bfloat16),
        ),
        in_specs=[scalars()] + [far()] * 3,
        out_specs=(far(), far()),
        scratch_shapes=[room(x) for x in (cotangent, weight, preact, cotangent, sent)]
        + [pltpu.SemaphoreType.DMA((5,))],
        compiler_params=params(60),
        cost_estimate=pl.CostEstimate(flops=268 * 10**6, bytes_accessed=4 * 10**6, transcendentals=0),
        name="build_sent",
    )(share, cotangent, weight, preact)


def prepare_kernel(x_ref, out_ref, wide):
    half = out_ref.shape[2]
    first = lax.broadcasted_iota(jnp.int32, (LANES, half), 1) == 0
    for row in range(x_ref.shape[0]):
        for part in range(x_ref.shape[2] // LANES):
            lanes = slice(part * LANES, (part + 1) * LANES)
            wide[...] = x_ref[row, :, lanes].astype(jnp.float32)
            even = wide[pl.ds(0, half, stride=2), :].T
            odd = wide[pl.ds(1, half, stride=2), :].T
            late = jnp.where(first, 0.0, pltpu.roll(odd, 1, 1))
            out_ref[3 * row, lanes, :] = late.astype(jnp.bfloat16)
            out_ref[3 * row + 1, lanes, :] = even.astype(jnp.bfloat16)
            out_ref[3 * row + 2, lanes, :] = odd.astype(jnp.bfloat16)


def prepare(x):
    rows, cols, channels = x.shape
    return pl.pallas_call(
        prepare_kernel,
        out_shape=jax.ShapeDtypeStruct((3 * rows, channels, cols // 2), jnp.bfloat16),
        in_specs=[whole()],
        out_specs=whole(),
        scratch_shapes=[pltpu.VMEM((cols, LANES), jnp.float32)],
        compiler_params=params(),
        cost_estimate=pl.CostEstimate(flops=10**7, bytes_accessed=3 * 10**6, transcendentals=0),
        name="prepare",
    )(x)


def terms_kernel(
    core_ref, arrived_hbm, preact_hbm, above_hbm, blocks_hbm, weighted_hbm,
    own_inner, other_inner, own_outer, other_outer, grad_hbm,
    arrived_ref, preact_ref, above_ref, blocks_ref, weighted_ref,
    grad_ref, turned, inner_ref, outer_ref, sems,
):
    pairs = (
        (arrived_hbm, arrived_ref),
        (preact_hbm, preact_ref),
        (blocks_hbm, blocks_ref),
        (above_hbm, above_ref),
        (weighted_hbm, weighted_ref),
    )
    copies = [pltpu.make_async_copy(a, b, sems.at[n]) for n, (a, b) in enumerate(pairs)]
    for copy in copies:
        copy.start()
    devices, chunk, channels = arrived_ref.shape
    rows, cols = preact_ref.shape[:2]
    chunk, band = chunk // 2, cols // devices
    copies[0].wait()
    copies[1].wait()
    for i in range(rows):
        hidden = arrived_ref[:, i * band : (i + 1) * band, :].astype(jnp.float32).reshape(cols, channels)
        kept = jnp.where(preact_ref[i].astype(jnp.float32) > 0.0, hidden, 0.0)
        grad_ref[i] = kept.astype(jnp.bfloat16)
    back = [pltpu.make_async_copy(grad_ref, grad_hbm, sems.at[5])]
    back[0].start()
    active = arrived_ref[:, chunk:, :].astype(jnp.float32).reshape(devices * chunk, channels)
    turned[...] = active.T.astype(jnp.bfloat16)

    def half_taps(row_tap, col_tap, start):
        total = None
        for i in range(rows):
            row = 2 * i + row_tap - 1
            source, at = (above_ref, col_tap) if row < 0 else (blocks_ref, 3 * row + col_tap)
            term = jnp.dot(
                source[at, pl.ds(start, LANES), :], grad_ref[i], preferred_element_type=jnp.float32
            )
            total = term if total is None else total + term
        return total

    for copy in copies[2:]:
        copy.wait()
    for n, (inner_hbm, outer_hbm) in enumerate(((other_inner, other_outer), (own_inner, own_outer))):
        owner = core_ref[0] if n else 1 - core_ref[0]
        start = pl.multiple_of(owner * LANES, LANES)
        for col_tap in range(3):
            for row_tap in (1, 2):
                at = (3 * (row_tap - 1) + col_tap) * LANES
                inner_ref[n, at : at + LANES, :] = half_taps(row_tap, col_tap, start)
        back.append(pltpu.make_async_copy(inner_ref.at[n], inner_hbm, sems.at[6 + 2 * n]))
        back[-1].start()
        for col_tap in range(3):
            at = col_tap * LANES
            outer_ref[n, at : at + LANES, :] = half_taps(0, col_tap, start)
        for k in range(weighted_ref.shape[1] // channels):
            at = (3 + k) * LANES
            outer_ref[n, at : at + LANES, :] = jnp.dot(
                turned[pl.ds(start, LANES), :],
                weighted_ref[:, k * channels : (k + 1) * channels],
                preferred_element_type=jnp.float32,
            )
        back.append(pltpu.make_async_copy(outer_ref.at[n], outer_hbm, sems.at[7 + 2 * n]))
        back[-1].start()
    for copy in back:
        copy.wait()


def terms(core, arrived, preact, above, blocks, weighted):
    rows, cols, channels = preact.shape
    inner = jax.ShapeDtypeStruct((6 * LANES, channels), jnp.float32)
    outer = jax.ShapeDtypeStruct((3 * LANES + weighted.shape[1] // 2, channels), jnp.float32)
    return pl.pallas_call(
        terms_kernel,
        out_shape=(inner, inner, outer, outer, jax.ShapeDtypeStruct(preact.shape, jnp.bfloat16)),
        in_specs=[scalars()] + [far()] * 5,
        out_specs=(far(),) * 5,
        scratch_shapes=[room(x) for x in (arrived, preact, above, blocks, weighted, preact)]
        + [
            pltpu.VMEM((channels, weighted.shape[0]), jnp.bfloat16),
            pltpu.VMEM((2,) + inner.shape, jnp.float32),
            pltpu.VMEM((2,) + outer.shape, jnp.float32),
            pltpu.SemaphoreType.DMA((10,)),
        ],
        compiler_params=params(54),
        cost_estimate=pl.CostEstimate(flops=870 * 10**6, bytes_accessed=8 * 10**6, transcendentals=0),
        name="terms",
    )(core, arrived, preact, above, blocks, weighted)


def combine_kernel(where_ref, *refs):
    hbm, (inner_hbm, *outer_hbm), room_refs, sems = refs[:4], refs[4:9], refs[9:13], refs[13]
    copies = [pltpu.make_async_copy(a, b, sems.at[n]) for n, (a, b) in enumerate(zip(hbm, room_refs))]
    for copy in copies:
        copy.start()
    own_inner, got_inner, own_outer, got_outer = room_refs
    rows = own_outer.shape[0] // 4
    copies[0].wait()
    copies[1].wait()
    own_inner[...] += got_inner[...]
    back = [pltpu.make_async_copy(own_inner, inner_hbm, sems.at[4])]
    back[0].start()
    copies[2].wait()
    copies[3].wait()
    own_outer[...] += got_outer[...]
    for by, out in enumerate(outer_hbm):
        at = pl.ds(pl.multiple_of(((where_ref[1] + by) & 3) * rows, 8), rows)
        back.append(pltpu.make_async_copy(own_outer.at[at, :], out, sems.at[5 + by]))
        back[-1].start()
    for copy in back:
        copy.wait()


def combine(where, *arrays):
    inner, outer = arrays[0], arrays[2]
    chunk = jax.ShapeDtypeStruct((outer.shape[0] // 4, outer.shape[1]), jnp.float32)
    return pl.pallas_call(
        combine_kernel,
        out_shape=(jax.ShapeDtypeStruct(inner.shape, jnp.float32),) + (chunk,) * 4,
        in_specs=[scalars()] + [far()] * 4,
        out_specs=(far(),) * 5,
        scratch_shapes=[room(x) for x in arrays] + [pltpu.SemaphoreType.DMA((9,))],
        compiler_params=params(24),
        cost_estimate=pl.CostEstimate(flops=10**6, bytes_accessed=5 * 10**6, transcendentals=0),
        name="combine",
    )(where, *arrays)


def input_kernel(grad_ref, below_ref, weight_ref, out_ref, wide):
    half = grad_ref.shape[1]
    last = lax.broadcasted_iota(jnp.int32, grad_ref.shape[1:], 0) == half - 1

    def early(g):
        moved = pltpu.roll(g.astype(jnp.float32), half - 1, 0)
        return jnp.where(last, 0.0, moved).astype(jnp.bfloat16)

    grads = [grad_ref[0], grad_ref[1], below_ref[0]]
    moved = [early(g) for g in grads]

    def times(g, row_tap, col_tap):
        return lax.dot_general(
            g,
            weight_ref[row_tap, col_tap],
            (((1,), (1,)), ((), ())),
            preferred_element_type=jnp.float32,
        )

    for row in range(4):
        i = row // 2
        terms = [(i, 1)] if row % 2 == 0 else [(i, 2), (i + 1, 0)]
        even = sum(times(grads[n], p, 1) for n, p in terms)
        odd = sum(times(grads[n], p, 2) + times(moved[n], p, 0) for n, p in terms)
        for part in range(even.shape[1] // LANES):
            lanes = slice(part * LANES, (part + 1) * LANES)
            wide[pl.ds(0, half, stride=2), :] = even[:, lanes]
            wide[pl.ds(1, half, stride=2), :] = odd[:, lanes]
            out_ref[row, :, lanes] = wide[...].astype(jnp.bfloat16)


def input_grad(grad, below, weight):
    rows, half, channels = grad.shape
    return pl.pallas_call(
        input_kernel,
        out_shape=jax.ShapeDtypeStruct((2 * rows, 2 * half, weight.shape[2]), jnp.bfloat16),
        in_specs=[whole()] * 3,
        out_specs=whole(),
        scratch_shapes=[pltpu.VMEM((2 * half, LANES), jnp.float32)],
        compiler_params=params(),
        cost_estimate=pl.CostEstimate(flops=604 * 10**6, bytes_accessed=3 * 10**6, transcendentals=0),
        name="input_grad",
    )(grad, below, weight)


def exchange(x, axis):
    return lax.all_to_all(x, axis, split_axis=0, concat_axis=0, tiled=True)


def place(axis, by=0):
    return (lax.axis_index(axis).astype(jnp.uint32) + jnp.uint32(by % SIZES[axis])) & jnp.uint32(SIZES[axis] - 1)


def pick(parts, index):
    zero = jnp.uint32(0)
    return lax.dynamic_slice(parts, (index, zero, zero), (1,) + parts.shape[1:])[0]


def put(parts, piece, index):
    zero = jnp.uint32(0)
    return lax.dynamic_update_slice(parts, piece[None], (index, zero, zero))


def rotated(x, axis, by):
    size = SIZES[axis]
    return lax.ppermute(x, axis, [(i, (i + by) % size) for i in range(size)])


def split(x):
    return x.reshape(4, x.shape[0] // 4, x.shape[1])


def swapped(x, axis, bit):
    return lax.ppermute(x, axis, [(i, i ^ bit) for i in range(SIZES[axis])])


def turned(x, by):
    pairs = []
    for i in range(SIZES["x"]):
        for k in range(SIZES["z"]):
            for j in range(SIZES["y"]):
                to = (i, (j + by) % 4) if k % 2 else ((i + by) % 4, j)
                pairs.append(((i * SIZES["z"] + k) * 4 + j, (to[0] * SIZES["z"] + k) * 4 + to[1]))
    return lax.ppermute(x, ("x", "z", "y"), pairs)


def turned_place(by=0):
    odd = (place("z") & jnp.uint32(1)) == 1
    return jnp.where(odd, place("y", by), place("x", by))


barrier = lax.optimization_barrier
STEPS = (1, 2, 3)


def total_sums(inner, outer, parts, scale, below, beside):
    inner, parts, below = barrier((split(inner), parts, below))
    inner = exchange(inner, "y")
    moved = [rotated(p, "x", by) for p, by in zip(parts, STEPS)]
    inner, moved = barrier((inner, moved))
    inner = jnp.sum(inner, axis=0)
    outer = sum(moved, outer)

    rows = outer.shape[0] - inner.shape[0]
    both = jnp.stack([jnp.pad(inner, ((0, rows), (0, 0))), outer])
    bit = place("z") & jnp.uint32(1)
    part = pick(both, bit) + swapped(pick(both, jnp.uint32(1) - bit), "z", 1)

    parts = split(part)
    moved = barrier([pick(parts, turned_place(by)) for by in STEPS])
    moved = [turned(p, by) for p, by in zip(moved, STEPS)]
    part = sum(moved, pick(parts, turned_place()))

    moved = [rotated(part, "z", by) for by in (2, 4, 6)]
    (two, four, six), beside = barrier((moved, beside(below)))
    part = ((part + four) + (two + six)) * scale

    whole_part = jnp.zeros((4,) + part.shape, part.dtype)
    for by in range(4):
        whole_part = put(whole_part, turned(part, by) if by else part, turned_place(-by))
    part = whole_part.reshape(-1, part.shape[1])
    got = swapped(part, "z", 1)
    inner = jnp.where(bit == 0, part, got)[: part.shape[0] - rows]
    outer = jnp.where(bit == 0, got, part)
    inner, outer = barrier((inner, outer))
    copies = barrier(jnp.broadcast_to(inner, (4,) + inner.shape))
    copies, moved = barrier((exchange(copies, "y"), [rotated(outer, "x", by) for by in STEPS]))
    return [copies.reshape(-1, part.shape[1])], [outer] + moved, beside


def assemble_kernel(where_ref, *refs):
    inner, pieces, (conv_ref, expand_ref, joined) = refs[:2], refs[2:10], refs[10:]
    channels = conv_ref.shape[2]
    core = where_ref[0]
    for by in range(4):
        rows = pieces[by].shape[0]
        at = pl.multiple_of(((where_ref[1] + 4 - by) & 3) * rows, 8)
        joined[core, pl.ds(at, rows), :] = pieces[by][...]
        joined[1 - core, pl.ds(at, rows), :] = pieces[4 + by][...]
    for tap in range(6):
        rows = slice(tap * LANES, (tap + 1) * LANES)
        conv_ref[3 + tap, pl.ds(pl.multiple_of(core * LANES, LANES), LANES), :] = inner[0][rows, :]
        conv_ref[3 + tap, pl.ds(pl.multiple_of((1 - core) * LANES, LANES), LANES), :] = inner[1][rows, :]
    for half in range(2):
        lanes = slice(half * LANES, (half + 1) * LANES)
        for tap in range(3):
            conv_ref[tap, lanes, :] = joined[half, tap * LANES : (tap + 1) * LANES, :]
        for n in range(expand_ref.shape[1] // channels):
            at = (3 + n) * LANES
            expand_ref[lanes, n * channels : (n + 1) * channels] = joined[half, at : at + LANES, :]


def assemble(where, groups, channels, deep):
    refs = [piece for group in groups for piece in group]
    return pl.pallas_call(
        assemble_kernel,
        out_shape=(
            jax.ShapeDtypeStruct((9, channels, channels), jnp.float32),
            jax.ShapeDtypeStruct((channels, deep), jnp.float32),
        ),
        in_specs=[scalars()] + [whole()] * len(refs),
        out_specs=(whole(), whole()),
        scratch_shapes=[pltpu.VMEM((2, 4 * groups[1][0].shape[0], channels), jnp.float32)],
        compiler_params=params(),
        cost_estimate=pl.CostEstimate(flops=0, bytes_accessed=7 * 10**6, transcendentals=0),
        name="assemble",
    )(where, *refs)


def body(stem_input, stem_preact, deep_cotangent, tissue_tiles, conv_weight, expand_weight):
    _, out_rows, out_cols, channels = stem_preact.shape
    _, all_rows, band, deep = deep_cotangent.shape
    devices = SIZES["x"] * SIZES["z"]
    preact = stem_preact[0]
    cotangent = deep_cotangent[0].reshape(all_rows * band, deep)
    share = tissue_tiles.astype(jnp.float32) / TILES
    core = lax.axis_index("core").astype(jnp.int32)
    where = jnp.stack([core, lax.axis_index("x")]).astype(jnp.int32)

    sent, weighted = build_sent(share, cotangent, expand_weight, preact, devices)
    blocks = prepare(stem_input[0])
    above = prepare(shifted(stem_input[0, -1:], 1))
    arrived = exchange(sent, SPACE)
    own_inner, other_inner, own_outer, other_outer, grad = terms(
        where[:1], arrived, preact, above, blocks, weighted
    )
    below = shifted(grad[:1], -1)

    samples_all = stem_input.shape[0] * SIZES["y"] * SIZES["core"]
    scale = float(samples_all * all_rows * out_cols) ** (-0.5)
    got_inner, got_outer = swapped(other_inner, "core", 1), swapped(other_outer, "core", 1)
    inner, outer, *parts = combine(where, own_inner, got_inner, own_outer, got_outer)
    inner, outer, grad_input = total_sums(
        inner, outer, parts, scale, below, lambda b: input_grad(grad, b, conv_weight)
    )
    groups = [pieces + [swapped(piece, "core", 1) for piece in pieces] for pieces in (inner, outer)]
    grad_conv, grad_expand = assemble(where, groups, channels, deep)
    return (grad_input[None], grad_conv.reshape(3, 3, channels, channels), grad_expand)


def solution(mesh):
    fine = Mesh(
        mesh.devices.reshape(SIZES["x"], SIZES["z"], SIZES["y"], SIZES["core"]),
        ("x", "z", "y", "core"),
    )
    return jax.shard_map(
        body,
        mesh=fine,
        in_specs=(
            P(REP, SPACE, None, None),
            P(REP, SPACE, None, None),
            P(REP, None, SPACE, None),
            P(REP),
            P(),
            P(),
        ),
        out_specs=(P(REP, SPACE, None, None), P(), P()),
        check_vma=False,
    )
```

```python
import functools

import jax
import jax.numpy as jnp
from jax import lax
from jax.experimental import pallas as pl
from jax.experimental.pallas import tpu as pltpu
from jax.sharding import Mesh
from jax.sharding import PartitionSpec as P

TILES = 64
LANES = 128
SIZES = {"x": 4, "z": 8, "y": 4, "core": 2}
SPACE = ("x", "z")
REP = ("y", "core")


def whole():
    return pl.BlockSpec(memory_space=pltpu.VMEM)


def far():
    return pl.BlockSpec(memory_space=pl.ANY)


def room(x):
    return pltpu.VMEM(x.shape, x.dtype)


def scalars():
    return pl.BlockSpec(memory_space=pltpu.SMEM)


def params(mib=24):
    return pltpu.CompilerParams(vmem_limit_bytes=mib * 1024 * 1024)


def shifted(x, by):
    length = SIZES["x"] * SIZES["z"]
    pairs = [(i, i + by) for i in range(length) if 0 <= i + by < length]
    return lax.ppermute(x, SPACE, pairs)


def send_kernel(
    share_ref, cotangent_hbm, weight_hbm, preact_hbm, sent_hbm, weighted_hbm,
    cotangent_ref, weight_ref, preact_ref, weighted_ref, sent_ref, sems,
):
    pairs = ((preact_hbm, preact_ref), (weight_hbm, weight_ref), (cotangent_hbm, cotangent_ref))
    copies = [pltpu.make_async_copy(a, b, sems.at[n]) for n, (a, b) in enumerate(pairs)]
    for copy in copies:
        copy.start()
    devices, chunk, channels = sent_ref.shape
    chunk = chunk // 2
    rows, cols = preact_ref.shape[:2]
    band = cols // devices
    copies[0].wait()
    for i in range(rows):
        active = jnp.maximum(preact_ref[i].astype(jnp.float32), 0.0).reshape(devices, band, channels)
        sent_ref[:, chunk + i * band : chunk + (i + 1) * band, :] = active.astype(jnp.bfloat16)
    copies[1].wait()
    copies[2].wait()
    weighted = (cotangent_ref[...].astype(jnp.float32) * share_ref[0]).astype(jnp.bfloat16)
    weighted_ref[...] = weighted
    back = pltpu.make_async_copy(weighted_ref, weighted_hbm, sems.at[3])
    back.start()
    hidden = lax.dot_general(
        weighted, weight_ref[...], (((1,), (1,)), ((), ())), preferred_element_type=jnp.float32
    )
    sent_ref[:, :chunk, :] = hidden.reshape(devices, chunk, channels).astype(jnp.bfloat16)
    out = pltpu.make_async_copy(sent_ref, sent_hbm, sems.at[4])
    out.start()
    back.wait()
    out.wait()


def build_sent(share, cotangent, weight, preact, devices):
    rows, cols, channels = preact.shape
    sent = jax.ShapeDtypeStruct((devices, 2 * rows * cols // devices, channels), jnp.bfloat16)
    return pl.pallas_call(
        send_kernel,
        out_shape=(
            sent,
            jax.ShapeDtypeStruct(cotangent.shape, jnp.bfloat16),
        ),
        in_specs=[scalars()] + [far()] * 3,
        out_specs=(far(), far()),
        scratch_shapes=[room(x) for x in (cotangent, weight, preact, cotangent, sent)]
        + [pltpu.SemaphoreType.DMA((5,))],
        compiler_params=params(60),
        cost_estimate=pl.CostEstimate(flops=268 * 10**6, bytes_accessed=4 * 10**6, transcendentals=0),
        name="build_sent",
    )(share, cotangent, weight, preact)


def prepare_kernel(x_ref, out_ref, wide):
    half = out_ref.shape[2]
    first = lax.broadcasted_iota(jnp.int32, (LANES, half), 1) == 0
    for row in range(x_ref.shape[0]):
        for part in range(x_ref.shape[2] // LANES):
            lanes = slice(part * LANES, (part + 1) * LANES)
            wide[...] = x_ref[row, :, lanes].astype(jnp.float32)
            even = wide[pl.ds(0, half, stride=2), :].T
            odd = wide[pl.ds(1, half, stride=2), :].T
            late = jnp.where(first, 0.0, pltpu.roll(odd, 1, 1))
            out_ref[3 * row, lanes, :] = late.astype(jnp.bfloat16)
            out_ref[3 * row + 1, lanes, :] = even.astype(jnp.bfloat16)
            out_ref[3 * row + 2, lanes, :] = odd.astype(jnp.bfloat16)


def prepare(x):
    rows, cols, channels = x.shape
    return pl.pallas_call(
        prepare_kernel,
        out_shape=jax.ShapeDtypeStruct((3 * rows, channels, cols // 2), jnp.bfloat16),
        in_specs=[whole()],
        out_specs=whole(),
        scratch_shapes=[pltpu.VMEM((cols, LANES), jnp.float32)],
        compiler_params=params(),
        cost_estimate=pl.CostEstimate(flops=10**7, bytes_accessed=3 * 10**6, transcendentals=0),
        name="prepare",
    )(x)


def fetch(pairs, sems):
    copies = [pltpu.make_async_copy(a, b, sems.at[n]) for n, (a, b) in enumerate(pairs)]
    for copy in copies:
        copy.start()
    return copies


def half_terms(start, grad_ref, turned, above_ref, blocks_ref, weighted_ref, inner_ref, outer_ref):
    channels = grad_ref.shape[2]

    def taps(row_tap, col_tap):
        total = None
        for i in range(grad_ref.shape[0]):
            row = 2 * i + row_tap - 1
            source, at = (above_ref, col_tap) if row < 0 else (blocks_ref, 3 * row + col_tap)
            term = jnp.dot(
                source[at, pl.ds(start, LANES), :], grad_ref[i], preferred_element_type=jnp.float32
            )
            total = term if total is None else total + term
        return total

    for col_tap in range(3):
        for row_tap in (1, 2):
            at = (3 * (row_tap - 1) + col_tap) * LANES
            inner_ref[at : at + LANES, :] = taps(row_tap, col_tap)
    for col_tap in range(3):
        at = col_tap * LANES
        outer_ref[at : at + LANES, :] = taps(0, col_tap)
    for k in range(weighted_ref.shape[1] // channels):
        at = (3 + k) * LANES
        outer_ref[at : at + LANES, :] = jnp.dot(
            turned[pl.ds(start, LANES), :],
            weighted_ref[:, k * channels : (k + 1) * channels],
            preferred_element_type=jnp.float32,
        )


def other_kernel(
    where_ref, arrived_hbm, preact_hbm, above_hbm, blocks_hbm, weighted_hbm,
    inner_hbm, outer_hbm, grad_hbm, first_hbm, turned_hbm,
    arrived_ref, preact_ref, above_ref, blocks_ref, weighted_ref,
    inner_ref, outer_ref, grad_ref, turned, sems,
):
    copies = fetch(
        (
            (arrived_hbm, arrived_ref),
            (preact_hbm, preact_ref),
            (blocks_hbm, blocks_ref),
            (above_hbm, above_ref),
            (weighted_hbm, weighted_ref),
        ),
        sems,
    )
    devices, chunk, channels = arrived_ref.shape
    rows, cols = preact_ref.shape[:2]
    chunk, band = chunk // 2, cols // devices
    copies[0].wait()
    copies[1].wait()
    for i in range(rows):
        hidden = arrived_ref[:, i * band : (i + 1) * band, :].astype(jnp.float32).reshape(cols, channels)
        kept = jnp.where(preact_ref[i].astype(jnp.float32) > 0.0, hidden, 0.0)
        grad_ref[i] = kept.astype(jnp.bfloat16)
    active = arrived_ref[:, chunk:, :].astype(jnp.float32).reshape(devices * chunk, channels)
    turned[...] = active.T.astype(jnp.bfloat16)
    for copy in copies[2:]:
        copy.wait()
    start = pl.multiple_of((1 - where_ref[0]) * LANES, LANES)
    half_terms(start, grad_ref, turned, above_ref, blocks_ref, weighted_ref, inner_ref, outer_ref)
    back = fetch(
        (
            (inner_ref, inner_hbm),
            (outer_ref, outer_hbm),
            (grad_ref, grad_hbm),
            (grad_ref.at[0:1], first_hbm),
            (turned, turned_hbm),
        ),
        sems,
    )
    for copy in back:
        copy.wait()


def other_terms(where, arrived, preact, above, blocks, weighted):
    rows, cols, channels = preact.shape
    arrays = (arrived, preact, above, blocks, weighted)
    inner = jax.ShapeDtypeStruct((6 * LANES, channels), jnp.float32)
    outer = jax.ShapeDtypeStruct((3 * LANES + weighted.shape[1] // 2, channels), jnp.float32)
    grad = jax.ShapeDtypeStruct(preact.shape, jnp.bfloat16)
    first = jax.ShapeDtypeStruct((1, cols, channels), jnp.bfloat16)
    turned = jax.ShapeDtypeStruct((channels, weighted.shape[0]), jnp.bfloat16)
    return pl.pallas_call(
        other_kernel,
        out_shape=(inner, outer, grad, first, turned),
        in_specs=[scalars()] + [far()] * 5,
        out_specs=(far(),) * 5,
        scratch_shapes=[room(x) for x in arrays + (inner, outer, grad, turned)]
        + [pltpu.SemaphoreType.DMA((5,))],
        compiler_params=params(54),
        cost_estimate=pl.CostEstimate(flops=435 * 10**6, bytes_accessed=6 * 10**6, transcendentals=0),
        name="other_terms",
    )(where, *arrays)


def own_kernel(
    where_ref, grad_ref, turned, above_ref, blocks_ref, weighted_ref, got_inner, got_outer, *refs
):
    outs, (inner_ref, outer_ref, sems) = refs[:10], refs[10:]
    start = pl.multiple_of(where_ref[0] * LANES, LANES)
    half_terms(start, grad_ref, turned, above_ref, blocks_ref, weighted_ref, inner_ref, outer_ref)
    inner_ref[...] += got_inner[...]
    outer_ref[...] += got_outer[...]
    pairs = []
    for n, source in enumerate((inner_ref, outer_ref)):
        rows = source.shape[0] // 4

        def cut(by, offset, count):
            at = ((where_ref[2 - n] + by) & 3) * rows + offset
            return source.at[pl.ds(pl.multiple_of(at, 8), count), :]

        half = rows // 2
        cuts = (cut(0, 0, rows), cut(1, 0, rows), cut(3, 0, rows), cut(2, 0, half), cut(2, half, half))
        pairs += zip(cuts, outs[5 * n : 5 * n + 5])
    for copy in fetch(pairs, sems):
        copy.wait()


def own_sums(where, grad, turned, above, blocks, weighted, got_inner, got_outer):
    outs = []
    for got in (got_inner, got_outer):
        rows = got.shape[0] // 4
        outs += [jax.ShapeDtypeStruct((n, got.shape[1]), jnp.float32) for n in (rows,) * 3 + (rows // 2,) * 2]
    arrays = (grad, turned, above, blocks, weighted, got_inner, got_outer)
    return pl.pallas_call(
        own_kernel,
        out_shape=tuple(outs),
        in_specs=[scalars()] + [whole()] * len(arrays),
        out_specs=(far(),) * 10,
        scratch_shapes=[room(got_inner), room(got_outer), pltpu.SemaphoreType.DMA((10,))],
        compiler_params=params(),
        cost_estimate=pl.CostEstimate(flops=435 * 10**6, bytes_accessed=8 * 10**6, transcendentals=0),
        name="own_sums",
    )(where, *arrays)


def relay_kernel(*refs):
    for n in range(2):
        above, below, upper, lower = refs[4 * n : 4 * n + 4]
        out_above, out_below = refs[8 + 2 * n : 10 + 2 * n]
        half = upper.shape[0]
        out_above[:half, :] = above[:half, :] + upper[...]
        out_above[half:, :] = above[half:, :]
        out_below[:half, :] = below[:half, :]
        out_below[half:, :] = below[half:, :] + lower[...]


def relay(*arrays):
    outs = [jax.ShapeDtypeStruct(arrays[n].shape, jnp.float32) for n in (0, 1, 4, 5)]
    return pl.pallas_call(
        relay_kernel,
        out_shape=tuple(outs),
        in_specs=[whole()] * 8,
        out_specs=(whole(),) * 4,
        compiler_params=params(),
        cost_estimate=pl.CostEstimate(flops=10**5, bytes_accessed=3 * 10**6, transcendentals=0),
        name="relay",
    )(*arrays)


def input_kernel(grad_ref, below_ref, weight_ref, out_ref, wide):
    half = grad_ref.shape[1]
    last = lax.broadcasted_iota(jnp.int32, grad_ref.shape[1:], 0) == half - 1

    def early(g):
        moved = pltpu.roll(g.astype(jnp.float32), half - 1, 0)
        return jnp.where(last, 0.0, moved).astype(jnp.bfloat16)

    grads = [grad_ref[0], grad_ref[1], below_ref[0]]
    moved = [early(g) for g in grads]

    def times(g, row_tap, col_tap):
        return lax.dot_general(
            g,
            weight_ref[row_tap, col_tap],
            (((1,), (1,)), ((), ())),
            preferred_element_type=jnp.float32,
        )

    for row in range(4):
        i = row // 2
        terms = [(i, 1)] if row % 2 == 0 else [(i, 2), (i + 1, 0)]
        even = sum(times(grads[n], p, 1) for n, p in terms)
        odd = sum(times(grads[n], p, 2) + times(moved[n], p, 0) for n, p in terms)
        for part in range(even.shape[1] // LANES):
            lanes = slice(part * LANES, (part + 1) * LANES)
            wide[pl.ds(0, half, stride=2), :] = even[:, lanes]
            wide[pl.ds(1, half, stride=2), :] = odd[:, lanes]
            out_ref[row, :, lanes] = wide[...].astype(jnp.bfloat16)


def input_grad(grad, below, weight):
    rows, half, channels = grad.shape
    return pl.pallas_call(
        input_kernel,
        out_shape=jax.ShapeDtypeStruct((2 * rows, 2 * half, weight.shape[2]), jnp.bfloat16),
        in_specs=[whole()] * 3,
        out_specs=whole(),
        scratch_shapes=[pltpu.VMEM((2 * half, LANES), jnp.float32)],
        compiler_params=params(),
        cost_estimate=pl.CostEstimate(flops=604 * 10**6, bytes_accessed=3 * 10**6, transcendentals=0),
        name="input_grad",
    )(grad, below, weight)


def exchange(x, axis):
    return lax.all_to_all(x, axis, split_axis=0, concat_axis=0, tiled=True)


def place(axis, by=0):
    return (lax.axis_index(axis).astype(jnp.uint32) + jnp.uint32(by % SIZES[axis])) & jnp.uint32(SIZES[axis] - 1)


def pick(parts, index):
    zero = jnp.uint32(0)
    return lax.dynamic_slice(parts, (index, zero, zero), (1,) + parts.shape[1:])[0]


def put(parts, piece, index):
    zero = jnp.uint32(0)
    return lax.dynamic_update_slice(parts, piece[None], (index, zero, zero))


def rotated(x, axis, by):
    size = SIZES[axis]
    return lax.ppermute(x, axis, [(i, (i + by) % size) for i in range(size)])


def split(x):
    return x.reshape(4, x.shape[0] // 4, x.shape[1])


def swapped(x, axis, bit):
    return lax.ppermute(x, axis, [(i, i ^ bit) for i in range(SIZES[axis])])


def turned(x, by):
    pairs = []
    for i in range(SIZES["x"]):
        for k in range(SIZES["z"]):
            for j in range(SIZES["y"]):
                to = (i, (j + by) % 4) if k % 2 else ((i + by) % 4, j)
                pairs.append(((i * SIZES["z"] + k) * 4 + j, (to[0] * SIZES["z"] + k) * 4 + to[1]))
    return lax.ppermute(x, ("x", "z", "y"), pairs)


def turned_place(by=0):
    odd = (place("z") & jnp.uint32(1)) == 1
    return jnp.where(odd, place("y", by), place("x", by))


barrier = lax.optimization_barrier
STEPS = (1, 2, 3)


def total_sums(cuts, scale, below, beside):
    cuts, below = barrier((cuts, below))
    axes = ("y", "x")
    passed = []
    for n, axis in enumerate(axes):
        passed += [rotated(cuts[5 * n + 3], axis, 1), rotated(cuts[5 * n + 4], axis, 3)]
    passed = barrier(passed)
    sums = relay(*cuts[1:3], *passed[:2], *cuts[6:8], *passed[2:])
    moved = []
    for n, axis in enumerate(axes):
        moved += [rotated(sums[2 * n], axis, 1), rotated(sums[2 * n + 1], axis, 3)]
    moved = barrier(moved)
    inner = cuts[0] + moved[0] + moved[1]
    outer = cuts[5] + moved[2] + moved[3]

    rows = outer.shape[0] - inner.shape[0]
    both = jnp.stack([jnp.pad(inner, ((0, rows), (0, 0))), outer])
    bit = place("z") & jnp.uint32(1)
    part = pick(both, bit) + swapped(pick(both, jnp.uint32(1) - bit), "z", 1)

    parts = split(part)
    moved = barrier([pick(parts, turned_place(by)) for by in STEPS])
    moved = [turned(p, by) for p, by in zip(moved, STEPS)]
    part = sum(moved, pick(parts, turned_place()))

    moved = [rotated(part, "z", by) for by in (2, 4, 6)]
    (two, four, six), beside = barrier((moved, beside(below)))
    part = ((part + four) + (two + six)) * scale

    whole_part = jnp.zeros((4,) + part.shape, part.dtype)
    for by in range(4):
        whole_part = put(whole_part, turned(part, by) if by else part, turned_place(-by))
    part = whole_part.reshape(-1, part.shape[1])
    got = swapped(part, "z", 1)
    inner = jnp.where(bit == 0, part, got)[: part.shape[0] - rows]
    outer = jnp.where(bit == 0, got, part)
    inner, outer = barrier((inner, outer))
    near = []
    for value, axis in ((inner, "y"), (outer, "x")):
        near += [rotated(value, axis, 1), rotated(value, axis, 3)]
    near = barrier(near)
    halves = []
    for n in range(2):
        half = near[2 * n].shape[0] // 2
        halves += [near[2 * n][:half], near[2 * n + 1][half:]]
    halves = barrier(halves)
    for n, axis in enumerate(axes):
        halves[2 * n] = rotated(halves[2 * n], axis, 1)
        halves[2 * n + 1] = rotated(halves[2 * n + 1], axis, 3)
    near, halves = barrier((near, halves))
    inner = jnp.concatenate([inner, near[0], *halves[:2], near[1]])
    outer = jnp.concatenate([outer, near[2], *halves[2:], near[3]])
    return inner, outer, beside


def assemble_kernel(where_ref, *refs):
    conv_ref, expand_ref = refs[4:6]
    scratch = refs[6:]
    channels = conv_ref.shape[2]
    core = where_ref[0]
    for n, whole_ref in enumerate(scratch):
        own, got = refs[2 * n : 2 * n + 2]
        rows = own.shape[0] // 4
        for by in range(4):
            piece = slice(by * rows, (by + 1) * rows)
            at = pl.multiple_of(((where_ref[2 - n] + 4 - by) & 3) * rows, 8)
            whole_ref[core, pl.ds(at, rows), :] = own[piece, :]
            whole_ref[1 - core, pl.ds(at, rows), :] = got[piece, :]
    for half in range(2):
        lanes = slice(half * LANES, (half + 1) * LANES)
        for tap in range(6):
            conv_ref[3 + tap, lanes, :] = scratch[0][half, tap * LANES : (tap + 1) * LANES, :]
        for tap in range(3):
            conv_ref[tap, lanes, :] = scratch[1][half, tap * LANES : (tap + 1) * LANES, :]
        for n in range(expand_ref.shape[1] // channels):
            at = (3 + n) * LANES
            expand_ref[lanes, n * channels : (n + 1) * channels] = scratch[1][half, at : at + LANES, :]


def assemble(where, groups, channels, deep):
    refs = [piece for group in groups for piece in group]
    return pl.pallas_call(
        assemble_kernel,
        out_shape=(
            jax.ShapeDtypeStruct((9, channels, channels), jnp.float32),
            jax.ShapeDtypeStruct((channels, deep), jnp.float32),
        ),
        in_specs=[scalars()] + [whole()] * len(refs),
        out_specs=(whole(), whole()),
        scratch_shapes=[pltpu.VMEM((2,) + group[0].shape, jnp.float32) for group in groups],
        compiler_params=params(),
        cost_estimate=pl.CostEstimate(flops=0, bytes_accessed=7 * 10**6, transcendentals=0),
        name="assemble",
    )(where, *refs)


def body(stem_input, stem_preact, deep_cotangent, tissue_tiles, conv_weight, expand_weight):
    _, out_rows, out_cols, channels = stem_preact.shape
    _, all_rows, band, deep = deep_cotangent.shape
    devices = SIZES["x"] * SIZES["z"]
    preact = stem_preact[0]
    cotangent = deep_cotangent[0].reshape(all_rows * band, deep)
    share = tissue_tiles.astype(jnp.float32) / TILES
    core = lax.axis_index("core").astype(jnp.int32)
    where = jnp.stack([core, lax.axis_index("x"), lax.axis_index("y")]).astype(jnp.int32)

    sent, weighted = build_sent(share, cotangent, expand_weight, preact, devices)
    blocks = prepare(stem_input[0])
    above = prepare(shifted(stem_input[0, -1:], 1))
    arrived = exchange(sent, SPACE)
    other_inner, other_outer, grad, first, turned_active = other_terms(
        where, arrived, preact, above, blocks, weighted
    )
    below = shifted(first, -1)

    samples_all = stem_input.shape[0] * SIZES["y"] * SIZES["core"]
    scale = float(samples_all * all_rows * out_cols) ** (-0.5)
    got_inner, got_outer = swapped(other_inner, "core", 1), swapped(other_outer, "core", 1)
    cuts = own_sums(where, grad, turned_active, above, blocks, weighted, got_inner, got_outer)
    inner, outer, grad_input = total_sums(
        cuts, scale, below, lambda b: input_grad(grad, b, conv_weight)
    )
    groups = [(x, swapped(x, "core", 1)) for x in (inner, outer)]
    grad_conv, grad_expand = assemble(where, groups, channels, deep)
    return (grad_input[None], grad_conv.reshape(3, 3, channels, channels), grad_expand)


def solution(mesh):
    fine = Mesh(
        mesh.devices.reshape(SIZES["x"], SIZES["z"], SIZES["y"], SIZES["core"]),
        ("x", "z", "y", "core"),
    )
    return jax.shard_map(
        body,
        mesh=fine,
        in_specs=(
            P(REP, SPACE, None, None),
            P(REP, SPACE, None, None),
            P(REP, None, SPACE, None),
            P(REP),
            P(),
            P(),
        ),
        out_specs=(P(REP, SPACE, None, None), P(), P()),
        check_vma=False,
    )
```

```python
import functools

import jax
import jax.numpy as jnp
from jax import lax
from jax.experimental import pallas as pl
from jax.experimental.pallas import tpu as pltpu
from jax.sharding import Mesh
from jax.sharding import PartitionSpec as P

TILES = 64
LANES = 128
SIZES = {"x": 4, "z": 8, "y": 4, "core": 2}
SPACE = ("x", "z")
REP = ("y", "core")


def whole():
    return pl.BlockSpec(memory_space=pltpu.VMEM)


def far():
    return pl.BlockSpec(memory_space=pl.ANY)


def room(x):
    return pltpu.VMEM(x.shape, x.dtype)


def scalars():
    return pl.BlockSpec(memory_space=pltpu.SMEM)


def params(mib=24):
    return pltpu.CompilerParams(vmem_limit_bytes=mib * 1024 * 1024)


def shifted(x, by):
    length = SIZES["x"] * SIZES["z"]
    pairs = [(i, i + by) for i in range(length) if 0 <= i + by < length]
    return lax.ppermute(x, SPACE, pairs)


def send_kernel(
    share_ref, cotangent_hbm, weight_hbm, preact_hbm, sent_hbm, weighted_hbm,
    cotangent_ref, weight_ref, preact_ref, weighted_ref, sent_ref, sems,
):
    pairs = ((preact_hbm, preact_ref), (weight_hbm, weight_ref), (cotangent_hbm, cotangent_ref))
    copies = [pltpu.make_async_copy(a, b, sems.at[n]) for n, (a, b) in enumerate(pairs)]
    for copy in copies:
        copy.start()
    devices, chunk, channels = sent_ref.shape
    chunk = chunk // 2
    rows, cols = preact_ref.shape[:2]
    band = cols // devices
    copies[0].wait()
    for i in range(rows):
        active = jnp.maximum(preact_ref[i].astype(jnp.float32), 0.0).reshape(devices, band, channels)
        sent_ref[:, chunk + i * band : chunk + (i + 1) * band, :] = active.astype(jnp.bfloat16)
    copies[1].wait()
    copies[2].wait()
    weighted = (cotangent_ref[...].astype(jnp.float32) * share_ref[0]).astype(jnp.bfloat16)
    weighted_ref[...] = weighted
    back = pltpu.make_async_copy(weighted_ref, weighted_hbm, sems.at[3])
    back.start()
    hidden = lax.dot_general(
        weighted, weight_ref[...], (((1,), (1,)), ((), ())), preferred_element_type=jnp.float32
    )
    sent_ref[:, :chunk, :] = hidden.reshape(devices, chunk, channels).astype(jnp.bfloat16)
    out = pltpu.make_async_copy(sent_ref, sent_hbm, sems.at[4])
    out.start()
    back.wait()
    out.wait()


def build_sent(share, cotangent, weight, preact, devices):
    rows, cols, channels = preact.shape
    sent = jax.ShapeDtypeStruct((devices, 2 * rows * cols // devices, channels), jnp.bfloat16)
    return pl.pallas_call(
        send_kernel,
        out_shape=(
            sent,
            jax.ShapeDtypeStruct(cotangent.shape, jnp.bfloat16),
        ),
        in_specs=[scalars()] + [far()] * 3,
        out_specs=(far(), far()),
        scratch_shapes=[room(x) for x in (cotangent, weight, preact, cotangent, sent)]
        + [pltpu.SemaphoreType.DMA((5,))],
        compiler_params=params(60),
        cost_estimate=pl.CostEstimate(flops=268 * 10**6, bytes_accessed=4 * 10**6, transcendentals=0),
        name="build_sent",
    )(share, cotangent, weight, preact)


def prepare_kernel(x_ref, out_ref, wide):
    half = out_ref.shape[2]
    first = lax.broadcasted_iota(jnp.int32, (LANES, half), 1) == 0
    for row in range(x_ref.shape[0]):
        for part in range(x_ref.shape[2] // LANES):
            lanes = slice(part * LANES, (part + 1) * LANES)
            wide[...] = x_ref[row, :, lanes].astype(jnp.float32)
            even = wide[pl.ds(0, half, stride=2), :].T
            odd = wide[pl.ds(1, half, stride=2), :].T
            late = jnp.where(first, 0.0, pltpu.roll(odd, 1, 1))
            out_ref[3 * row, lanes, :] = late.astype(jnp.bfloat16)
            out_ref[3 * row + 1, lanes, :] = even.astype(jnp.bfloat16)
            out_ref[3 * row + 2, lanes, :] = odd.astype(jnp.bfloat16)


def prepare(x):
    rows, cols, channels = x.shape
    return pl.pallas_call(
        prepare_kernel,
        out_shape=jax.ShapeDtypeStruct((3 * rows, channels, cols // 2), jnp.bfloat16),
        in_specs=[whole()],
        out_specs=whole(),
        scratch_shapes=[pltpu.VMEM((cols, LANES), jnp.float32)],
        compiler_params=params(),
        cost_estimate=pl.CostEstimate(flops=10**7, bytes_accessed=3 * 10**6, transcendentals=0),
        name="prepare",
    )(x)


def terms_kernel(
    core_ref, arrived_hbm, preact_hbm, above_hbm, blocks_hbm, weighted_hbm,
    inner_hbm, own_outer, other_outer, grad_hbm, first_hbm,
    arrived_ref, preact_ref, above_ref, blocks_ref, weighted_ref,
    grad_ref, turned, inner_ref, outer_ref, sems,
):
    pairs = (
        (arrived_hbm, arrived_ref),
        (preact_hbm, preact_ref),
        (blocks_hbm, blocks_ref),
        (above_hbm, above_ref),
        (weighted_hbm, weighted_ref),
    )
    copies = [pltpu.make_async_copy(a, b, sems.at[n]) for n, (a, b) in enumerate(pairs)]
    for copy in copies:
        copy.start()
    devices, chunk, channels = arrived_ref.shape
    rows, cols = preact_ref.shape[:2]
    chunk, band = chunk // 2, cols // devices
    copies[0].wait()
    copies[1].wait()
    for i in range(rows):
        hidden = arrived_ref[:, i * band : (i + 1) * band, :].astype(jnp.float32).reshape(cols, channels)
        kept = jnp.where(preact_ref[i].astype(jnp.float32) > 0.0, hidden, 0.0)
        grad_ref[i] = kept.astype(jnp.bfloat16)
    back = [
        pltpu.make_async_copy(grad_ref, grad_hbm, sems.at[5]),
        pltpu.make_async_copy(grad_ref.at[0:1], first_hbm, sems.at[6]),
    ]
    active = arrived_ref[:, chunk:, :].astype(jnp.float32).reshape(devices * chunk, channels)
    turned[...] = active.T.astype(jnp.bfloat16)

    def half_taps(row_tap, col_tap, start):
        total = None
        for i in range(rows):
            row = 2 * i + row_tap - 1
            source, at = (above_ref, col_tap) if row < 0 else (blocks_ref, 3 * row + col_tap)
            term = jnp.dot(
                source[at, pl.ds(start, LANES), :], grad_ref[i], preferred_element_type=jnp.float32
            )
            total = term if total is None else total + term
        return total

    for copy in copies[2:]:
        copy.wait()
    back[0].start()
    back[1].start()
    pieces = inner_hbm.shape[0] // 2
    rows_each = inner_ref.shape[1] // pieces
    for half in range(2):
        for col_tap in range(3):
            for row_tap in (1, 2):
                at = (3 * (row_tap - 1) + col_tap) * LANES
                inner_ref[half, at : at + LANES, :] = half_taps(row_tap, col_tap, half * LANES)
        for n in range(pieces):
            piece = inner_ref.at[half, n * rows_each : (n + 1) * rows_each, :]
            back.append(pltpu.make_async_copy(piece, inner_hbm.at[2 * n + half], sems.at[9 + 2 * n + half]))
            back[-1].start()
    for n, outer_hbm in enumerate((other_outer, own_outer)):
        owner = core_ref[0] if n else 1 - core_ref[0]
        start = pl.multiple_of(owner * LANES, LANES)
        for col_tap in range(3):
            at = col_tap * LANES
            outer_ref[n, at : at + LANES, :] = half_taps(0, col_tap, start)
        for k in range(weighted_ref.shape[1] // channels):
            at = (3 + k) * LANES
            outer_ref[n, at : at + LANES, :] = jnp.dot(
                turned[pl.ds(start, LANES), :],
                weighted_ref[:, k * channels : (k + 1) * channels],
                preferred_element_type=jnp.float32,
            )
        back.append(pltpu.make_async_copy(outer_ref.at[n], outer_hbm, sems.at[7 + n]))
        back[-1].start()
    for copy in back:
        copy.wait()


def terms(core, arrived, preact, above, blocks, weighted):
    rows, cols, channels = preact.shape
    inner = jax.ShapeDtypeStruct((8, 6 * LANES // 4, channels), jnp.float32)
    outer = jax.ShapeDtypeStruct((3 * LANES + weighted.shape[1] // 2, channels), jnp.float32)
    return pl.pallas_call(
        terms_kernel,
        out_shape=(
            inner,
            outer,
            outer,
            jax.ShapeDtypeStruct(preact.shape, jnp.bfloat16),
            jax.ShapeDtypeStruct((1, cols, channels), jnp.bfloat16),
        ),
        in_specs=[scalars()] + [far()] * 5,
        out_specs=(far(),) * 5,
        scratch_shapes=[room(x) for x in (arrived, preact, above, blocks, weighted, preact)]
        + [
            pltpu.VMEM((channels, weighted.shape[0]), jnp.bfloat16),
            pltpu.VMEM((2, 6 * LANES, channels), jnp.float32),
            pltpu.VMEM((2,) + outer.shape, jnp.float32),
            pltpu.SemaphoreType.DMA((17,)),
        ],
        compiler_params=params(54),
        cost_estimate=pl.CostEstimate(flops=870 * 10**6, bytes_accessed=8 * 10**6, transcendentals=0),
        name="terms",
    )(core, arrived, preact, above, blocks, weighted)


def combine_kernel(where_ref, own, got, *out_refs):
    rows = out_refs[0].shape[0]
    for by, out_ref in enumerate(out_refs):
        at = pl.ds(pl.multiple_of(((where_ref[1] + by) & 3) * rows, 8), rows)
        out_ref[...] = own[at, :] + got[at, :]


def combine(where, own, got):
    chunk = jax.ShapeDtypeStruct((own.shape[0] // 4, own.shape[1]), jnp.float32)
    return pl.pallas_call(
        combine_kernel,
        out_shape=(chunk,) * 4,
        in_specs=[scalars()] + [whole()] * 2,
        out_specs=(whole(),) * 4,
        compiler_params=params(24),
        cost_estimate=pl.CostEstimate(flops=10**6, bytes_accessed=3 * 10**6, transcendentals=0),
        name="combine",
    )(where, own, got)


def input_kernel(grad_ref, below_ref, weight_ref, out_ref, wide):
    half = grad_ref.shape[1]
    last = lax.broadcasted_iota(jnp.int32, grad_ref.shape[1:], 0) == half - 1

    def early(g):
        moved = pltpu.roll(g.astype(jnp.float32), half - 1, 0)
        return jnp.where(last, 0.0, moved).astype(jnp.bfloat16)

    grads = [grad_ref[0], grad_ref[1], below_ref[0]]
    moved = [early(g) for g in grads]

    def times(g, row_tap, col_tap):
        return lax.dot_general(
            g,
            weight_ref[row_tap, col_tap],
            (((1,), (1,)), ((), ())),
            preferred_element_type=jnp.float32,
        )

    for row in range(4):
        i = row // 2
        terms = [(i, 1)] if row % 2 == 0 else [(i, 2), (i + 1, 0)]
        even = sum(times(grads[n], p, 1) for n, p in terms)
        odd = sum(times(grads[n], p, 2) + times(moved[n], p, 0) for n, p in terms)
        for part in range(even.shape[1] // LANES):
            lanes = slice(part * LANES, (part + 1) * LANES)
            wide[pl.ds(0, half, stride=2), :] = even[:, lanes]
            wide[pl.ds(1, half, stride=2), :] = odd[:, lanes]
            out_ref[row, :, lanes] = wide[...].astype(jnp.bfloat16)


def input_grad(grad, below, weight):
    rows, half, channels = grad.shape
    return pl.pallas_call(
        input_kernel,
        out_shape=jax.ShapeDtypeStruct((2 * rows, 2 * half, weight.shape[2]), jnp.bfloat16),
        in_specs=[whole()] * 3,
        out_specs=whole(),
        scratch_shapes=[pltpu.VMEM((2 * half, LANES), jnp.float32)],
        compiler_params=params(),
        cost_estimate=pl.CostEstimate(flops=604 * 10**6, bytes_accessed=3 * 10**6, transcendentals=0),
        name="input_grad",
    )(grad, below, weight)


def exchange(x, axis):
    return lax.all_to_all(x, axis, split_axis=0, concat_axis=0, tiled=True)


def place(axis, by=0):
    return (lax.axis_index(axis).astype(jnp.uint32) + jnp.uint32(by % SIZES[axis])) & jnp.uint32(SIZES[axis] - 1)


def pick(parts, index):
    zero = jnp.uint32(0)
    return lax.dynamic_slice(parts, (index, zero, zero), (1,) + parts.shape[1:])[0]


def put(parts, piece, index):
    zero = jnp.uint32(0)
    return lax.dynamic_update_slice(parts, piece[None], (index, zero, zero))


def rotated(x, axis, by):
    size = SIZES[axis]
    return lax.ppermute(x, axis, [(i, (i + by) % size) for i in range(size)])


def split(x):
    return x.reshape(4, x.shape[0] // 4, x.shape[1])


def swapped(x, axis, bit):
    return lax.ppermute(x, axis, [(i, i ^ bit) for i in range(SIZES[axis])])


def turned(x, by):
    pairs = []
    for i in range(SIZES["x"]):
        for k in range(SIZES["z"]):
            for j in range(SIZES["y"]):
                to = (i, (j + by) % 4) if k % 2 else ((i + by) % 4, j)
                pairs.append(((i * SIZES["z"] + k) * 4 + j, (to[0] * SIZES["z"] + k) * 4 + to[1]))
    return lax.ppermute(x, ("x", "z", "y"), pairs)


def turned_place(by=0):
    odd = (place("z") & jnp.uint32(1)) == 1
    return jnp.where(odd, place("y", by), place("x", by))


barrier = lax.optimization_barrier
STEPS = (1, 2, 3)


def total_sums(inner, outer, parts, scale, first, beside):
    moved = barrier([rotated(p, "x", by) for p, by in zip(parts, STEPS)])
    outer = sum(moved, outer)

    rows = outer.shape[0] - inner.shape[0]
    both = jnp.stack([jnp.pad(inner, ((0, rows), (0, 0))), outer])
    bit = place("z") & jnp.uint32(1)
    own, other, first = barrier((pick(both, bit), pick(both, jnp.uint32(1) - bit), first))
    part = own + swapped(other, "z", 1)
    below = shifted(first, -1)

    parts = split(part)
    moved = barrier([pick(parts, turned_place(by)) for by in STEPS])
    moved = [turned(p, by) for p, by in zip(moved, STEPS)]
    part = sum(moved, pick(parts, turned_place()))

    moved = [rotated(part, "z", by) for by in (2, 4, 6)]
    (two, four, six), beside = barrier((moved, beside(below)))
    part = ((part + four) + (two + six)) * scale

    whole_part = jnp.zeros((4,) + part.shape, part.dtype)
    for by in range(4):
        whole_part = put(whole_part, turned(part, by) if by else part, turned_place(-by))
    part = whole_part.reshape(-1, part.shape[1])
    got = swapped(part, "z", 1)
    inner = jnp.where(bit == 0, part, got)[: part.shape[0] - rows]
    outer = jnp.where(bit == 0, got, part)
    inner, outer = barrier((inner, outer))
    inner = lax.all_gather(inner, REP, axis=0, tiled=True)
    return inner, [outer] + [rotated(outer, "x", by) for by in STEPS], beside


def assemble_kernel(where_ref, *refs):
    inner, pieces, (conv_ref, expand_ref, joined) = refs[0], refs[1:9], refs[9:]
    channels = conv_ref.shape[2]
    core = where_ref[0]
    for by in range(4):
        rows = pieces[by].shape[0]
        at = pl.multiple_of(((where_ref[1] + 4 - by) & 3) * rows, 8)
        joined[core, pl.ds(at, rows), :] = pieces[by][...]
        joined[1 - core, pl.ds(at, rows), :] = pieces[4 + by][...]
    rows = inner.shape[0] // 8
    step = LANES // 2
    for half in range(2):
        for at in range(0, 4 * rows, step):
            source = (2 * (at // rows) + half) * rows + at % rows
            target = half * LANES + at % LANES
            conv_ref[3 + at // LANES, target : target + step, :] = inner[source : source + step, :]
    for half in range(2):
        lanes = slice(half * LANES, (half + 1) * LANES)
        for tap in range(3):
            conv_ref[tap, lanes, :] = joined[half, tap * LANES : (tap + 1) * LANES, :]
        for n in range(expand_ref.shape[1] // channels):
            at = (3 + n) * LANES
            expand_ref[lanes, n * channels : (n + 1) * channels] = joined[half, at : at + LANES, :]


def assemble(where, inner, pieces, channels, deep):
    refs = [inner] + pieces
    return pl.pallas_call(
        assemble_kernel,
        out_shape=(
            jax.ShapeDtypeStruct((9, channels, channels), jnp.float32),
            jax.ShapeDtypeStruct((channels, deep), jnp.float32),
        ),
        in_specs=[scalars()] + [whole()] * len(refs),
        out_specs=(whole(), whole()),
        scratch_shapes=[pltpu.VMEM((2, 4 * pieces[0].shape[0], channels), jnp.float32)],
        compiler_params=params(),
        cost_estimate=pl.CostEstimate(flops=0, bytes_accessed=7 * 10**6, transcendentals=0),
        name="assemble",
    )(where, *refs)


def body(stem_input, stem_preact, deep_cotangent, tissue_tiles, conv_weight, expand_weight):
    _, out_rows, out_cols, channels = stem_preact.shape
    _, all_rows, band, deep = deep_cotangent.shape
    devices = SIZES["x"] * SIZES["z"]
    preact = stem_preact[0]
    cotangent = deep_cotangent[0].reshape(all_rows * band, deep)
    share = tissue_tiles.astype(jnp.float32) / TILES
    core = lax.axis_index("core").astype(jnp.int32)
    where = jnp.stack([core, lax.axis_index("x")]).astype(jnp.int32)

    sent, weighted = build_sent(share, cotangent, expand_weight, preact, devices)
    blocks = prepare(stem_input[0])
    above = prepare(shifted(stem_input[0, -1:], 1))
    arrived = exchange(sent, SPACE)
    inner, own, other, grad, first = terms(where[:1], arrived, preact, above, blocks, weighted)
    inner = lax.psum_scatter(inner.reshape(-1, channels), REP, scatter_dimension=0, tiled=True)

    samples_all = stem_input.shape[0] * SIZES["y"] * SIZES["core"]
    scale = float(samples_all * all_rows * out_cols) ** (-0.5)
    outer, *parts = combine(where, own, swapped(other, "core", 1))
    inner, pieces, grad_input = total_sums(
        inner, outer, parts, scale, first, lambda b: input_grad(grad, b, conv_weight)
    )
    pieces = pieces + [swapped(piece, "core", 1) for piece in pieces]
    grad_conv, grad_expand = assemble(where, inner, pieces, channels, deep)
    return (grad_input[None], grad_conv.reshape(3, 3, channels, channels), grad_expand)


def solution(mesh):
    fine = Mesh(
        mesh.devices.reshape(SIZES["x"], SIZES["z"], SIZES["y"], SIZES["core"]),
        ("x", "z", "y", "core"),
    )
    return jax.shard_map(
        body,
        mesh=fine,
        in_specs=(
            P(REP, SPACE, None, None),
            P(REP, SPACE, None, None),
            P(REP, None, SPACE, None),
            P(REP),
            P(),
            P(),
        ),
        out_specs=(P(REP, SPACE, None, None), P(), P()),
        check_vma=False,
    )
```

```python
import functools

import jax
import jax.numpy as jnp
from jax import lax
from jax.experimental import pallas as pl
from jax.experimental.pallas import tpu as pltpu
from jax.sharding import Mesh
from jax.sharding import PartitionSpec as P

TILES = 64
LANES = 128
SIZES = {"x": 4, "z": 8, "y": 4, "core": 2}
SPACE = ("x", "z")
REP = ("y", "core")


def whole():
    return pl.BlockSpec(memory_space=pltpu.VMEM)


def far():
    return pl.BlockSpec(memory_space=pl.ANY)


def room(x):
    return pltpu.VMEM(x.shape, x.dtype)


def scalars():
    return pl.BlockSpec(memory_space=pltpu.SMEM)


def params(mib=24):
    return pltpu.CompilerParams(vmem_limit_bytes=mib * 1024 * 1024)


def shifted(x, by):
    length = SIZES["x"] * SIZES["z"]
    pairs = [(i, i + by) for i in range(length) if 0 <= i + by < length]
    return lax.ppermute(x, SPACE, pairs)


def send_kernel(
    share_ref, cotangent_hbm, weight_hbm, preact_hbm, sent_hbm, weighted_hbm,
    cotangent_ref, weight_ref, preact_ref, weighted_ref, sent_ref, sems,
):
    pairs = ((preact_hbm, preact_ref), (weight_hbm, weight_ref), (cotangent_hbm, cotangent_ref))
    copies = [pltpu.make_async_copy(a, b, sems.at[n]) for n, (a, b) in enumerate(pairs)]
    for copy in copies:
        copy.start()
    devices, chunk, channels = sent_ref.shape
    chunk = chunk // 2
    rows, cols = preact_ref.shape[:2]
    band = cols // devices
    copies[0].wait()
    for i in range(rows):
        active = jnp.maximum(preact_ref[i].astype(jnp.float32), 0.0).reshape(devices, band, channels)
        sent_ref[:, chunk + i * band : chunk + (i + 1) * band, :] = active.astype(jnp.bfloat16)
    copies[1].wait()
    copies[2].wait()
    weighted = (cotangent_ref[...].astype(jnp.float32) * share_ref[0]).astype(jnp.bfloat16)
    weighted_ref[...] = weighted
    back = pltpu.make_async_copy(weighted_ref, weighted_hbm, sems.at[3])
    back.start()
    hidden = lax.dot_general(
        weighted, weight_ref[...], (((1,), (1,)), ((), ())), preferred_element_type=jnp.float32
    )
    sent_ref[:, :chunk, :] = hidden.reshape(devices, chunk, channels).astype(jnp.bfloat16)
    out = pltpu.make_async_copy(sent_ref, sent_hbm, sems.at[4])
    out.start()
    back.wait()
    out.wait()


def build_sent(share, cotangent, weight, preact, devices):
    rows, cols, channels = preact.shape
    sent = jax.ShapeDtypeStruct((devices, 2 * rows * cols // devices, channels), jnp.bfloat16)
    return pl.pallas_call(
        send_kernel,
        out_shape=(
            sent,
            jax.ShapeDtypeStruct(cotangent.shape, jnp.bfloat16),
        ),
        in_specs=[scalars()] + [far()] * 3,
        out_specs=(far(), far()),
        scratch_shapes=[room(x) for x in (cotangent, weight, preact, cotangent, sent)]
        + [pltpu.SemaphoreType.DMA((5,))],
        compiler_params=params(60),
        cost_estimate=pl.CostEstimate(flops=268 * 10**6, bytes_accessed=4 * 10**6, transcendentals=0),
        name="build_sent",
    )(share, cotangent, weight, preact)


def prepare_kernel(x_ref, out_ref, wide):
    half = out_ref.shape[2]
    first = lax.broadcasted_iota(jnp.int32, (LANES, half), 1) == 0
    for row in range(x_ref.shape[0]):
        for part in range(x_ref.shape[2] // LANES):
            lanes = slice(part * LANES, (part + 1) * LANES)
            wide[...] = x_ref[row, :, lanes].astype(jnp.float32)
            even = wide[pl.ds(0, half, stride=2), :].T
            odd = wide[pl.ds(1, half, stride=2), :].T
            late = jnp.where(first, 0.0, pltpu.roll(odd, 1, 1))
            out_ref[3 * row, lanes, :] = late.astype(jnp.bfloat16)
            out_ref[3 * row + 1, lanes, :] = even.astype(jnp.bfloat16)
            out_ref[3 * row + 2, lanes, :] = odd.astype(jnp.bfloat16)


def prepare(x):
    rows, cols, channels = x.shape
    return pl.pallas_call(
        prepare_kernel,
        out_shape=jax.ShapeDtypeStruct((3 * rows, channels, cols // 2), jnp.bfloat16),
        in_specs=[whole()],
        out_specs=whole(),
        scratch_shapes=[pltpu.VMEM((cols, LANES), jnp.float32)],
        compiler_params=params(),
        cost_estimate=pl.CostEstimate(flops=10**7, bytes_accessed=3 * 10**6, transcendentals=0),
        name="prepare",
    )(x)


def terms_kernel(
    core_ref, arrived_hbm, preact_hbm, above_hbm, blocks_hbm, weighted_hbm,
    own_inner, other_inner, own_outer, other_outer, grad_hbm, first_hbm,
    arrived_ref, preact_ref, above_ref, blocks_ref, weighted_ref,
    grad_ref, turned, inner_ref, outer_ref, sems,
):
    pairs = (
        (arrived_hbm, arrived_ref),
        (preact_hbm, preact_ref),
        (blocks_hbm, blocks_ref),
        (above_hbm, above_ref),
        (weighted_hbm, weighted_ref),
    )
    copies = [pltpu.make_async_copy(a, b, sems.at[n]) for n, (a, b) in enumerate(pairs)]
    for copy in copies:
        copy.start()
    devices, chunk, channels = arrived_ref.shape
    rows, cols = preact_ref.shape[:2]
    chunk, band = chunk // 2, cols // devices
    copies[0].wait()
    copies[1].wait()
    for i in range(rows):
        hidden = arrived_ref[:, i * band : (i + 1) * band, :].astype(jnp.float32).reshape(cols, channels)
        kept = jnp.where(preact_ref[i].astype(jnp.float32) > 0.0, hidden, 0.0)
        grad_ref[i] = kept.astype(jnp.bfloat16)
    back = [
        pltpu.make_async_copy(grad_ref, grad_hbm, sems.at[5]),
        pltpu.make_async_copy(grad_ref.at[0:1], first_hbm, sems.at[10]),
    ]
    active = arrived_ref[:, chunk:, :].astype(jnp.float32).reshape(devices * chunk, channels)
    turned[...] = active.T.astype(jnp.bfloat16)

    def half_taps(row_tap, col_tap, start):
        total = None
        for i in range(rows):
            row = 2 * i + row_tap - 1
            source, at = (above_ref, col_tap) if row < 0 else (blocks_ref, 3 * row + col_tap)
            term = jnp.dot(
                source[at, pl.ds(start, LANES), :], grad_ref[i], preferred_element_type=jnp.float32
            )
            total = term if total is None else total + term
        return total

    for copy in copies[2:]:
        copy.wait()
    back[0].start()
    back[1].start()
    for n, (inner_hbm, outer_hbm) in enumerate(((other_inner, other_outer), (own_inner, own_outer))):
        owner = core_ref[0] if n else 1 - core_ref[0]
        start = pl.multiple_of(owner * LANES, LANES)
        for col_tap in range(3):
            for row_tap in (1, 2):
                at = (3 * (row_tap - 1) + col_tap) * LANES
                inner_ref[n, at : at + LANES, :] = half_taps(row_tap, col_tap, start)
        back.append(pltpu.make_async_copy(inner_ref.at[n], inner_hbm, sems.at[6 + 2 * n]))
        back[-1].start()
        for col_tap in range(3):
            at = col_tap * LANES
            outer_ref[n, at : at + LANES, :] = half_taps(0, col_tap, start)
        for k in range(weighted_ref.shape[1] // channels):
            at = (3 + k) * LANES
            outer_ref[n, at : at + LANES, :] = jnp.dot(
                turned[pl.ds(start, LANES), :],
                weighted_ref[:, k * channels : (k + 1) * channels],
                preferred_element_type=jnp.float32,
            )
        back.append(pltpu.make_async_copy(outer_ref.at[n], outer_hbm, sems.at[7 + 2 * n]))
        back[-1].start()
    for copy in back:
        copy.wait()


def terms(core, arrived, preact, above, blocks, weighted):
    rows, cols, channels = preact.shape
    inner = jax.ShapeDtypeStruct((6 * LANES, channels), jnp.float32)
    outer = jax.ShapeDtypeStruct((3 * LANES + weighted.shape[1] // 2, channels), jnp.float32)
    return pl.pallas_call(
        terms_kernel,
        out_shape=(
            inner,
            inner,
            outer,
            outer,
            jax.ShapeDtypeStruct(preact.shape, jnp.bfloat16),
            jax.ShapeDtypeStruct((1, cols, channels), jnp.bfloat16),
        ),
        in_specs=[scalars()] + [far()] * 5,
        out_specs=(far(),) * 6,
        scratch_shapes=[room(x) for x in (arrived, preact, above, blocks, weighted, preact)]
        + [
            pltpu.VMEM((channels, weighted.shape[0]), jnp.bfloat16),
            pltpu.VMEM((2,) + inner.shape, jnp.float32),
            pltpu.VMEM((2,) + outer.shape, jnp.float32),
            pltpu.SemaphoreType.DMA((11,)),
        ],
        compiler_params=params(54),
        cost_estimate=pl.CostEstimate(flops=870 * 10**6, bytes_accessed=8 * 10**6, transcendentals=0),
        name="terms",
    )(core, arrived, preact, above, blocks, weighted)


def combine_kernel(where_ref, own, got, *out_refs):
    rows = out_refs[0].shape[0]
    for by, out_ref in enumerate(out_refs):
        at = pl.ds(pl.multiple_of(((where_ref[1] + by) & 3) * rows, 8), rows)
        out_ref[...] = own[at, :] + got[at, :]


def combine(where, own, got):
    chunk = jax.ShapeDtypeStruct((own.shape[0] // 4, own.shape[1]), jnp.float32)
    return pl.pallas_call(
        combine_kernel,
        out_shape=(chunk,) * 4,
        in_specs=[scalars()] + [whole()] * 2,
        out_specs=(whole(),) * 4,
        compiler_params=params(24),
        cost_estimate=pl.CostEstimate(flops=10**6, bytes_accessed=3 * 10**6, transcendentals=0),
        name="combine",
    )(where, own, got)


def input_kernel(grad_ref, below_ref, weight_ref, out_ref, wide):
    half = grad_ref.shape[1]
    last = lax.broadcasted_iota(jnp.int32, grad_ref.shape[1:], 0) == half - 1

    def early(g):
        moved = pltpu.roll(g.astype(jnp.float32), half - 1, 0)
        return jnp.where(last, 0.0, moved).astype(jnp.bfloat16)

    grads = [grad_ref[0], grad_ref[1], below_ref[0]]
    moved = [early(g) for g in grads]

    def times(g, row_tap, col_tap):
        return lax.dot_general(
            g,
            weight_ref[row_tap, col_tap],
            (((1,), (1,)), ((), ())),
            preferred_element_type=jnp.float32,
        )

    for row in range(4):
        i = row // 2
        terms = [(i, 1)] if row % 2 == 0 else [(i, 2), (i + 1, 0)]
        even = sum(times(grads[n], p, 1) for n, p in terms)
        odd = sum(times(grads[n], p, 2) + times(moved[n], p, 0) for n, p in terms)
        for part in range(even.shape[1] // LANES):
            lanes = slice(part * LANES, (part + 1) * LANES)
            wide[pl.ds(0, half, stride=2), :] = even[:, lanes]
            wide[pl.ds(1, half, stride=2), :] = odd[:, lanes]
            out_ref[row, :, lanes] = wide[...].astype(jnp.bfloat16)


def input_grad(grad, below, weight):
    rows, half, channels = grad.shape
    return pl.pallas_call(
        input_kernel,
        out_shape=jax.ShapeDtypeStruct((2 * rows, 2 * half, weight.shape[2]), jnp.bfloat16),
        in_specs=[whole()] * 3,
        out_specs=whole(),
        scratch_shapes=[pltpu.VMEM((2 * half, LANES), jnp.float32)],
        compiler_params=params(),
        cost_estimate=pl.CostEstimate(flops=604 * 10**6, bytes_accessed=3 * 10**6, transcendentals=0),
        name="input_grad",
    )(grad, below, weight)


def exchange(x, axis):
    return lax.all_to_all(x, axis, split_axis=0, concat_axis=0, tiled=True)


def place(axis, by=0):
    return (lax.axis_index(axis).astype(jnp.uint32) + jnp.uint32(by % SIZES[axis])) & jnp.uint32(SIZES[axis] - 1)


def pick(parts, index):
    zero = jnp.uint32(0)
    return lax.dynamic_slice(parts, (index, zero, zero), (1,) + parts.shape[1:])[0]


def put(parts, piece, index):
    zero = jnp.uint32(0)
    return lax.dynamic_update_slice(parts, piece[None], (index, zero, zero))


def rotated(x, axis, by):
    size = SIZES[axis]
    return lax.ppermute(x, axis, [(i, (i + by) % size) for i in range(size)])


def split(x):
    return x.reshape(4, x.shape[0] // 4, x.shape[1])


def swapped(x, axis, bit):
    return lax.ppermute(x, axis, [(i, i ^ bit) for i in range(SIZES[axis])])


def turned(x, by):
    pairs = []
    for i in range(SIZES["x"]):
        for k in range(SIZES["z"]):
            for j in range(SIZES["y"]):
                to = (i, (j + by) % 4) if k % 2 else ((i + by) % 4, j)
                pairs.append(((i * SIZES["z"] + k) * 4 + j, (to[0] * SIZES["z"] + k) * 4 + to[1]))
    return lax.ppermute(x, ("x", "z", "y"), pairs)


def turned_place(by=0):
    odd = (place("z") & jnp.uint32(1)) == 1
    return jnp.where(odd, place("y", by), place("x", by))


barrier = lax.optimization_barrier
STEPS = (1, 2, 3)


def total_sums(inner, outer, parts, scale, first, beside):
    inner, parts = exchange(split(inner), "y"), barrier(parts)
    moved = [rotated(p, "x", by) for p, by in zip(parts, STEPS)]
    inner, moved = barrier((inner, moved))
    inner = jnp.sum(inner, axis=0)
    outer = sum(moved, outer)

    rows = outer.shape[0] - inner.shape[0]
    both = jnp.stack([jnp.pad(inner, ((0, rows), (0, 0))), outer])
    bit = place("z") & jnp.uint32(1)
    other, first = barrier((pick(both, jnp.uint32(1) - bit), first))
    got, below = barrier((swapped(other, "z", 1), shifted(first, -1)))
    part = pick(both, bit) + got

    parts = split(part)
    moved = barrier([pick(parts, turned_place(by)) for by in STEPS])
    moved = [turned(p, by) for p, by in zip(moved, STEPS)]
    part = sum(moved, pick(parts, turned_place()))

    moved = [rotated(part, "z", by) for by in (2, 4, 6)]
    (two, four, six), beside = barrier((moved, beside(below)))
    part = ((part + four) + (two + six)) * scale

    whole_part = jnp.zeros((4,) + part.shape, part.dtype)
    for by in range(4):
        whole_part = put(whole_part, turned(part, by) if by else part, turned_place(-by))
    part = whole_part.reshape(-1, part.shape[1])
    got = swapped(part, "z", 1)
    inner = jnp.where(bit == 0, part, got)[: part.shape[0] - rows]
    outer = jnp.where(bit == 0, got, part)
    inner, outer = barrier((inner, outer))
    copies = barrier(jnp.broadcast_to(inner, (4,) + inner.shape))
    copies, moved = barrier((exchange(copies, "y"), [rotated(outer, "x", by) for by in STEPS]))
    return [copies.reshape(-1, part.shape[1])], [outer] + moved, beside


def assemble_kernel(where_ref, *refs):
    inner, pieces, (conv_ref, expand_ref, joined) = refs[:2], refs[2:10], refs[10:]
    channels = conv_ref.shape[2]
    core = where_ref[0]
    for by in range(4):
        rows = pieces[by].shape[0]
        at = pl.multiple_of(((where_ref[1] + 4 - by) & 3) * rows, 8)
        joined[core, pl.ds(at, rows), :] = pieces[by][...]
        joined[1 - core, pl.ds(at, rows), :] = pieces[4 + by][...]
    for tap in range(6):
        rows = slice(tap * LANES, (tap + 1) * LANES)
        conv_ref[3 + tap, pl.ds(pl.multiple_of(core * LANES, LANES), LANES), :] = inner[0][rows, :]
        conv_ref[3 + tap, pl.ds(pl.multiple_of((1 - core) * LANES, LANES), LANES), :] = inner[1][rows, :]
    for half in range(2):
        lanes = slice(half * LANES, (half + 1) * LANES)
        for tap in range(3):
            conv_ref[tap, lanes, :] = joined[half, tap * LANES : (tap + 1) * LANES, :]
        for n in range(expand_ref.shape[1] // channels):
            at = (3 + n) * LANES
            expand_ref[lanes, n * channels : (n + 1) * channels] = joined[half, at : at + LANES, :]


def assemble(where, groups, channels, deep):
    refs = [piece for group in groups for piece in group]
    return pl.pallas_call(
        assemble_kernel,
        out_shape=(
            jax.ShapeDtypeStruct((9, channels, channels), jnp.float32),
            jax.ShapeDtypeStruct((channels, deep), jnp.float32),
        ),
        in_specs=[scalars()] + [whole()] * len(refs),
        out_specs=(whole(), whole()),
        scratch_shapes=[pltpu.VMEM((2, 4 * groups[1][0].shape[0], channels), jnp.float32)],
        compiler_params=params(),
        cost_estimate=pl.CostEstimate(flops=0, bytes_accessed=7 * 10**6, transcendentals=0),
        name="assemble",
    )(where, *refs)


def body(stem_input, stem_preact, deep_cotangent, tissue_tiles, conv_weight, expand_weight):
    _, out_rows, out_cols, channels = stem_preact.shape
    _, all_rows, band, deep = deep_cotangent.shape
    devices = SIZES["x"] * SIZES["z"]
    preact = stem_preact[0]
    cotangent = deep_cotangent[0].reshape(all_rows * band, deep)
    share = tissue_tiles.astype(jnp.float32) / TILES
    core = lax.axis_index("core").astype(jnp.int32)
    where = jnp.stack([core, lax.axis_index("x")]).astype(jnp.int32)

    sent, weighted = build_sent(share, cotangent, expand_weight, preact, devices)
    blocks = prepare(stem_input[0])
    above = prepare(shifted(stem_input[0, -1:], 1))
    arrived = exchange(sent, SPACE)
    own_inner, other_inner, own_outer, other_outer, grad, first = terms(
        where[:1], arrived, preact, above, blocks, weighted
    )

    samples_all = stem_input.shape[0] * SIZES["y"] * SIZES["core"]
    scale = float(samples_all * all_rows * out_cols) ** (-0.5)
    inner = own_inner + swapped(other_inner, "core", 1)
    outer, *parts = combine(where, own_outer, swapped(other_outer, "core", 1))
    inner, outer, grad_input = total_sums(
        inner, outer, parts, scale, first, lambda b: input_grad(grad, b, conv_weight)
    )
    groups = [pieces + [swapped(piece, "core", 1) for piece in pieces] for pieces in (inner, outer)]
    grad_conv, grad_expand = assemble(where, groups, channels, deep)
    return (grad_input[None], grad_conv.reshape(3, 3, channels, channels), grad_expand)


def solution(mesh):
    fine = Mesh(
        mesh.devices.reshape(SIZES["x"], SIZES["z"], SIZES["y"], SIZES["core"]),
        ("x", "z", "y", "core"),
    )
    return jax.shard_map(
        body,
        mesh=fine,
        in_specs=(
            P(REP, SPACE, None, None),
            P(REP, SPACE, None, None),
            P(REP, None, SPACE, None),
            P(REP),
            P(),
            P(),
        ),
        out_specs=(P(REP, SPACE, None, None), P(), P()),
        check_vma=False,
    )
```

```python
import functools

import jax
import jax.numpy as jnp
from jax import lax
from jax.experimental import pallas as pl
from jax.experimental.pallas import tpu as pltpu
from jax.sharding import Mesh
from jax.sharding import PartitionSpec as P

TILES = 64
LANES = 128
SIZES = {"x": 4, "z": 8, "y": 4, "core": 2}
SPACE = ("x", "z")
REP = ("y", "core")


def whole():
    return pl.BlockSpec(memory_space=pltpu.VMEM)


def far():
    return pl.BlockSpec(memory_space=pl.ANY)


def room(x):
    return pltpu.VMEM(x.shape, x.dtype)


def scalars():
    return pl.BlockSpec(memory_space=pltpu.SMEM)


def params(mib=24):
    return pltpu.CompilerParams(vmem_limit_bytes=mib * 1024 * 1024)


def shifted(x, by):
    length = SIZES["x"] * SIZES["z"]
    pairs = [(i, i + by) for i in range(length) if 0 <= i + by < length]
    return lax.ppermute(x, SPACE, pairs)


def send_kernel(
    share_ref, cotangent_hbm, weight_hbm, preact_hbm, sent_hbm, weighted_hbm,
    cotangent_ref, weight_ref, preact_ref, weighted_ref, sent_ref, sems,
):
    pairs = ((preact_hbm, preact_ref), (weight_hbm, weight_ref), (cotangent_hbm, cotangent_ref))
    copies = [pltpu.make_async_copy(a, b, sems.at[n]) for n, (a, b) in enumerate(pairs)]
    for copy in copies:
        copy.start()
    devices, chunk, channels = sent_ref.shape
    chunk = chunk // 2
    rows, cols = preact_ref.shape[:2]
    band = cols // devices
    copies[0].wait()
    for i in range(rows):
        active = jnp.maximum(preact_ref[i].astype(jnp.float32), 0.0).reshape(devices, band, channels)
        sent_ref[:, chunk + i * band : chunk + (i + 1) * band, :] = active.astype(jnp.bfloat16)
    copies[1].wait()
    copies[2].wait()
    weighted = (cotangent_ref[...].astype(jnp.float32) * share_ref[0]).astype(jnp.bfloat16)
    weighted_ref[...] = weighted
    back = pltpu.make_async_copy(weighted_ref, weighted_hbm, sems.at[3])
    back.start()
    hidden = lax.dot_general(
        weighted, weight_ref[...], (((1,), (1,)), ((), ())), preferred_element_type=jnp.float32
    )
    sent_ref[:, :chunk, :] = hidden.reshape(devices, chunk, channels).astype(jnp.bfloat16)
    out = pltpu.make_async_copy(sent_ref, sent_hbm, sems.at[4])
    out.start()
    back.wait()
    out.wait()


def build_sent(share, cotangent, weight, preact, devices):
    rows, cols, channels = preact.shape
    sent = jax.ShapeDtypeStruct((devices, 2 * rows * cols // devices, channels), jnp.bfloat16)
    return pl.pallas_call(
        send_kernel,
        out_shape=(
            sent,
            jax.ShapeDtypeStruct(cotangent.shape, jnp.bfloat16),
        ),
        in_specs=[scalars()] + [far()] * 3,
        out_specs=(far(), far()),
        scratch_shapes=[room(x) for x in (cotangent, weight, preact, cotangent, sent)]
        + [pltpu.SemaphoreType.DMA((5,))],
        compiler_params=params(60),
        cost_estimate=pl.CostEstimate(flops=268 * 10**6, bytes_accessed=4 * 10**6, transcendentals=0),
        name="build_sent",
    )(share, cotangent, weight, preact)


def prepare_kernel(x_ref, out_ref, wide):
    half = out_ref.shape[2]
    first = lax.broadcasted_iota(jnp.int32, (LANES, half), 1) == 0
    for row in range(x_ref.shape[0]):
        for part in range(x_ref.shape[2] // LANES):
            lanes = slice(part * LANES, (part + 1) * LANES)
            wide[...] = x_ref[row, :, lanes].astype(jnp.float32)
            even = wide[pl.ds(0, half, stride=2), :].T
            odd = wide[pl.ds(1, half, stride=2), :].T
            late = jnp.where(first, 0.0, pltpu.roll(odd, 1, 1))
            out_ref[3 * row, lanes, :] = late.astype(jnp.bfloat16)
            out_ref[3 * row + 1, lanes, :] = even.astype(jnp.bfloat16)
            out_ref[3 * row + 2, lanes, :] = odd.astype(jnp.bfloat16)


def prepare(x):
    rows, cols, channels = x.shape
    return pl.pallas_call(
        prepare_kernel,
        out_shape=jax.ShapeDtypeStruct((3 * rows, channels, cols // 2), jnp.bfloat16),
        in_specs=[whole()],
        out_specs=whole(),
        scratch_shapes=[pltpu.VMEM((cols, LANES), jnp.float32)],
        compiler_params=params(),
        cost_estimate=pl.CostEstimate(flops=10**7, bytes_accessed=3 * 10**6, transcendentals=0),
        name="prepare",
    )(x)


def terms_kernel(
    core_ref, arrived_hbm, preact_hbm, above_hbm, blocks_hbm, weighted_hbm,
    own_inner, other_inner, own_outer, other_outer, grad_hbm, first_hbm,
    arrived_ref, preact_ref, above_ref, blocks_ref, weighted_ref,
    grad_ref, turned, inner_ref, outer_ref, sems,
):
    pairs = (
        (arrived_hbm, arrived_ref),
        (preact_hbm, preact_ref),
        (blocks_hbm, blocks_ref),
        (above_hbm, above_ref),
        (weighted_hbm, weighted_ref),
    )
    copies = [pltpu.make_async_copy(a, b, sems.at[n]) for n, (a, b) in enumerate(pairs)]
    for copy in copies:
        copy.start()
    devices, chunk, channels = arrived_ref.shape
    rows, cols = preact_ref.shape[:2]
    chunk, band = chunk // 2, cols // devices
    copies[0].wait()
    copies[1].wait()
    for i in range(rows):
        hidden = arrived_ref[:, i * band : (i + 1) * band, :].astype(jnp.float32).reshape(cols, channels)
        kept = jnp.where(preact_ref[i].astype(jnp.float32) > 0.0, hidden, 0.0)
        grad_ref[i] = kept.astype(jnp.bfloat16)
    back = [
        pltpu.make_async_copy(grad_ref, grad_hbm, sems.at[5]),
        pltpu.make_async_copy(grad_ref.at[0:1], first_hbm, sems.at[10]),
    ]
    active = arrived_ref[:, chunk:, :].astype(jnp.float32).reshape(devices * chunk, channels)
    turned[...] = active.T.astype(jnp.bfloat16)

    def half_taps(row_tap, col_tap, start):
        total = None
        for i in range(rows):
            row = 2 * i + row_tap - 1
            source, at = (above_ref, col_tap) if row < 0 else (blocks_ref, 3 * row + col_tap)
            term = jnp.dot(
                source[at, pl.ds(start, LANES), :], grad_ref[i], preferred_element_type=jnp.float32
            )
            total = term if total is None else total + term
        return total

    for copy in copies[2:]:
        copy.wait()
    back[0].start()
    back[1].start()
    for n, (inner_hbm, outer_hbm) in enumerate(((other_inner, other_outer), (own_inner, own_outer))):
        owner = core_ref[0] if n else 1 - core_ref[0]
        start = pl.multiple_of(owner * LANES, LANES)
        for col_tap in range(3):
            for row_tap in (1, 2):
                at = (3 * (row_tap - 1) + col_tap) * LANES
                inner_ref[n, at : at + LANES, :] = half_taps(row_tap, col_tap, start)
        back.append(pltpu.make_async_copy(inner_ref.at[n], inner_hbm, sems.at[6 + 2 * n]))
        back[-1].start()
        for col_tap in range(3):
            at = col_tap * LANES
            outer_ref[n, at : at + LANES, :] = half_taps(0, col_tap, start)
        for k in range(weighted_ref.shape[1] // channels):
            at = (3 + k) * LANES
            outer_ref[n, at : at + LANES, :] = jnp.dot(
                turned[pl.ds(start, LANES), :],
                weighted_ref[:, k * channels : (k + 1) * channels],
                preferred_element_type=jnp.float32,
            )
        back.append(pltpu.make_async_copy(outer_ref.at[n], outer_hbm, sems.at[7 + 2 * n]))
        back[-1].start()
    for copy in back:
        copy.wait()


def terms(core, arrived, preact, above, blocks, weighted):
    rows, cols, channels = preact.shape
    inner = jax.ShapeDtypeStruct((6 * LANES, channels), jnp.float32)
    outer = jax.ShapeDtypeStruct((3 * LANES + weighted.shape[1] // 2, channels), jnp.float32)
    return pl.pallas_call(
        terms_kernel,
        out_shape=(
            inner,
            inner,
            outer,
            outer,
            jax.ShapeDtypeStruct(preact.shape, jnp.bfloat16),
            jax.ShapeDtypeStruct((1, cols, channels), jnp.bfloat16),
        ),
        in_specs=[scalars()] + [far()] * 5,
        out_specs=(far(),) * 6,
        scratch_shapes=[room(x) for x in (arrived, preact, above, blocks, weighted, preact)]
        + [
            pltpu.VMEM((channels, weighted.shape[0]), jnp.bfloat16),
            pltpu.VMEM((2,) + inner.shape, jnp.float32),
            pltpu.VMEM((2,) + outer.shape, jnp.float32),
            pltpu.SemaphoreType.DMA((11,)),
        ],
        compiler_params=params(54),
        cost_estimate=pl.CostEstimate(flops=870 * 10**6, bytes_accessed=8 * 10**6, transcendentals=0),
        name="terms",
    )(core, arrived, preact, above, blocks, weighted)


def add_kernel(own, got, out_ref):
    out_ref[...] = own[...] + got[...]


def add(own, got):
    return pl.pallas_call(
        add_kernel,
        out_shape=jax.ShapeDtypeStruct(own.shape, own.dtype),
        in_specs=[whole()] * 2,
        out_specs=whole(),
        compiler_params=params(24),
        cost_estimate=pl.CostEstimate(flops=10**5, bytes_accessed=2 * 10**6, transcendentals=0),
        name="add",
    )(own, got)


def combine_kernel(where_ref, own, got, *out_refs):
    rows = out_refs[0].shape[0]
    for by, out_ref in enumerate(out_refs):
        at = pl.ds(pl.multiple_of(((where_ref[1] + by) & 3) * rows, 8), rows)
        out_ref[...] = own[at, :] + got[at, :]


def combine(where, own, got):
    chunk = jax.ShapeDtypeStruct((own.shape[0] // 4, own.shape[1]), jnp.float32)
    return pl.pallas_call(
        combine_kernel,
        out_shape=(chunk,) * 4,
        in_specs=[scalars()] + [whole()] * 2,
        out_specs=(whole(),) * 4,
        compiler_params=params(24),
        cost_estimate=pl.CostEstimate(flops=10**6, bytes_accessed=3 * 10**6, transcendentals=0),
        name="combine",
    )(where, own, got)


def input_kernel(grad_ref, below_ref, weight_ref, out_ref, wide):
    half = grad_ref.shape[1]
    last = lax.broadcasted_iota(jnp.int32, grad_ref.shape[1:], 0) == half - 1

    def early(g):
        moved = pltpu.roll(g.astype(jnp.float32), half - 1, 0)
        return jnp.where(last, 0.0, moved).astype(jnp.bfloat16)

    grads = [grad_ref[0], grad_ref[1], below_ref[0]]
    moved = [early(g) for g in grads]

    def times(g, row_tap, col_tap):
        return lax.dot_general(
            g,
            weight_ref[row_tap, col_tap],
            (((1,), (1,)), ((), ())),
            preferred_element_type=jnp.float32,
        )

    for row in range(4):
        i = row // 2
        terms = [(i, 1)] if row % 2 == 0 else [(i, 2), (i + 1, 0)]
        even = sum(times(grads[n], p, 1) for n, p in terms)
        odd = sum(times(grads[n], p, 2) + times(moved[n], p, 0) for n, p in terms)
        for part in range(even.shape[1] // LANES):
            lanes = slice(part * LANES, (part + 1) * LANES)
            wide[pl.ds(0, half, stride=2), :] = even[:, lanes]
            wide[pl.ds(1, half, stride=2), :] = odd[:, lanes]
            out_ref[row, :, lanes] = wide[...].astype(jnp.bfloat16)


def input_grad(grad, below, weight):
    rows, half, channels = grad.shape
    return pl.pallas_call(
        input_kernel,
        out_shape=jax.ShapeDtypeStruct((2 * rows, 2 * half, weight.shape[2]), jnp.bfloat16),
        in_specs=[whole()] * 3,
        out_specs=whole(),
        scratch_shapes=[pltpu.VMEM((2 * half, LANES), jnp.float32)],
        compiler_params=params(),
        cost_estimate=pl.CostEstimate(flops=604 * 10**6, bytes_accessed=3 * 10**6, transcendentals=0),
        name="input_grad",
    )(grad, below, weight)


def exchange(x, axis):
    return lax.all_to_all(x, axis, split_axis=0, concat_axis=0, tiled=True)


def place(axis, by=0):
    return (lax.axis_index(axis).astype(jnp.uint32) + jnp.uint32(by % SIZES[axis])) & jnp.uint32(SIZES[axis] - 1)


def pick(parts, index):
    zero = jnp.uint32(0)
    return lax.dynamic_slice(parts, (index, zero, zero), (1,) + parts.shape[1:])[0]


def put(parts, piece, index):
    zero = jnp.uint32(0)
    return lax.dynamic_update_slice(parts, piece[None], (index, zero, zero))


def rotated(x, axis, by):
    size = SIZES[axis]
    return lax.ppermute(x, axis, [(i, (i + by) % size) for i in range(size)])


def split(x):
    return x.reshape(4, x.shape[0] // 4, x.shape[1])


def swapped(x, axis, bit):
    return lax.ppermute(x, axis, [(i, i ^ bit) for i in range(SIZES[axis])])


def turned(x, by):
    pairs = []
    for i in range(SIZES["x"]):
        for k in range(SIZES["z"]):
            for j in range(SIZES["y"]):
                to = (i, (j + by) % 4) if k % 2 else ((i + by) % 4, j)
                pairs.append(((i * SIZES["z"] + k) * 4 + j, (to[0] * SIZES["z"] + k) * 4 + to[1]))
    return lax.ppermute(x, ("x", "z", "y"), pairs)


def turned_place(by=0):
    odd = (place("z") & jnp.uint32(1)) == 1
    return jnp.where(odd, place("y", by), place("x", by))


barrier = lax.optimization_barrier
STEPS = (1, 2, 3)


def total_sums(inner, outer, parts, scale, first, beside):
    inner, parts = exchange(split(inner), "y"), barrier(parts)
    moved = [rotated(p, "x", by) for p, by in zip(parts, STEPS)]
    inner, moved = barrier((inner, moved))
    inner = jnp.sum(inner, axis=0)
    outer = sum(moved, outer)

    rows = outer.shape[0] - inner.shape[0]
    both = jnp.stack([jnp.pad(inner, ((0, rows), (0, 0))), outer])
    bit = place("z") & jnp.uint32(1)
    part = pick(both, bit) + swapped(pick(both, jnp.uint32(1) - bit), "z", 1)

    parts = split(part)
    moved, first = barrier(([pick(parts, turned_place(by)) for by in STEPS], first))
    moved = [turned(p, by) for p, by in zip(moved, STEPS)]
    below = shifted(first, -1)
    part = sum(moved, pick(parts, turned_place()))

    moved = [rotated(part, "z", by) for by in (2, 4, 6)]
    (two, four, six), beside = barrier((moved, beside(below)))
    part = ((part + four) + (two + six)) * scale

    whole_part = jnp.zeros((4,) + part.shape, part.dtype)
    for by in range(4):
        whole_part = put(whole_part, turned(part, by) if by else part, turned_place(-by))
    part = whole_part.reshape(-1, part.shape[1])
    got = swapped(part, "z", 1)
    inner = jnp.where(bit == 0, part, got)[: part.shape[0] - rows]
    outer = jnp.where(bit == 0, got, part)
    inner, outer = barrier((inner, outer))
    copies = barrier(jnp.broadcast_to(inner, (4,) + inner.shape))
    copies, moved = barrier((exchange(copies, "y"), [rotated(outer, "x", by) for by in STEPS]))
    return [copies.reshape(-1, part.shape[1])], [outer] + moved, beside


def assemble_kernel(where_ref, *refs):
    inner, pieces, (conv_ref, expand_ref, joined) = refs[:2], refs[2:10], refs[10:]
    channels = conv_ref.shape[2]
    core = where_ref[0]
    for by in range(4):
        rows = pieces[by].shape[0]
        at = pl.multiple_of(((where_ref[1] + 4 - by) & 3) * rows, 8)
        joined[core, pl.ds(at, rows), :] = pieces[by][...]
        joined[1 - core, pl.ds(at, rows), :] = pieces[4 + by][...]
    for tap in range(6):
        rows = slice(tap * LANES, (tap + 1) * LANES)
        conv_ref[3 + tap, pl.ds(pl.multiple_of(core * LANES, LANES), LANES), :] = inner[0][rows, :]
        conv_ref[3 + tap, pl.ds(pl.multiple_of((1 - core) * LANES, LANES), LANES), :] = inner[1][rows, :]
    for half in range(2):
        lanes = slice(half * LANES, (half + 1) * LANES)
        for tap in range(3):
            conv_ref[tap, lanes, :] = joined[half, tap * LANES : (tap + 1) * LANES, :]
        for n in range(expand_ref.shape[1] // channels):
            at = (3 + n) * LANES
            expand_ref[lanes, n * channels : (n + 1) * channels] = joined[half, at : at + LANES, :]


def assemble(where, groups, channels, deep):
    refs = [piece for group in groups for piece in group]
    return pl.pallas_call(
        assemble_kernel,
        out_shape=(
            jax.ShapeDtypeStruct((9, channels, channels), jnp.float32),
            jax.ShapeDtypeStruct((channels, deep), jnp.float32),
        ),
        in_specs=[scalars()] + [whole()] * len(refs),
        out_specs=(whole(), whole()),
        scratch_shapes=[pltpu.VMEM((2, 4 * groups[1][0].shape[0], channels), jnp.float32)],
        compiler_params=params(),
        cost_estimate=pl.CostEstimate(flops=0, bytes_accessed=7 * 10**6, transcendentals=0),
        name="assemble",
    )(where, *refs)


def body(stem_input, stem_preact, deep_cotangent, tissue_tiles, conv_weight, expand_weight):
    _, out_rows, out_cols, channels = stem_preact.shape
    _, all_rows, band, deep = deep_cotangent.shape
    devices = SIZES["x"] * SIZES["z"]
    preact = stem_preact[0]
    cotangent = deep_cotangent[0].reshape(all_rows * band, deep)
    share = tissue_tiles.astype(jnp.float32) / TILES
    core = lax.axis_index("core").astype(jnp.int32)
    where = jnp.stack([core, lax.axis_index("x")]).astype(jnp.int32)

    sent, weighted = build_sent(share, cotangent, expand_weight, preact, devices)
    blocks = prepare(stem_input[0])
    above = prepare(shifted(stem_input[0, -1:], 1))
    arrived = exchange(sent, SPACE)
    own_inner, other_inner, own_outer, other_outer, grad, first = terms(
        where[:1], arrived, preact, above, blocks, weighted
    )

    samples_all = stem_input.shape[0] * SIZES["y"] * SIZES["core"]
    scale = float(samples_all * all_rows * out_cols) ** (-0.5)
    inner = add(own_inner, swapped(other_inner, "core", 1))
    outer, *parts = combine(where, own_outer, swapped(other_outer, "core", 1))
    inner, outer, grad_input = total_sums(
        inner, outer, parts, scale, first, lambda b: input_grad(grad, b, conv_weight)
    )
    groups = [pieces + [swapped(piece, "core", 1) for piece in pieces] for pieces in (inner, outer)]
    grad_conv, grad_expand = assemble(where, groups, channels, deep)
    return (grad_input[None], grad_conv.reshape(3, 3, channels, channels), grad_expand)


def solution(mesh):
    fine = Mesh(
        mesh.devices.reshape(SIZES["x"], SIZES["z"], SIZES["y"], SIZES["core"]),
        ("x", "z", "y", "core"),
    )
    return jax.shard_map(
        body,
        mesh=fine,
        in_specs=(
            P(REP, SPACE, None, None),
            P(REP, SPACE, None, None),
            P(REP, None, SPACE, None),
            P(REP),
            P(),
            P(),
        ),
        out_specs=(P(REP, SPACE, None, None), P(), P()),
        check_vma=False,
    )
```

```python
import functools

import jax
import jax.numpy as jnp
from jax import lax
from jax.experimental import pallas as pl
from jax.experimental.pallas import tpu as pltpu
from jax.sharding import Mesh
from jax.sharding import PartitionSpec as P

TILES = 64
LANES = 128
INNER_TAPS = ((1, 0), (1, 1), (1, 2), (2, 0), (2, 1), (2, 2), (0, 0))
OUTER_TAPS = ((0, 1), (0, 2))
SIZES = {"x": 4, "z": 8, "y": 4, "core": 2}
SPACE = ("x", "z")
REP = ("y", "core")


def whole():
    return pl.BlockSpec(memory_space=pltpu.VMEM)


def far():
    return pl.BlockSpec(memory_space=pl.ANY)


def room(x):
    return pltpu.VMEM(x.shape, x.dtype)


def scalars():
    return pl.BlockSpec(memory_space=pltpu.SMEM)


def params(mib=24):
    return pltpu.CompilerParams(vmem_limit_bytes=mib * 1024 * 1024)


def shifted(x, by):
    length = SIZES["x"] * SIZES["z"]
    pairs = [(i, i + by) for i in range(length) if 0 <= i + by < length]
    return lax.ppermute(x, SPACE, pairs)


def send_kernel(
    share_ref, cotangent_hbm, weight_hbm, preact_hbm, sent_hbm, weighted_hbm,
    cotangent_ref, weight_ref, preact_ref, weighted_ref, sent_ref, sems,
):
    pairs = ((preact_hbm, preact_ref), (weight_hbm, weight_ref), (cotangent_hbm, cotangent_ref))
    copies = [pltpu.make_async_copy(a, b, sems.at[n]) for n, (a, b) in enumerate(pairs)]
    for copy in copies:
        copy.start()
    devices, chunk, channels = sent_ref.shape
    chunk = chunk // 2
    rows, cols = preact_ref.shape[:2]
    band = cols // devices
    copies[0].wait()
    for i in range(rows):
        active = jnp.maximum(preact_ref[i].astype(jnp.float32), 0.0).reshape(devices, band, channels)
        sent_ref[:, chunk + i * band : chunk + (i + 1) * band, :] = active.astype(jnp.bfloat16)
    copies[1].wait()
    copies[2].wait()
    weighted = (cotangent_ref[...].astype(jnp.float32) * share_ref[0]).astype(jnp.bfloat16)
    weighted_ref[...] = weighted
    back = pltpu.make_async_copy(weighted_ref, weighted_hbm, sems.at[3])
    back.start()
    hidden = lax.dot_general(
        weighted, weight_ref[...], (((1,), (1,)), ((), ())), preferred_element_type=jnp.float32
    )
    sent_ref[:, :chunk, :] = hidden.reshape(devices, chunk, channels).astype(jnp.bfloat16)
    out = pltpu.make_async_copy(sent_ref, sent_hbm, sems.at[4])
    out.start()
    back.wait()
    out.wait()


def build_sent(share, cotangent, weight, preact, devices):
    rows, cols, channels = preact.shape
    sent = jax.ShapeDtypeStruct((devices, 2 * rows * cols // devices, channels), jnp.bfloat16)
    return pl.pallas_call(
        send_kernel,
        out_shape=(
            sent,
            jax.ShapeDtypeStruct(cotangent.shape, jnp.bfloat16),
        ),
        in_specs=[scalars()] + [far()] * 3,
        out_specs=(far(), far()),
        scratch_shapes=[room(x) for x in (cotangent, weight, preact, cotangent, sent)]
        + [pltpu.SemaphoreType.DMA((5,))],
        compiler_params=params(60),
        cost_estimate=pl.CostEstimate(flops=268 * 10**6, bytes_accessed=4 * 10**6, transcendentals=0),
        name="build_sent",
    )(share, cotangent, weight, preact)


def prepare_kernel(x_ref, out_ref, wide):
    half = out_ref.shape[2]
    first = lax.broadcasted_iota(jnp.int32, (LANES, half), 1) == 0
    for row in range(x_ref.shape[0]):
        for part in range(x_ref.shape[2] // LANES):
            lanes = slice(part * LANES, (part + 1) * LANES)
            wide[...] = x_ref[row, :, lanes].astype(jnp.float32)
            even = wide[pl.ds(0, half, stride=2), :].T
            odd = wide[pl.ds(1, half, stride=2), :].T
            late = jnp.where(first, 0.0, pltpu.roll(odd, 1, 1))
            out_ref[3 * row, lanes, :] = late.astype(jnp.bfloat16)
            out_ref[3 * row + 1, lanes, :] = even.astype(jnp.bfloat16)
            out_ref[3 * row + 2, lanes, :] = odd.astype(jnp.bfloat16)


def prepare(x):
    rows, cols, channels = x.shape
    return pl.pallas_call(
        prepare_kernel,
        out_shape=jax.ShapeDtypeStruct((3 * rows, channels, cols // 2), jnp.bfloat16),
        in_specs=[whole()],
        out_specs=whole(),
        scratch_shapes=[pltpu.VMEM((cols, LANES), jnp.float32)],
        compiler_params=params(),
        cost_estimate=pl.CostEstimate(flops=10**7, bytes_accessed=3 * 10**6, transcendentals=0),
        name="prepare",
    )(x)


def terms_kernel(
    core_ref, arrived_hbm, preact_hbm, above_hbm, blocks_hbm, weighted_hbm,
    own_inner, other_inner, own_outer, other_outer, grad_hbm, first_hbm,
    arrived_ref, preact_ref, above_ref, blocks_ref, weighted_ref,
    grad_ref, turned, inner_ref, outer_ref, sems,
):
    pairs = (
        (arrived_hbm, arrived_ref),
        (preact_hbm, preact_ref),
        (blocks_hbm, blocks_ref),
        (above_hbm, above_ref),
        (weighted_hbm, weighted_ref),
    )
    copies = [pltpu.make_async_copy(a, b, sems.at[n]) for n, (a, b) in enumerate(pairs)]
    for copy in copies:
        copy.start()
    devices, chunk, channels = arrived_ref.shape
    rows, cols = preact_ref.shape[:2]
    chunk, band = chunk // 2, cols // devices
    copies[0].wait()
    copies[1].wait()
    for i in range(rows):
        hidden = arrived_ref[:, i * band : (i + 1) * band, :].astype(jnp.float32).reshape(cols, channels)
        kept = jnp.where(preact_ref[i].astype(jnp.float32) > 0.0, hidden, 0.0)
        grad_ref[i] = kept.astype(jnp.bfloat16)
    back = [
        pltpu.make_async_copy(grad_ref, grad_hbm, sems.at[5]),
        pltpu.make_async_copy(grad_ref.at[0:1], first_hbm, sems.at[10]),
    ]
    active = arrived_ref[:, chunk:, :].astype(jnp.float32).reshape(devices * chunk, channels)
    turned[...] = active.T.astype(jnp.bfloat16)

    def half_taps(row_tap, col_tap, start):
        total = None
        for i in range(rows):
            row = 2 * i + row_tap - 1
            source, at = (above_ref, col_tap) if row < 0 else (blocks_ref, 3 * row + col_tap)
            term = jnp.dot(
                source[at, pl.ds(start, LANES), :], grad_ref[i], preferred_element_type=jnp.float32
            )
            total = term if total is None else total + term
        return total

    for copy in copies[2:]:
        copy.wait()
    back[0].start()
    back[1].start()
    for n, (inner_hbm, outer_hbm) in enumerate(((other_inner, other_outer), (own_inner, own_outer))):
        owner = core_ref[0] if n else 1 - core_ref[0]
        start = pl.multiple_of(owner * LANES, LANES)
        for at, (row_tap, col_tap) in enumerate(INNER_TAPS):
            inner_ref[n, at * LANES : (at + 1) * LANES, :] = half_taps(row_tap, col_tap, start)
        back.append(pltpu.make_async_copy(inner_ref.at[n], inner_hbm, sems.at[6 + 2 * n]))
        back[-1].start()
        for at, (row_tap, col_tap) in enumerate(OUTER_TAPS):
            outer_ref[n, at * LANES : (at + 1) * LANES, :] = half_taps(row_tap, col_tap, start)
        for k in range(weighted_ref.shape[1] // channels):
            at = (len(OUTER_TAPS) + k) * LANES
            outer_ref[n, at : at + LANES, :] = jnp.dot(
                turned[pl.ds(start, LANES), :],
                weighted_ref[:, k * channels : (k + 1) * channels],
                preferred_element_type=jnp.float32,
            )
        back.append(pltpu.make_async_copy(outer_ref.at[n], outer_hbm, sems.at[7 + 2 * n]))
        back[-1].start()
    for copy in back:
        copy.wait()


def terms(core, arrived, preact, above, blocks, weighted):
    rows, cols, channels = preact.shape
    inner = jax.ShapeDtypeStruct((len(INNER_TAPS) * LANES, channels), jnp.float32)
    outer = jax.ShapeDtypeStruct((len(OUTER_TAPS) * LANES + weighted.shape[1] // 2, channels), jnp.float32)
    return pl.pallas_call(
        terms_kernel,
        out_shape=(
            inner,
            inner,
            outer,
            outer,
            jax.ShapeDtypeStruct(preact.shape, jnp.bfloat16),
            jax.ShapeDtypeStruct((1, cols, channels), jnp.bfloat16),
        ),
        in_specs=[scalars()] + [far()] * 5,
        out_specs=(far(),) * 6,
        scratch_shapes=[room(x) for x in (arrived, preact, above, blocks, weighted, preact)]
        + [
            pltpu.VMEM((channels, weighted.shape[0]), jnp.bfloat16),
            pltpu.VMEM((2,) + inner.shape, jnp.float32),
            pltpu.VMEM((2,) + outer.shape, jnp.float32),
            pltpu.SemaphoreType.DMA((11,)),
        ],
        compiler_params=params(54),
        cost_estimate=pl.CostEstimate(flops=870 * 10**6, bytes_accessed=8 * 10**6, transcendentals=0),
        name="terms",
    )(core, arrived, preact, above, blocks, weighted)


def add_kernel(own, got, out_ref):
    out_ref[...] = own[...] + got[...]


def add(own, got):
    return pl.pallas_call(
        add_kernel,
        out_shape=jax.ShapeDtypeStruct(own.shape, own.dtype),
        in_specs=[whole()] * 2,
        out_specs=whole(),
        compiler_params=params(24),
        cost_estimate=pl.CostEstimate(flops=10**5, bytes_accessed=2 * 10**6, transcendentals=0),
        name="add",
    )(own, got)


def combine_kernel(where_ref, own, got, *out_refs):
    rows = out_refs[0].shape[0]
    for by, out_ref in enumerate(out_refs):
        at = pl.ds(pl.multiple_of(((where_ref[1] + by) & 3) * rows, 8), rows)
        out_ref[...] = own[at, :] + got[at, :]


def combine(where, own, got):
    chunk = jax.ShapeDtypeStruct((own.shape[0] // 4, own.shape[1]), jnp.float32)
    return pl.pallas_call(
        combine_kernel,
        out_shape=(chunk,) * 4,
        in_specs=[scalars()] + [whole()] * 2,
        out_specs=(whole(),) * 4,
        compiler_params=params(24),
        cost_estimate=pl.CostEstimate(flops=10**6, bytes_accessed=3 * 10**6, transcendentals=0),
        name="combine",
    )(where, own, got)


def input_kernel(grad_ref, below_ref, weight_ref, out_ref, wide):
    half = grad_ref.shape[1]
    last = lax.broadcasted_iota(jnp.int32, grad_ref.shape[1:], 0) == half - 1

    def early(g):
        moved = pltpu.roll(g.astype(jnp.float32), half - 1, 0)
        return jnp.where(last, 0.0, moved).astype(jnp.bfloat16)

    grads = [grad_ref[0], grad_ref[1], below_ref[0]]
    moved = [early(g) for g in grads]

    def times(g, row_tap, col_tap):
        return lax.dot_general(
            g,
            weight_ref[row_tap, col_tap],
            (((1,), (1,)), ((), ())),
            preferred_element_type=jnp.float32,
        )

    for row in range(4):
        i = row // 2
        terms = [(i, 1)] if row % 2 == 0 else [(i, 2), (i + 1, 0)]
        even = sum(times(grads[n], p, 1) for n, p in terms)
        odd = sum(times(grads[n], p, 2) + times(moved[n], p, 0) for n, p in terms)
        for part in range(even.shape[1] // LANES):
            lanes = slice(part * LANES, (part + 1) * LANES)
            wide[pl.ds(0, half, stride=2), :] = even[:, lanes]
            wide[pl.ds(1, half, stride=2), :] = odd[:, lanes]
            out_ref[row, :, lanes] = wide[...].astype(jnp.bfloat16)


def input_grad(grad, below, weight):
    rows, half, channels = grad.shape
    return pl.pallas_call(
        input_kernel,
        out_shape=jax.ShapeDtypeStruct((2 * rows, 2 * half, weight.shape[2]), jnp.bfloat16),
        in_specs=[whole()] * 3,
        out_specs=whole(),
        scratch_shapes=[pltpu.VMEM((2 * half, LANES), jnp.float32)],
        compiler_params=params(),
        cost_estimate=pl.CostEstimate(flops=604 * 10**6, bytes_accessed=3 * 10**6, transcendentals=0),
        name="input_grad",
    )(grad, below, weight)


def exchange(x, axis):
    return lax.all_to_all(x, axis, split_axis=0, concat_axis=0, tiled=True)


def place(axis, by=0):
    return (lax.axis_index(axis).astype(jnp.uint32) + jnp.uint32(by % SIZES[axis])) & jnp.uint32(SIZES[axis] - 1)


def pick(parts, index):
    zero = jnp.uint32(0)
    return lax.dynamic_slice(parts, (index, zero, zero), (1,) + parts.shape[1:])[0]


def put(parts, piece, index):
    zero = jnp.uint32(0)
    return lax.dynamic_update_slice(parts, piece[None], (index, zero, zero))


def rotated(x, axis, by):
    size = SIZES[axis]
    return lax.ppermute(x, axis, [(i, (i + by) % size) for i in range(size)])


def split(x):
    return x.reshape(4, x.shape[0] // 4, x.shape[1])


def swapped(x, axis, bit):
    return lax.ppermute(x, axis, [(i, i ^ bit) for i in range(SIZES[axis])])


def turned(x, by):
    pairs = []
    for i in range(SIZES["x"]):
        for k in range(SIZES["z"]):
            for j in range(SIZES["y"]):
                to = (i, (j + by) % 4) if k % 2 else ((i + by) % 4, j)
                pairs.append(((i * SIZES["z"] + k) * 4 + j, (to[0] * SIZES["z"] + k) * 4 + to[1]))
    return lax.ppermute(x, ("x", "z", "y"), pairs)


def turned_place(by=0):
    odd = (place("z") & jnp.uint32(1)) == 1
    return jnp.where(odd, place("y", by), place("x", by))


barrier = lax.optimization_barrier
STEPS = (1, 2, 3)


def total_sums(inner, outer, parts, scale, first, beside):
    inner, parts = exchange(split(inner), "y"), barrier(parts)
    moved = [rotated(p, "x", by) for p, by in zip(parts, STEPS)]
    inner, moved = barrier((inner, moved))
    inner = jnp.sum(inner, axis=0)
    outer = sum(moved, outer)

    rows = inner.shape[0] - outer.shape[0]
    both = jnp.stack([inner, jnp.pad(outer, ((0, rows), (0, 0)))])
    bit = place("z") & jnp.uint32(1)
    part = pick(both, bit) + swapped(pick(both, jnp.uint32(1) - bit), "z", 1)

    parts = split(part)
    moved, first = barrier(([pick(parts, turned_place(by)) for by in STEPS], first))
    moved = [turned(p, by) for p, by in zip(moved, STEPS)]
    below = shifted(first, -1)
    part = sum(moved, pick(parts, turned_place()))

    moved = [rotated(part, "z", by) for by in (2, 4, 6)]
    (two, four, six), beside = barrier((moved, beside(below)))
    part = ((part + four) + (two + six)) * scale

    whole_part = jnp.zeros((4,) + part.shape, part.dtype)
    for by in range(4):
        whole_part = put(whole_part, turned(part, by) if by else part, turned_place(-by))
    part = whole_part.reshape(-1, part.shape[1])
    got = swapped(part, "z", 1)
    inner = jnp.where(bit == 0, part, got)
    outer = jnp.where(bit == 0, got, part)[: part.shape[0] - rows]
    copies = barrier(jnp.broadcast_to(inner, (4,) + inner.shape))
    copies, moved = barrier((exchange(copies, "y"), [rotated(outer, "x", by) for by in STEPS]))
    return [copies.reshape(-1, part.shape[1])], [outer] + moved, beside


def assemble_kernel(where_ref, *refs):
    inner, pieces, (conv_ref, expand_ref, joined) = refs[:2], refs[2:10], refs[10:]
    channels = conv_ref.shape[2]
    core = where_ref[0]
    for by in range(4):
        rows = pieces[by].shape[0]
        at = pl.multiple_of(((where_ref[1] + 4 - by) & 3) * rows, 8)
        joined[core, pl.ds(at, rows), :] = pieces[by][...]
        joined[1 - core, pl.ds(at, rows), :] = pieces[4 + by][...]
    for at, (row_tap, col_tap) in enumerate(INNER_TAPS):
        rows, tap = slice(at * LANES, (at + 1) * LANES), 3 * row_tap + col_tap
        conv_ref[tap, pl.ds(pl.multiple_of(core * LANES, LANES), LANES), :] = inner[0][rows, :]
        conv_ref[tap, pl.ds(pl.multiple_of((1 - core) * LANES, LANES), LANES), :] = inner[1][rows, :]
    for half in range(2):
        lanes = slice(half * LANES, (half + 1) * LANES)
        for at, (row_tap, col_tap) in enumerate(OUTER_TAPS):
            conv_ref[3 * row_tap + col_tap, lanes, :] = joined[half, at * LANES : (at + 1) * LANES, :]
        for n in range(expand_ref.shape[1] // channels):
            at = (len(OUTER_TAPS) + n) * LANES
            expand_ref[lanes, n * channels : (n + 1) * channels] = joined[half, at : at + LANES, :]


def assemble(where, groups, channels, deep):
    refs = [piece for group in groups for piece in group]
    return pl.pallas_call(
        assemble_kernel,
        out_shape=(
            jax.ShapeDtypeStruct((9, channels, channels), jnp.float32),
            jax.ShapeDtypeStruct((channels, deep), jnp.float32),
        ),
        in_specs=[scalars()] + [whole()] * len(refs),
        out_specs=(whole(), whole()),
        scratch_shapes=[pltpu.VMEM((2, 4 * groups[1][0].shape[0], channels), jnp.float32)],
        compiler_params=params(),
        cost_estimate=pl.CostEstimate(flops=0, bytes_accessed=7 * 10**6, transcendentals=0),
        name="assemble",
    )(where, *refs)


def body(stem_input, stem_preact, deep_cotangent, tissue_tiles, conv_weight, expand_weight):
    _, out_rows, out_cols, channels = stem_preact.shape
    _, all_rows, band, deep = deep_cotangent.shape
    devices = SIZES["x"] * SIZES["z"]
    preact = stem_preact[0]
    cotangent = deep_cotangent[0].reshape(all_rows * band, deep)
    share = tissue_tiles.astype(jnp.float32) / TILES
    core = lax.axis_index("core").astype(jnp.int32)
    where = jnp.stack([core, lax.axis_index("x")]).astype(jnp.int32)

    sent, weighted = build_sent(share, cotangent, expand_weight, preact, devices)
    blocks = prepare(stem_input[0])
    above = prepare(shifted(stem_input[0, -1:], 1))
    arrived = exchange(sent, SPACE)
    own_inner, other_inner, own_outer, other_outer, grad, first = terms(
        where[:1], arrived, preact, above, blocks, weighted
    )

    samples_all = stem_input.shape[0] * SIZES["y"] * SIZES["core"]
    scale = float(samples_all * all_rows * out_cols) ** (-0.5)
    inner = add(own_inner, swapped(other_inner, "core", 1))
    outer, *parts = combine(where, own_outer, swapped(other_outer, "core", 1))
    inner, outer, grad_input = total_sums(
        inner, outer, parts, scale, first, lambda b: input_grad(grad, b, conv_weight)
    )
    groups = [pieces + [swapped(piece, "core", 1) for piece in pieces] for pieces in (inner, outer)]
    grad_conv, grad_expand = assemble(where, groups, channels, deep)
    return (grad_input[None], grad_conv.reshape(3, 3, channels, channels), grad_expand)


def solution(mesh):
    fine = Mesh(
        mesh.devices.reshape(SIZES["x"], SIZES["z"], SIZES["y"], SIZES["core"]),
        ("x", "z", "y", "core"),
    )
    return jax.shard_map(
        body,
        mesh=fine,
        in_specs=(
            P(REP, SPACE, None, None),
            P(REP, SPACE, None, None),
            P(REP, None, SPACE, None),
            P(REP),
            P(),
            P(),
        ),
        out_specs=(P(REP, SPACE, None, None), P(), P()),
        check_vma=False,
    )
```

```python
import functools

import jax
import jax.numpy as jnp
from jax import lax
from jax.experimental import pallas as pl
from jax.experimental.pallas import tpu as pltpu
from jax.sharding import Mesh
from jax.sharding import PartitionSpec as P

TILES = 64
LANES = 128
INNER_TAPS = ((1, 0), (1, 1), (1, 2), (2, 0), (2, 1), (2, 2), (0, 0))
OUTER_TAPS = ((0, 1), (0, 2))
SIZES = {"x": 4, "z": 8, "y": 4, "core": 2}
SPACE = ("x", "z")
REP = ("y", "core")


def whole():
    return pl.BlockSpec(memory_space=pltpu.VMEM)


def far():
    return pl.BlockSpec(memory_space=pl.ANY)


def room(x):
    return pltpu.VMEM(x.shape, x.dtype)


def scalars():
    return pl.BlockSpec(memory_space=pltpu.SMEM)


def params(mib=24):
    return pltpu.CompilerParams(vmem_limit_bytes=mib * 1024 * 1024)


def shifted(x, by):
    length = SIZES["x"] * SIZES["z"]
    pairs = [(i, i + by) for i in range(length) if 0 <= i + by < length]
    return lax.ppermute(x, SPACE, pairs)


def send_kernel(
    share_ref, cotangent_hbm, weight_hbm, preact_hbm, sent_hbm, weighted_hbm,
    cotangent_ref, weight_ref, preact_ref, weighted_ref, sent_ref, sems,
):
    pairs = ((preact_hbm, preact_ref), (weight_hbm, weight_ref), (cotangent_hbm, cotangent_ref))
    copies = [pltpu.make_async_copy(a, b, sems.at[n]) for n, (a, b) in enumerate(pairs)]
    for copy in copies:
        copy.start()
    devices, chunk, channels = sent_ref.shape
    chunk = chunk // 2
    rows, cols = preact_ref.shape[:2]
    band = cols // devices
    copies[0].wait()
    for i in range(rows):
        active = jnp.maximum(preact_ref[i].astype(jnp.float32), 0.0).reshape(devices, band, channels)
        sent_ref[:, chunk + i * band : chunk + (i + 1) * band, :] = active.astype(jnp.bfloat16)
    copies[1].wait()
    copies[2].wait()
    weighted = (cotangent_ref[...].astype(jnp.float32) * share_ref[0]).astype(jnp.bfloat16)
    weighted_ref[...] = weighted
    back = pltpu.make_async_copy(weighted_ref, weighted_hbm, sems.at[3])
    back.start()
    hidden = lax.dot_general(
        weighted, weight_ref[...], (((1,), (1,)), ((), ())), preferred_element_type=jnp.float32
    )
    sent_ref[:, :chunk, :] = hidden.reshape(devices, chunk, channels).astype(jnp.bfloat16)
    out = pltpu.make_async_copy(sent_ref, sent_hbm, sems.at[4])
    out.start()
    back.wait()
    out.wait()


def build_sent(share, cotangent, weight, preact, devices):
    rows, cols, channels = preact.shape
    sent = jax.ShapeDtypeStruct((devices, 2 * rows * cols // devices, channels), jnp.bfloat16)
    return pl.pallas_call(
        send_kernel,
        out_shape=(
            sent,
            jax.ShapeDtypeStruct(cotangent.shape, jnp.bfloat16),
        ),
        in_specs=[scalars()] + [far()] * 3,
        out_specs=(far(), far()),
        scratch_shapes=[room(x) for x in (cotangent, weight, preact, cotangent, sent)]
        + [pltpu.SemaphoreType.DMA((5,))],
        compiler_params=params(60),
        cost_estimate=pl.CostEstimate(flops=268 * 10**6, bytes_accessed=4 * 10**6, transcendentals=0),
        name="build_sent",
    )(share, cotangent, weight, preact)


def prepare_kernel(x_ref, out_ref, wide):
    half = out_ref.shape[2]
    first = lax.broadcasted_iota(jnp.int32, (LANES, half), 1) == 0
    for row in range(x_ref.shape[0]):
        for part in range(x_ref.shape[2] // LANES):
            lanes = slice(part * LANES, (part + 1) * LANES)
            wide[...] = x_ref[row, :, lanes].astype(jnp.float32)
            even = wide[pl.ds(0, half, stride=2), :].T
            odd = wide[pl.ds(1, half, stride=2), :].T
            late = jnp.where(first, 0.0, pltpu.roll(odd, 1, 1))
            out_ref[3 * row, lanes, :] = late.astype(jnp.bfloat16)
            out_ref[3 * row + 1, lanes, :] = even.astype(jnp.bfloat16)
            out_ref[3 * row + 2, lanes, :] = odd.astype(jnp.bfloat16)


def prepare(x):
    rows, cols, channels = x.shape
    return pl.pallas_call(
        prepare_kernel,
        out_shape=jax.ShapeDtypeStruct((3 * rows, channels, cols // 2), jnp.bfloat16),
        in_specs=[whole()],
        out_specs=whole(),
        scratch_shapes=[pltpu.VMEM((cols, LANES), jnp.float32)],
        compiler_params=params(),
        cost_estimate=pl.CostEstimate(flops=10**7, bytes_accessed=3 * 10**6, transcendentals=0),
        name="prepare",
    )(x)


def terms_kernel(
    core_ref, arrived_hbm, preact_hbm, above_hbm, blocks_hbm, weighted_hbm,
    own_inner, other_inner, own_outer, other_outer, grad_hbm, first_hbm,
    arrived_ref, preact_ref, above_ref, blocks_ref, weighted_ref,
    grad_ref, turned, inner_ref, outer_ref, sems,
):
    pairs = (
        (arrived_hbm, arrived_ref),
        (preact_hbm, preact_ref),
        (blocks_hbm, blocks_ref),
        (above_hbm, above_ref),
        (weighted_hbm, weighted_ref),
    )
    copies = [pltpu.make_async_copy(a, b, sems.at[n]) for n, (a, b) in enumerate(pairs)]
    for copy in copies:
        copy.start()
    devices, chunk, channels = arrived_ref.shape
    rows, cols = preact_ref.shape[:2]
    chunk, band = chunk // 2, cols // devices
    copies[0].wait()
    copies[1].wait()
    for i in range(rows):
        hidden = arrived_ref[:, i * band : (i + 1) * band, :].astype(jnp.float32).reshape(cols, channels)
        kept = jnp.where(preact_ref[i].astype(jnp.float32) > 0.0, hidden, 0.0)
        grad_ref[i] = kept.astype(jnp.bfloat16)
    back = [
        pltpu.make_async_copy(grad_ref, grad_hbm, sems.at[5]),
        pltpu.make_async_copy(grad_ref.at[0:1], first_hbm, sems.at[10]),
    ]
    active = arrived_ref[:, chunk:, :].astype(jnp.float32).reshape(devices * chunk, channels)
    turned[...] = active.T.astype(jnp.bfloat16)

    def half_taps(row_tap, col_tap, start):
        total = None
        for i in range(rows):
            row = 2 * i + row_tap - 1
            source, at = (above_ref, col_tap) if row < 0 else (blocks_ref, 3 * row + col_tap)
            term = jnp.dot(
                source[at, pl.ds(start, LANES), :], grad_ref[i], preferred_element_type=jnp.float32
            )
            total = term if total is None else total + term
        return total

    for copy in copies[2:]:
        copy.wait()
    back[0].start()
    back[1].start()
    for n, (inner_hbm, outer_hbm) in enumerate(((other_inner, other_outer), (own_inner, own_outer))):
        owner = core_ref[0] if n else 1 - core_ref[0]
        start = pl.multiple_of(owner * LANES, LANES)
        for at, (row_tap, col_tap) in enumerate(INNER_TAPS):
            inner_ref[n, at * LANES : (at + 1) * LANES, :] = half_taps(row_tap, col_tap, start)
        back.append(pltpu.make_async_copy(inner_ref.at[n], inner_hbm, sems.at[6 + 2 * n]))
        back[-1].start()
        for at, (row_tap, col_tap) in enumerate(OUTER_TAPS):
            outer_ref[n, at * LANES : (at + 1) * LANES, :] = half_taps(row_tap, col_tap, start)
        for k in range(weighted_ref.shape[1] // channels):
            at = (len(OUTER_TAPS) + k) * LANES
            outer_ref[n, at : at + LANES, :] = jnp.dot(
                turned[pl.ds(start, LANES), :],
                weighted_ref[:, k * channels : (k + 1) * channels],
                preferred_element_type=jnp.float32,
            )
        back.append(pltpu.make_async_copy(outer_ref.at[n], outer_hbm, sems.at[7 + 2 * n]))
        back[-1].start()
    for copy in back:
        copy.wait()


def terms(core, arrived, preact, above, blocks, weighted):
    rows, cols, channels = preact.shape
    inner = jax.ShapeDtypeStruct((len(INNER_TAPS) * LANES, channels), jnp.float32)
    outer = jax.ShapeDtypeStruct((len(OUTER_TAPS) * LANES + weighted.shape[1] // 2, channels), jnp.float32)
    return pl.pallas_call(
        terms_kernel,
        out_shape=(
            inner,
            inner,
            outer,
            outer,
            jax.ShapeDtypeStruct(preact.shape, jnp.bfloat16),
            jax.ShapeDtypeStruct((1, cols, channels), jnp.bfloat16),
        ),
        in_specs=[scalars()] + [far()] * 5,
        out_specs=(far(),) * 6,
        scratch_shapes=[room(x) for x in (arrived, preact, above, blocks, weighted, preact)]
        + [
            pltpu.VMEM((channels, weighted.shape[0]), jnp.bfloat16),
            pltpu.VMEM((2,) + inner.shape, jnp.float32),
            pltpu.VMEM((2,) + outer.shape, jnp.float32),
            pltpu.SemaphoreType.DMA((11,)),
        ],
        compiler_params=params(50),
        cost_estimate=pl.CostEstimate(flops=870 * 10**6, bytes_accessed=8 * 10**6, transcendentals=0),
        name="terms",
    )(core, arrived, preact, above, blocks, weighted)


def add_kernel(own, got, out_ref):
    out_ref[...] = own[...] + got[...]


def add(own, got):
    return pl.pallas_call(
        add_kernel,
        out_shape=jax.ShapeDtypeStruct(own.shape, own.dtype),
        in_specs=[whole()] * 2,
        out_specs=whole(),
        compiler_params=params(24),
        cost_estimate=pl.CostEstimate(flops=10**5, bytes_accessed=2 * 10**6, transcendentals=0),
        name="add",
    )(own, got)


def combine_kernel(where_ref, own, got, *out_refs):
    rows = out_refs[0].shape[0]
    for by, out_ref in enumerate(out_refs):
        at = pl.ds(pl.multiple_of(((where_ref[1] + by) & 3) * rows, 8), rows)
        out_ref[...] = own[at, :] + got[at, :]


def combine(where, own, got):
    chunk = jax.ShapeDtypeStruct((own.shape[0] // 4, own.shape[1]), jnp.float32)
    return pl.pallas_call(
        combine_kernel,
        out_shape=(chunk,) * 4,
        in_specs=[scalars()] + [whole()] * 2,
        out_specs=(whole(),) * 4,
        compiler_params=params(24),
        cost_estimate=pl.CostEstimate(flops=10**6, bytes_accessed=3 * 10**6, transcendentals=0),
        name="combine",
    )(where, own, got)


def input_kernel(grad_ref, below_ref, weight_ref, out_ref, wide):
    half = grad_ref.shape[1]
    last = lax.broadcasted_iota(jnp.int32, grad_ref.shape[1:], 0) == half - 1

    def early(g):
        moved = pltpu.roll(g.astype(jnp.float32), half - 1, 0)
        return jnp.where(last, 0.0, moved).astype(jnp.bfloat16)

    grads = [grad_ref[0], grad_ref[1], below_ref[0]]
    moved = [early(g) for g in grads]

    def times(g, row_tap, col_tap):
        return lax.dot_general(
            g,
            weight_ref[row_tap, col_tap],
            (((1,), (1,)), ((), ())),
            preferred_element_type=jnp.float32,
        )

    for row in range(4):
        i = row // 2
        terms = [(i, 1)] if row % 2 == 0 else [(i, 2), (i + 1, 0)]
        even = sum(times(grads[n], p, 1) for n, p in terms)
        odd = sum(times(grads[n], p, 2) + times(moved[n], p, 0) for n, p in terms)
        for part in range(even.shape[1] // LANES):
            lanes = slice(part * LANES, (part + 1) * LANES)
            wide[pl.ds(0, half, stride=2), :] = even[:, lanes]
            wide[pl.ds(1, half, stride=2), :] = odd[:, lanes]
            out_ref[row, :, lanes] = wide[...].astype(jnp.bfloat16)


def input_grad(grad, below, weight):
    rows, half, channels = grad.shape
    return pl.pallas_call(
        input_kernel,
        out_shape=jax.ShapeDtypeStruct((2 * rows, 2 * half, weight.shape[2]), jnp.bfloat16),
        in_specs=[whole()] * 3,
        out_specs=whole(),
        scratch_shapes=[pltpu.VMEM((2 * half, LANES), jnp.float32)],
        compiler_params=params(),
        cost_estimate=pl.CostEstimate(flops=604 * 10**6, bytes_accessed=3 * 10**6, transcendentals=0),
        name="input_grad",
    )(grad, below, weight)


def exchange(x, axis):
    return lax.all_to_all(x, axis, split_axis=0, concat_axis=0, tiled=True)


def place(axis, by=0):
    return (lax.axis_index(axis).astype(jnp.uint32) + jnp.uint32(by % SIZES[axis])) & jnp.uint32(SIZES[axis] - 1)


def pick(parts, index):
    zero = jnp.uint32(0)
    return lax.dynamic_slice(parts, (index, zero, zero), (1,) + parts.shape[1:])[0]


def put(parts, piece, index):
    zero = jnp.uint32(0)
    return lax.dynamic_update_slice(parts, piece[None], (index, zero, zero))


def rotated(x, axis, by):
    size = SIZES[axis]
    return lax.ppermute(x, axis, [(i, (i + by) % size) for i in range(size)])


def split(x):
    return x.reshape(4, x.shape[0] // 4, x.shape[1])


def swapped(x, axis, bit):
    return lax.ppermute(x, axis, [(i, i ^ bit) for i in range(SIZES[axis])])


def turned(x, by):
    pairs = []
    for i in range(SIZES["x"]):
        for k in range(SIZES["z"]):
            for j in range(SIZES["y"]):
                to = (i, (j + by) % 4) if k % 2 else ((i + by) % 4, j)
                pairs.append(((i * SIZES["z"] + k) * 4 + j, (to[0] * SIZES["z"] + k) * 4 + to[1]))
    return lax.ppermute(x, ("x", "z", "y"), pairs)


def turned_place(by=0):
    odd = (place("z") & jnp.uint32(1)) == 1
    return jnp.where(odd, place("y", by), place("x", by))


barrier = lax.optimization_barrier
STEPS = (1, 2, 3)


def total_sums(inner, outer, parts, scale, first, beside):
    inner, parts = exchange(split(inner), "y"), barrier(parts)
    moved = [rotated(p, "x", by) for p, by in zip(parts, STEPS)]
    inner, moved = barrier((inner, moved))
    inner = jnp.sum(inner, axis=0)
    outer = sum(moved, outer)

    rows = inner.shape[0] - outer.shape[0]
    both = jnp.stack([inner, jnp.pad(outer, ((0, rows), (0, 0)))])
    bit = place("z") & jnp.uint32(1)
    part = pick(both, bit) + swapped(pick(both, jnp.uint32(1) - bit), "z", 1)

    parts = split(part)
    moved, first = barrier(([pick(parts, turned_place(by)) for by in STEPS], first))
    moved = [turned(p, by) for p, by in zip(moved, STEPS)]
    below = shifted(first, -1)
    part = sum(moved, pick(parts, turned_place()))

    moved = [rotated(part, "z", by) for by in (2, 4, 6)]
    (two, four, six), beside = barrier((moved, beside(below)))
    part = ((part + four) + (two + six)) * scale

    whole_part = jnp.zeros((4,) + part.shape, part.dtype)
    for by in range(4):
        whole_part = put(whole_part, turned(part, by) if by else part, turned_place(-by))
    part = whole_part.reshape(-1, part.shape[1])
    got = swapped(part, "z", 1)
    inner = jnp.where(bit == 0, part, got)
    outer = jnp.where(bit == 0, got, part)[: part.shape[0] - rows]
    copies = barrier(jnp.broadcast_to(inner, (4,) + inner.shape))
    copies, moved = barrier((exchange(copies, "y"), [rotated(outer, "x", by) for by in STEPS]))
    return [copies.reshape(-1, part.shape[1])], [outer] + moved, beside


def assemble_kernel(where_ref, *refs):
    inner, pieces, (conv_ref, expand_ref, joined) = refs[:2], refs[2:10], refs[10:]
    channels = conv_ref.shape[2]
    core = where_ref[0]
    for by in range(4):
        rows = pieces[by].shape[0]
        at = pl.multiple_of(((where_ref[1] + 4 - by) & 3) * rows, 8)
        joined[core, pl.ds(at, rows), :] = pieces[by][...]
        joined[1 - core, pl.ds(at, rows), :] = pieces[4 + by][...]
    for at, (row_tap, col_tap) in enumerate(INNER_TAPS):
        rows, tap = slice(at * LANES, (at + 1) * LANES), 3 * row_tap + col_tap
        conv_ref[tap, pl.ds(pl.multiple_of(core * LANES, LANES), LANES), :] = inner[0][rows, :]
        conv_ref[tap, pl.ds(pl.multiple_of((1 - core) * LANES, LANES), LANES), :] = inner[1][rows, :]
    for half in range(2):
        lanes = slice(half * LANES, (half + 1) * LANES)
        for at, (row_tap, col_tap) in enumerate(OUTER_TAPS):
            conv_ref[3 * row_tap + col_tap, lanes, :] = joined[half, at * LANES : (at + 1) * LANES, :]
        for n in range(expand_ref.shape[1] // channels):
            at = (len(OUTER_TAPS) + n) * LANES
            expand_ref[lanes, n * channels : (n + 1) * channels] = joined[half, at : at + LANES, :]


def assemble(where, groups, channels, deep):
    refs = [piece for group in groups for piece in group]
    return pl.pallas_call(
        assemble_kernel,
        out_shape=(
            jax.ShapeDtypeStruct((9, channels, channels), jnp.float32),
            jax.ShapeDtypeStruct((channels, deep), jnp.float32),
        ),
        in_specs=[scalars()] + [whole()] * len(refs),
        out_specs=(whole(), whole()),
        scratch_shapes=[pltpu.VMEM((2, 4 * groups[1][0].shape[0], channels), jnp.float32)],
        compiler_params=params(),
        cost_estimate=pl.CostEstimate(flops=0, bytes_accessed=7 * 10**6, transcendentals=0),
        name="assemble",
    )(where, *refs)


def body(stem_input, stem_preact, deep_cotangent, tissue_tiles, conv_weight, expand_weight):
    _, out_rows, out_cols, channels = stem_preact.shape
    _, all_rows, band, deep = deep_cotangent.shape
    devices = SIZES["x"] * SIZES["z"]
    preact = stem_preact[0]
    cotangent = deep_cotangent[0].reshape(all_rows * band, deep)
    share = tissue_tiles.astype(jnp.float32) / TILES
    core = lax.axis_index("core").astype(jnp.int32)
    where = jnp.stack([core, lax.axis_index("x")]).astype(jnp.int32)

    sent, weighted = build_sent(share, cotangent, expand_weight, preact, devices)
    blocks = prepare(stem_input[0])
    above = prepare(shifted(stem_input[0, -1:], 1))
    arrived = exchange(sent, SPACE)
    own_inner, other_inner, own_outer, other_outer, grad, first = terms(
        where[:1], arrived, preact, above, blocks, weighted
    )

    samples_all = stem_input.shape[0] * SIZES["y"] * SIZES["core"]
    scale = float(samples_all * all_rows * out_cols) ** (-0.5)
    inner = add(own_inner, swapped(other_inner, "core", 1))
    outer, *parts = combine(where, own_outer, swapped(other_outer, "core", 1))
    inner, outer, grad_input = total_sums(
        inner, outer, parts, scale, first, lambda b: input_grad(grad, b, conv_weight)
    )
    groups = [pieces + [swapped(piece, "core", 1) for piece in pieces] for pieces in (inner, outer)]
    grad_conv, grad_expand = assemble(where, groups, channels, deep)
    return (grad_input[None], grad_conv.reshape(3, 3, channels, channels), grad_expand)


def solution(mesh):
    fine = Mesh(
        mesh.devices.reshape(SIZES["x"], SIZES["z"], SIZES["y"], SIZES["core"]),
        ("x", "z", "y", "core"),
    )
    return jax.shard_map(
        body,
        mesh=fine,
        in_specs=(
            P(REP, SPACE, None, None),
            P(REP, SPACE, None, None),
            P(REP, None, SPACE, None),
            P(REP),
            P(),
            P(),
        ),
        out_specs=(P(REP, SPACE, None, None), P(), P()),
        check_vma=False,
    )
```

```python
import functools

import jax
import jax.numpy as jnp
from jax import lax
from jax.experimental import pallas as pl
from jax.experimental.pallas import tpu as pltpu
from jax.sharding import Mesh
from jax.sharding import PartitionSpec as P

TILES = 64
LANES = 128
INNER_TAPS = ((1, 0), (1, 1), (1, 2), (2, 0), (2, 1), (2, 2), (0, 0))
OUTER_TAPS = ((0, 1), (0, 2))
SIZES = {"x": 4, "z": 8, "y": 4, "core": 2}
SPACE = ("x", "z")
REP = ("y", "core")


def whole():
    return pl.BlockSpec(memory_space=pltpu.VMEM)


def far():
    return pl.BlockSpec(memory_space=pl.ANY)


def room(x):
    return pltpu.VMEM(x.shape, x.dtype)


def scalars():
    return pl.BlockSpec(memory_space=pltpu.SMEM)


def params(mib=24):
    return pltpu.CompilerParams(vmem_limit_bytes=mib * 1024 * 1024)


def shifted(x, by):
    length = SIZES["x"] * SIZES["z"]
    pairs = [(i, i + by) for i in range(length) if 0 <= i + by < length]
    return lax.ppermute(x, SPACE, pairs)


def send_kernel(
    share_ref, cotangent_hbm, weight_hbm, preact_hbm, sent_hbm, weighted_hbm,
    cotangent_ref, weight_ref, preact_ref, weighted_ref, sent_ref, sems,
):
    pairs = ((preact_hbm, preact_ref), (weight_hbm, weight_ref), (cotangent_hbm, cotangent_ref))
    copies = [pltpu.make_async_copy(a, b, sems.at[n]) for n, (a, b) in enumerate(pairs)]
    for copy in copies:
        copy.start()
    devices, chunk, channels = sent_ref.shape
    chunk = chunk // 2
    rows, cols = preact_ref.shape[:2]
    band = cols // devices
    copies[0].wait()
    for i in range(rows):
        active = jnp.maximum(preact_ref[i].astype(jnp.float32), 0.0).reshape(devices, band, channels)
        sent_ref[:, chunk + i * band : chunk + (i + 1) * band, :] = active.astype(jnp.bfloat16)
    copies[1].wait()
    copies[2].wait()
    weighted = (cotangent_ref[...].astype(jnp.float32) * share_ref[0]).astype(jnp.bfloat16)
    weighted_ref[...] = weighted
    back = pltpu.make_async_copy(weighted_ref, weighted_hbm, sems.at[3])
    back.start()
    hidden = lax.dot_general(
        weighted, weight_ref[...], (((1,), (1,)), ((), ())), preferred_element_type=jnp.float32
    )
    sent_ref[:, :chunk, :] = hidden.reshape(devices, chunk, channels).astype(jnp.bfloat16)
    out = pltpu.make_async_copy(sent_ref, sent_hbm, sems.at[4])
    out.start()
    back.wait()
    out.wait()


def build_sent(share, cotangent, weight, preact, devices):
    rows, cols, channels = preact.shape
    sent = jax.ShapeDtypeStruct((devices, 2 * rows * cols // devices, channels), jnp.bfloat16)
    return pl.pallas_call(
        send_kernel,
        out_shape=(
            sent,
            jax.ShapeDtypeStruct(cotangent.shape, jnp.bfloat16),
        ),
        in_specs=[scalars()] + [far()] * 3,
        out_specs=(far(), far()),
        scratch_shapes=[room(x) for x in (cotangent, weight, preact, cotangent, sent)]
        + [pltpu.SemaphoreType.DMA((5,))],
        compiler_params=params(60),
        cost_estimate=pl.CostEstimate(flops=268 * 10**6, bytes_accessed=4 * 10**6, transcendentals=0),
        name="build_sent",
    )(share, cotangent, weight, preact)


def prepare_kernel(x_ref, out_ref, wide):
    half = out_ref.shape[2]
    first = lax.broadcasted_iota(jnp.int32, (LANES, half), 1) == 0
    for row in range(x_ref.shape[0]):
        for part in range(x_ref.shape[2] // LANES):
            lanes = slice(part * LANES, (part + 1) * LANES)
            wide[...] = x_ref[row, :, lanes].astype(jnp.float32)
            even = wide[pl.ds(0, half, stride=2), :].T
            odd = wide[pl.ds(1, half, stride=2), :].T
            late = jnp.where(first, 0.0, pltpu.roll(odd, 1, 1))
            out_ref[3 * row, lanes, :] = late.astype(jnp.bfloat16)
            out_ref[3 * row + 1, lanes, :] = even.astype(jnp.bfloat16)
            out_ref[3 * row + 2, lanes, :] = odd.astype(jnp.bfloat16)


def prepare(x):
    rows, cols, channels = x.shape
    return pl.pallas_call(
        prepare_kernel,
        out_shape=jax.ShapeDtypeStruct((3 * rows, channels, cols // 2), jnp.bfloat16),
        in_specs=[whole()],
        out_specs=whole(),
        scratch_shapes=[pltpu.VMEM((cols, LANES), jnp.float32)],
        compiler_params=params(),
        cost_estimate=pl.CostEstimate(flops=10**7, bytes_accessed=3 * 10**6, transcendentals=0),
        name="prepare",
    )(x)


def terms_kernel(
    core_ref, arrived_hbm, preact_hbm, above_hbm, blocks_hbm, weighted_hbm,
    own_inner, other_inner, own_outer, other_outer, grad_hbm, first_hbm,
    arrived_ref, preact_ref, above_ref, blocks_ref, weighted_ref,
    grad_ref, turned, inner_ref, outer_ref, sems,
):
    pairs = (
        (arrived_hbm, arrived_ref),
        (preact_hbm, preact_ref),
        (blocks_hbm, blocks_ref),
        (above_hbm, above_ref),
        (weighted_hbm, weighted_ref),
    )
    copies = [pltpu.make_async_copy(a, b, sems.at[n]) for n, (a, b) in enumerate(pairs)]
    for copy in copies:
        copy.start()
    devices, chunk, channels = arrived_ref.shape
    rows, cols = preact_ref.shape[:2]
    chunk, band = chunk // 2, cols // devices
    copies[0].wait()
    copies[1].wait()
    for i in range(rows):
        hidden = arrived_ref[:, i * band : (i + 1) * band, :].astype(jnp.float32).reshape(cols, channels)
        kept = jnp.where(preact_ref[i].astype(jnp.float32) > 0.0, hidden, 0.0)
        grad_ref[i] = kept.astype(jnp.bfloat16)
    back = [
        pltpu.make_async_copy(grad_ref, grad_hbm, sems.at[5]),
        pltpu.make_async_copy(grad_ref.at[0:1], first_hbm, sems.at[10]),
    ]
    active = arrived_ref[:, chunk:, :].astype(jnp.float32).reshape(devices * chunk, channels)
    turned[...] = active.T.astype(jnp.bfloat16)

    def half_taps(row_tap, col_tap, start):
        total = None
        for i in range(rows):
            row = 2 * i + row_tap - 1
            source, at = (above_ref, col_tap) if row < 0 else (blocks_ref, 3 * row + col_tap)
            term = jnp.dot(
                source[at, pl.ds(start, LANES), :], grad_ref[i], preferred_element_type=jnp.float32
            )
            total = term if total is None else total + term
        return total

    for copy in copies[2:]:
        copy.wait()
    back[0].start()
    back[1].start()
    for n, (inner_hbm, outer_hbm) in enumerate(((other_inner, other_outer), (own_inner, own_outer))):
        owner = core_ref[0] if n else 1 - core_ref[0]
        start = pl.multiple_of(owner * LANES, LANES)
        for at, (row_tap, col_tap) in enumerate(INNER_TAPS):
            inner_ref[n, at * LANES : (at + 1) * LANES, :] = half_taps(row_tap, col_tap, start)
        back.append(pltpu.make_async_copy(inner_ref.at[n], inner_hbm, sems.at[6 + 2 * n]))
        back[-1].start()
        for at, (row_tap, col_tap) in enumerate(OUTER_TAPS):
            outer_ref[n, at * LANES : (at + 1) * LANES, :] = half_taps(row_tap, col_tap, start)
        for k in range(weighted_ref.shape[1] // channels):
            at = (len(OUTER_TAPS) + k) * LANES
            outer_ref[n, at : at + LANES, :] = jnp.dot(
                turned[pl.ds(start, LANES), :],
                weighted_ref[:, k * channels : (k + 1) * channels],
                preferred_element_type=jnp.float32,
            )
        back.append(pltpu.make_async_copy(outer_ref.at[n], outer_hbm, sems.at[7 + 2 * n]))
        back[-1].start()
    for copy in back:
        copy.wait()


def terms(core, arrived, preact, above, blocks, weighted):
    rows, cols, channels = preact.shape
    inner = jax.ShapeDtypeStruct((len(INNER_TAPS) * LANES, channels), jnp.float32)
    outer = jax.ShapeDtypeStruct((len(OUTER_TAPS) * LANES + weighted.shape[1] // 2, channels), jnp.float32)
    return pl.pallas_call(
        terms_kernel,
        out_shape=(
            inner,
            inner,
            outer,
            outer,
            jax.ShapeDtypeStruct(preact.shape, jnp.bfloat16),
            jax.ShapeDtypeStruct((1, cols, channels), jnp.bfloat16),
        ),
        in_specs=[scalars()] + [far()] * 5,
        out_specs=(far(),) * 6,
        scratch_shapes=[room(x) for x in (arrived, preact, above, blocks, weighted, preact)]
        + [
            pltpu.VMEM((channels, weighted.shape[0]), jnp.bfloat16),
            pltpu.VMEM((2,) + inner.shape, jnp.float32),
            pltpu.VMEM((2,) + outer.shape, jnp.float32),
            pltpu.SemaphoreType.DMA((11,)),
        ],
        compiler_params=params(50),
        cost_estimate=pl.CostEstimate(flops=870 * 10**6, bytes_accessed=8 * 10**6, transcendentals=0),
        name="terms",
    )(core, arrived, preact, above, blocks, weighted)


def add_kernel(own, got, out_ref):
    out_ref[...] = own[...] + got[...]


def add(own, got):
    return pl.pallas_call(
        add_kernel,
        out_shape=jax.ShapeDtypeStruct(own.shape, own.dtype),
        in_specs=[whole()] * 2,
        out_specs=whole(),
        compiler_params=params(24),
        cost_estimate=pl.CostEstimate(flops=10**5, bytes_accessed=2 * 10**6, transcendentals=0),
        name="add",
    )(own, got)


def combine_kernel(where_ref, own, got, *out_refs):
    rows = out_refs[0].shape[0]
    for by, out_ref in enumerate(out_refs):
        at = pl.ds(pl.multiple_of(((where_ref[1] + by) & 3) * rows, 8), rows)
        out_ref[...] = own[at, :] + got[at, :]


def combine(where, own, got):
    chunk = jax.ShapeDtypeStruct((own.shape[0] // 4, own.shape[1]), jnp.float32)
    return pl.pallas_call(
        combine_kernel,
        out_shape=(chunk,) * 4,
        in_specs=[scalars()] + [whole()] * 2,
        out_specs=(whole(),) * 4,
        compiler_params=params(24),
        cost_estimate=pl.CostEstimate(flops=10**6, bytes_accessed=3 * 10**6, transcendentals=0),
        name="combine",
    )(where, own, got)


def input_kernel(grad_ref, below_ref, weight_ref, out_ref, wide):
    half = grad_ref.shape[1]
    last = lax.broadcasted_iota(jnp.int32, grad_ref.shape[1:], 0) == half - 1

    def early(g):
        moved = pltpu.roll(g.astype(jnp.float32), half - 1, 0)
        return jnp.where(last, 0.0, moved).astype(jnp.bfloat16)

    grads = [grad_ref[0], grad_ref[1], below_ref[0]]
    moved = [early(g) for g in grads]

    def times(g, row_tap, col_tap):
        return lax.dot_general(
            g,
            weight_ref[row_tap, col_tap],
            (((1,), (1,)), ((), ())),
            preferred_element_type=jnp.float32,
        )

    for row in range(4):
        i = row // 2
        terms = [(i, 1)] if row % 2 == 0 else [(i, 2), (i + 1, 0)]
        even = sum(times(grads[n], p, 1) for n, p in terms)
        odd = sum(times(grads[n], p, 2) + times(moved[n], p, 0) for n, p in terms)
        for part in range(even.shape[1] // LANES):
            lanes = slice(part * LANES, (part + 1) * LANES)
            wide[pl.ds(0, half, stride=2), :] = even[:, lanes]
            wide[pl.ds(1, half, stride=2), :] = odd[:, lanes]
            out_ref[row, :, lanes] = wide[...].astype(jnp.bfloat16)


def input_grad(grad, below, weight):
    rows, half, channels = grad.shape
    return pl.pallas_call(
        input_kernel,
        out_shape=jax.ShapeDtypeStruct((2 * rows, 2 * half, weight.shape[2]), jnp.bfloat16),
        in_specs=[whole()] * 3,
        out_specs=whole(),
        scratch_shapes=[pltpu.VMEM((2 * half, LANES), jnp.float32)],
        compiler_params=params(),
        cost_estimate=pl.CostEstimate(flops=604 * 10**6, bytes_accessed=3 * 10**6, transcendentals=0),
        name="input_grad",
    )(grad, below, weight)


def exchange(x, axis):
    return lax.all_to_all(x, axis, split_axis=0, concat_axis=0, tiled=True)


def place(axis, by=0):
    return (lax.axis_index(axis).astype(jnp.uint32) + jnp.uint32(by % SIZES[axis])) & jnp.uint32(SIZES[axis] - 1)


def pick(parts, index):
    zero = jnp.uint32(0)
    return lax.dynamic_slice(parts, (index, zero, zero), (1,) + parts.shape[1:])[0]


def put(parts, piece, index):
    zero = jnp.uint32(0)
    return lax.dynamic_update_slice(parts, piece[None], (index, zero, zero))


def rotated(x, axis, by):
    size = SIZES[axis]
    return lax.ppermute(x, axis, [(i, (i + by) % size) for i in range(size)])


def split(x):
    return x.reshape(4, x.shape[0] // 4, x.shape[1])


def swapped(x, axis, bit):
    return lax.ppermute(x, axis, [(i, i ^ bit) for i in range(SIZES[axis])])


def turned(x, by):
    pairs = []
    for i in range(SIZES["x"]):
        for k in range(SIZES["z"]):
            for j in range(SIZES["y"]):
                to = (i, (j + by) % 4) if k % 2 else ((i + by) % 4, j)
                pairs.append(((i * SIZES["z"] + k) * 4 + j, (to[0] * SIZES["z"] + k) * 4 + to[1]))
    return lax.ppermute(x, ("x", "z", "y"), pairs)


def turned_place(by=0):
    odd = (place("z") & jnp.uint32(1)) == 1
    return jnp.where(odd, place("y", by), place("x", by))


barrier = lax.optimization_barrier
STEPS = (2, 1, 3)


def total_sums(inner, outer, parts, scale, first, beside):
    inner, parts = exchange(split(inner), "y"), barrier(parts)
    moved = [rotated(parts[by - 1], "x", by) for by in STEPS]
    inner, moved = barrier((inner, moved))
    inner = jnp.sum(inner, axis=0)
    outer = sum(moved, outer)

    rows = inner.shape[0] - outer.shape[0]
    both = jnp.stack([inner, jnp.pad(outer, ((0, rows), (0, 0)))])
    bit = place("z") & jnp.uint32(1)
    part = pick(both, bit) + swapped(pick(both, jnp.uint32(1) - bit), "z", 1)

    parts = split(part)
    moved, first = barrier(([pick(parts, turned_place(by)) for by in STEPS], first))
    moved = [turned(p, by) for p, by in zip(moved, STEPS)]
    below = shifted(first, -1)
    part = sum(moved, pick(parts, turned_place()))

    moved = [rotated(part, "z", by) for by in (2, 4, 6)]
    (two, four, six), beside = barrier((moved, beside(below)))
    part = ((part + four) + (two + six)) * scale

    whole_part = jnp.zeros((4,) + part.shape, part.dtype)
    for by in range(4):
        whole_part = put(whole_part, turned(part, by) if by else part, turned_place(-by))
    part = whole_part.reshape(-1, part.shape[1])
    got = swapped(part, "z", 1)
    inner = jnp.where(bit == 0, part, got)
    outer = jnp.where(bit == 0, got, part)[: part.shape[0] - rows]
    copies = barrier(jnp.broadcast_to(inner, (4,) + inner.shape))
    copies, moved = barrier((exchange(copies, "y"), {by: rotated(outer, "x", by) for by in STEPS}))
    return [copies.reshape(-1, part.shape[1])], [outer] + [moved[by] for by in sorted(STEPS)], beside


def assemble_kernel(where_ref, *refs):
    inner, pieces, (conv_ref, expand_ref, joined) = refs[:2], refs[2:10], refs[10:]
    channels = conv_ref.shape[2]
    core = where_ref[0]
    for by in range(4):
        rows = pieces[by].shape[0]
        at = pl.multiple_of(((where_ref[1] + 4 - by) & 3) * rows, 8)
        joined[core, pl.ds(at, rows), :] = pieces[by][...]
        joined[1 - core, pl.ds(at, rows), :] = pieces[4 + by][...]
    for at, (row_tap, col_tap) in enumerate(INNER_TAPS):
        rows, tap = slice(at * LANES, (at + 1) * LANES), 3 * row_tap + col_tap
        conv_ref[tap, pl.ds(pl.multiple_of(core * LANES, LANES), LANES), :] = inner[0][rows, :]
        conv_ref[tap, pl.ds(pl.multiple_of((1 - core) * LANES, LANES), LANES), :] = inner[1][rows, :]
    for half in range(2):
        lanes = slice(half * LANES, (half + 1) * LANES)
        for at, (row_tap, col_tap) in enumerate(OUTER_TAPS):
            conv_ref[3 * row_tap + col_tap, lanes, :] = joined[half, at * LANES : (at + 1) * LANES, :]
        for n in range(expand_ref.shape[1] // channels):
            at = (len(OUTER_TAPS) + n) * LANES
            expand_ref[lanes, n * channels : (n + 1) * channels] = joined[half, at : at + LANES, :]


def assemble(where, groups, channels, deep):
    refs = [piece for group in groups for piece in group]
    return pl.pallas_call(
        assemble_kernel,
        out_shape=(
            jax.ShapeDtypeStruct((9, channels, channels), jnp.float32),
            jax.ShapeDtypeStruct((channels, deep), jnp.float32),
        ),
        in_specs=[scalars()] + [whole()] * len(refs),
        out_specs=(whole(), whole()),
        scratch_shapes=[pltpu.VMEM((2, 4 * groups[1][0].shape[0], channels), jnp.float32)],
        compiler_params=params(),
        cost_estimate=pl.CostEstimate(flops=0, bytes_accessed=7 * 10**6, transcendentals=0),
        name="assemble",
    )(where, *refs)


def body(stem_input, stem_preact, deep_cotangent, tissue_tiles, conv_weight, expand_weight):
    _, out_rows, out_cols, channels = stem_preact.shape
    _, all_rows, band, deep = deep_cotangent.shape
    devices = SIZES["x"] * SIZES["z"]
    preact = stem_preact[0]
    cotangent = deep_cotangent[0].reshape(all_rows * band, deep)
    share = tissue_tiles.astype(jnp.float32) / TILES
    core = lax.axis_index("core").astype(jnp.int32)
    where = jnp.stack([core, lax.axis_index("x")]).astype(jnp.int32)

    sent, weighted = build_sent(share, cotangent, expand_weight, preact, devices)
    blocks = prepare(stem_input[0])
    above = prepare(shifted(stem_input[0, -1:], 1))
    arrived = exchange(sent, SPACE)
    own_inner, other_inner, own_outer, other_outer, grad, first = terms(
        where[:1], arrived, preact, above, blocks, weighted
    )

    samples_all = stem_input.shape[0] * SIZES["y"] * SIZES["core"]
    scale = float(samples_all * all_rows * out_cols) ** (-0.5)
    inner = add(own_inner, swapped(other_inner, "core", 1))
    outer, *parts = combine(where, own_outer, swapped(other_outer, "core", 1))
    inner, outer, grad_input = total_sums(
        inner, outer, parts, scale, first, lambda b: input_grad(grad, b, conv_weight)
    )
    groups = [pieces + [swapped(piece, "core", 1) for piece in pieces] for pieces in (inner, outer)]
    grad_conv, grad_expand = assemble(where, groups, channels, deep)
    return (grad_input[None], grad_conv.reshape(3, 3, channels, channels), grad_expand)


def solution(mesh):
    fine = Mesh(
        mesh.devices.reshape(SIZES["x"], SIZES["z"], SIZES["y"], SIZES["core"]),
        ("x", "z", "y", "core"),
    )
    return jax.shard_map(
        body,
        mesh=fine,
        in_specs=(
            P(REP, SPACE, None, None),
            P(REP, SPACE, None, None),
            P(REP, None, SPACE, None),
            P(REP),
            P(),
            P(),
        ),
        out_specs=(P(REP, SPACE, None, None), P(), P()),
        check_vma=False,
    )
```

```python
import functools

import jax
import jax.numpy as jnp
from jax import lax
from jax.experimental import pallas as pl
from jax.experimental.pallas import tpu as pltpu
from jax.sharding import Mesh
from jax.sharding import PartitionSpec as P

TILES = 64
LANES = 128
INNER_TAPS = ((1, 0), (1, 1), (1, 2), (2, 0), (2, 1), (2, 2), (0, 0))
OUTER_TAPS = ((0, 1), (0, 2))
SIZES = {"x": 4, "z": 8, "y": 4, "core": 2}
SPACE = ("x", "z")
REP = ("y", "core")


def whole():
    return pl.BlockSpec(memory_space=pltpu.VMEM)


def far():
    return pl.BlockSpec(memory_space=pl.ANY)


def room(x):
    return pltpu.VMEM(x.shape, x.dtype)


def scalars():
    return pl.BlockSpec(memory_space=pltpu.SMEM)


def params(mib=24):
    return pltpu.CompilerParams(vmem_limit_bytes=mib * 1024 * 1024)


def shifted(x, by):
    length = SIZES["x"] * SIZES["z"]
    pairs = [(i, i + by) for i in range(length) if 0 <= i + by < length]
    return lax.ppermute(x, SPACE, pairs)


def send_kernel(
    share_ref, cotangent_hbm, weight_hbm, preact_hbm, sent_hbm, weighted_hbm,
    cotangent_ref, weight_ref, preact_ref, weighted_ref, sent_ref, sems,
):
    pairs = ((preact_hbm, preact_ref), (weight_hbm, weight_ref), (cotangent_hbm, cotangent_ref))
    copies = [pltpu.make_async_copy(a, b, sems.at[n]) for n, (a, b) in enumerate(pairs)]
    for copy in copies:
        copy.start()
    devices, chunk, channels = sent_ref.shape
    chunk = chunk // 2
    rows, cols = preact_ref.shape[:2]
    band = cols // devices
    copies[0].wait()
    for i in range(rows):
        active = jnp.maximum(preact_ref[i].astype(jnp.float32), 0.0).reshape(devices, band, channels)
        sent_ref[:, chunk + i * band : chunk + (i + 1) * band, :] = active.astype(jnp.bfloat16)
    copies[1].wait()
    copies[2].wait()
    weighted = (cotangent_ref[...].astype(jnp.float32) * share_ref[0]).astype(jnp.bfloat16)
    weighted_ref[...] = weighted
    back = pltpu.make_async_copy(weighted_ref, weighted_hbm, sems.at[3])
    back.start()
    hidden = lax.dot_general(
        weighted, weight_ref[...], (((1,), (1,)), ((), ())), preferred_element_type=jnp.float32
    )
    sent_ref[:, :chunk, :] = hidden.reshape(devices, chunk, channels).astype(jnp.bfloat16)
    out = pltpu.make_async_copy(sent_ref, sent_hbm, sems.at[4])
    out.start()
    back.wait()
    out.wait()


def build_sent(share, cotangent, weight, preact, devices):
    rows, cols, channels = preact.shape
    sent = jax.ShapeDtypeStruct((devices, 2 * rows * cols // devices, channels), jnp.bfloat16)
    return pl.pallas_call(
        send_kernel,
        out_shape=(
            sent,
            jax.ShapeDtypeStruct(cotangent.shape, jnp.bfloat16),
        ),
        in_specs=[scalars()] + [far()] * 3,
        out_specs=(far(), far()),
        scratch_shapes=[room(x) for x in (cotangent, weight, preact, cotangent, sent)]
        + [pltpu.SemaphoreType.DMA((5,))],
        compiler_params=params(60),
        cost_estimate=pl.CostEstimate(flops=268 * 10**6, bytes_accessed=4 * 10**6, transcendentals=0),
        name="build_sent",
    )(share, cotangent, weight, preact)


def prepare_kernel(x_ref, out_ref, wide):
    half = out_ref.shape[2]
    first = lax.broadcasted_iota(jnp.int32, (LANES, half), 1) == 0
    for row in range(x_ref.shape[0]):
        for part in range(x_ref.shape[2] // LANES):
            lanes = slice(part * LANES, (part + 1) * LANES)
            wide[...] = x_ref[row, :, lanes].astype(jnp.float32)
            even = wide[pl.ds(0, half, stride=2), :].T
            odd = wide[pl.ds(1, half, stride=2), :].T
            late = jnp.where(first, 0.0, pltpu.roll(odd, 1, 1))
            out_ref[3 * row, lanes, :] = late.astype(jnp.bfloat16)
            out_ref[3 * row + 1, lanes, :] = even.astype(jnp.bfloat16)
            out_ref[3 * row + 2, lanes, :] = odd.astype(jnp.bfloat16)


def prepare(x):
    rows, cols, channels = x.shape
    return pl.pallas_call(
        prepare_kernel,
        out_shape=jax.ShapeDtypeStruct((3 * rows, channels, cols // 2), jnp.bfloat16),
        in_specs=[whole()],
        out_specs=whole(),
        scratch_shapes=[pltpu.VMEM((cols, LANES), jnp.float32)],
        compiler_params=params(),
        cost_estimate=pl.CostEstimate(flops=10**7, bytes_accessed=3 * 10**6, transcendentals=0),
        name="prepare",
    )(x)


def terms_kernel(
    core_ref, arrived_hbm, preact_hbm, above_hbm, blocks_hbm, weighted_hbm,
    own_inner, other_inner, own_outer, other_outer, grad_hbm, first_hbm,
    arrived_ref, preact_ref, above_ref, blocks_ref, weighted_ref,
    grad_ref, turned, inner_ref, outer_ref, sems,
):
    pairs = (
        (arrived_hbm, arrived_ref),
        (preact_hbm, preact_ref),
        (blocks_hbm, blocks_ref),
        (above_hbm, above_ref),
        (weighted_hbm, weighted_ref),
    )
    copies = [pltpu.make_async_copy(a, b, sems.at[n]) for n, (a, b) in enumerate(pairs)]
    for copy in copies:
        copy.start()
    devices, chunk, channels = arrived_ref.shape
    rows, cols = preact_ref.shape[:2]
    chunk, band = chunk // 2, cols // devices
    copies[0].wait()
    copies[1].wait()
    for i in range(rows):
        hidden = arrived_ref[:, i * band : (i + 1) * band, :].astype(jnp.float32).reshape(cols, channels)
        kept = jnp.where(preact_ref[i].astype(jnp.float32) > 0.0, hidden, 0.0)
        grad_ref[i] = kept.astype(jnp.bfloat16)
    back = [
        pltpu.make_async_copy(grad_ref, grad_hbm, sems.at[5]),
        pltpu.make_async_copy(grad_ref.at[0:1], first_hbm, sems.at[10]),
    ]
    active = arrived_ref[:, chunk:, :].astype(jnp.float32).reshape(devices * chunk, channels)
    turned[...] = active.T.astype(jnp.bfloat16)

    def half_taps(row_tap, col_tap, start):
        total = None
        for i in range(rows):
            row = 2 * i + row_tap - 1
            source, at = (above_ref, col_tap) if row < 0 else (blocks_ref, 3 * row + col_tap)
            term = jnp.dot(
                source[at, pl.ds(start, LANES), :], grad_ref[i], preferred_element_type=jnp.float32
            )
            total = term if total is None else total + term
        return total

    for copy in copies[2:]:
        copy.wait()
    back[0].start()
    back[1].start()
    for n, (inner_hbm, outer_hbm) in enumerate(((other_inner, other_outer), (own_inner, own_outer))):
        owner = core_ref[0] if n else 1 - core_ref[0]
        start = pl.multiple_of(owner * LANES, LANES)
        for at, (row_tap, col_tap) in enumerate(INNER_TAPS):
            inner_ref[n, at * LANES : (at + 1) * LANES, :] = half_taps(row_tap, col_tap, start)
        back.append(pltpu.make_async_copy(inner_ref.at[n], inner_hbm, sems.at[6 + 2 * n]))
        back[-1].start()
        for at, (row_tap, col_tap) in enumerate(OUTER_TAPS):
            outer_ref[n, at * LANES : (at + 1) * LANES, :] = half_taps(row_tap, col_tap, start)
        for k in range(weighted_ref.shape[1] // channels):
            at = (len(OUTER_TAPS) + k) * LANES
            outer_ref[n, at : at + LANES, :] = jnp.dot(
                turned[pl.ds(start, LANES), :],
                weighted_ref[:, k * channels : (k + 1) * channels],
                preferred_element_type=jnp.float32,
            )
        back.append(pltpu.make_async_copy(outer_ref.at[n], outer_hbm, sems.at[7 + 2 * n]))
        back[-1].start()
    for copy in back:
        copy.wait()


def terms(core, arrived, preact, above, blocks, weighted):
    rows, cols, channels = preact.shape
    inner = jax.ShapeDtypeStruct((len(INNER_TAPS) * LANES, channels), jnp.float32)
    outer = jax.ShapeDtypeStruct((len(OUTER_TAPS) * LANES + weighted.shape[1] // 2, channels), jnp.float32)
    return pl.pallas_call(
        terms_kernel,
        out_shape=(
            inner,
            inner,
            outer,
            outer,
            jax.ShapeDtypeStruct(preact.shape, jnp.bfloat16),
            jax.ShapeDtypeStruct((1, cols, channels), jnp.bfloat16),
        ),
        in_specs=[scalars()] + [far()] * 5,
        out_specs=(far(),) * 6,
        scratch_shapes=[room(x) for x in (arrived, preact, above, blocks, weighted, preact)]
        + [
            pltpu.VMEM((channels, weighted.shape[0]), jnp.bfloat16),
            pltpu.VMEM((2,) + inner.shape, jnp.float32),
            pltpu.VMEM((2,) + outer.shape, jnp.float32),
            pltpu.SemaphoreType.DMA((11,)),
        ],
        compiler_params=params(50),
        cost_estimate=pl.CostEstimate(flops=870 * 10**6, bytes_accessed=8 * 10**6, transcendentals=0),
        name="terms",
    )(core, arrived, preact, above, blocks, weighted)


def add_kernel(own, got, out_ref):
    out_ref[...] = own[...] + got[...]


def add(own, got):
    return pl.pallas_call(
        add_kernel,
        out_shape=jax.ShapeDtypeStruct(own.shape, own.dtype),
        in_specs=[whole()] * 2,
        out_specs=whole(),
        compiler_params=params(24),
        cost_estimate=pl.CostEstimate(flops=10**5, bytes_accessed=2 * 10**6, transcendentals=0),
        name="add",
    )(own, got)


def combine_kernel(where_ref, own, got, *out_refs):
    rows = out_refs[0].shape[0]
    for by, out_ref in enumerate(out_refs):
        at = pl.ds(pl.multiple_of(((where_ref[1] + by) & 3) * rows, 8), rows)
        out_ref[...] = own[at, :] + got[at, :]


def combine(where, own, got):
    chunk = jax.ShapeDtypeStruct((own.shape[0] // 4, own.shape[1]), jnp.float32)
    return pl.pallas_call(
        combine_kernel,
        out_shape=(chunk,) * 4,
        in_specs=[scalars()] + [whole()] * 2,
        out_specs=(whole(),) * 4,
        compiler_params=params(24),
        cost_estimate=pl.CostEstimate(flops=10**6, bytes_accessed=3 * 10**6, transcendentals=0),
        name="combine",
    )(where, own, got)


def input_kernel(grad_ref, below_ref, weight_ref, out_ref, wide):
    half = grad_ref.shape[1]
    last = lax.broadcasted_iota(jnp.int32, grad_ref.shape[1:], 0) == half - 1

    def early(g):
        moved = pltpu.roll(g.astype(jnp.float32), half - 1, 0)
        return jnp.where(last, 0.0, moved).astype(jnp.bfloat16)

    grads = [grad_ref[0], grad_ref[1], below_ref[0]]
    moved = [early(g) for g in grads]

    def times(g, row_tap, col_tap):
        return lax.dot_general(
            g,
            weight_ref[row_tap, col_tap],
            (((1,), (1,)), ((), ())),
            preferred_element_type=jnp.float32,
        )

    for row in range(4):
        i = row // 2
        terms = [(i, 1)] if row % 2 == 0 else [(i, 2), (i + 1, 0)]
        even = sum(times(grads[n], p, 1) for n, p in terms)
        odd = sum(times(grads[n], p, 2) + times(moved[n], p, 0) for n, p in terms)
        for part in range(even.shape[1] // LANES):
            lanes = slice(part * LANES, (part + 1) * LANES)
            wide[pl.ds(0, half, stride=2), :] = even[:, lanes]
            wide[pl.ds(1, half, stride=2), :] = odd[:, lanes]
            out_ref[row, :, lanes] = wide[...].astype(jnp.bfloat16)


def input_grad(grad, below, weight):
    rows, half, channels = grad.shape
    return pl.pallas_call(
        input_kernel,
        out_shape=jax.ShapeDtypeStruct((2 * rows, 2 * half, weight.shape[2]), jnp.bfloat16),
        in_specs=[whole()] * 3,
        out_specs=whole(),
        scratch_shapes=[pltpu.VMEM((2 * half, LANES), jnp.float32)],
        compiler_params=params(),
        cost_estimate=pl.CostEstimate(flops=604 * 10**6, bytes_accessed=3 * 10**6, transcendentals=0),
        name="input_grad",
    )(grad, below, weight)


def exchange(x, axis):
    return lax.all_to_all(x, axis, split_axis=0, concat_axis=0, tiled=True)


def place(axis, by=0):
    return (lax.axis_index(axis).astype(jnp.uint32) + jnp.uint32(by % SIZES[axis])) & jnp.uint32(SIZES[axis] - 1)


def pick(parts, index):
    zero = jnp.uint32(0)
    return lax.dynamic_slice(parts, (index, zero, zero), (1,) + parts.shape[1:])[0]


def put(parts, piece, index):
    zero = jnp.uint32(0)
    return lax.dynamic_update_slice(parts, piece[None], (index, zero, zero))


def rotated(x, axis, by):
    size = SIZES[axis]
    return lax.ppermute(x, axis, [(i, (i + by) % size) for i in range(size)])


def split(x):
    return x.reshape(4, x.shape[0] // 4, x.shape[1])


def swapped(x, axis, bit):
    return lax.ppermute(x, axis, [(i, i ^ bit) for i in range(SIZES[axis])])


def turned(x, by):
    pairs = []
    for i in range(SIZES["x"]):
        for k in range(SIZES["z"]):
            for j in range(SIZES["y"]):
                to = (i, (j + by) % 4) if k % 2 else ((i + by) % 4, j)
                pairs.append(((i * SIZES["z"] + k) * 4 + j, (to[0] * SIZES["z"] + k) * 4 + to[1]))
    return lax.ppermute(x, ("x", "z", "y"), pairs)


def turned_place(by=0):
    odd = (place("z") & jnp.uint32(1)) == 1
    return jnp.where(odd, place("y", by), place("x", by))


def spread_kernel(bit_ref, part, got, copies_ref, outer_ref):
    even = bit_ref[0] == 0
    first = jnp.where(even, part[...], got[...])
    for n in range(copies_ref.shape[0]):
        copies_ref[n] = first
    outer_ref[...] = jnp.where(even, got[...], part[...])[: outer_ref.shape[0], :]


def spread(bit, part, got, rows):
    return pl.pallas_call(
        spread_kernel,
        out_shape=(
            jax.ShapeDtypeStruct((4,) + part.shape, part.dtype),
            jax.ShapeDtypeStruct((rows, part.shape[1]), part.dtype),
        ),
        in_specs=[scalars()] + [whole()] * 2,
        out_specs=(whole(), whole()),
        compiler_params=params(24),
        cost_estimate=pl.CostEstimate(flops=0, bytes_accessed=2 * 10**6, transcendentals=0),
        name="spread",
    )(bit, part, got)


barrier = lax.optimization_barrier
STEPS = (1, 2, 3)


def total_sums(inner, outer, parts, scale, first, beside):
    inner, parts = exchange(split(inner), "y"), barrier(parts)
    moved = [rotated(p, "x", by) for p, by in zip(parts, STEPS)]
    inner, moved = barrier((inner, moved))
    inner = jnp.sum(inner, axis=0)
    outer = sum(moved, outer)

    rows = inner.shape[0] - outer.shape[0]
    both = jnp.stack([inner, jnp.pad(outer, ((0, rows), (0, 0)))])
    bit = place("z") & jnp.uint32(1)
    part = pick(both, bit) + swapped(pick(both, jnp.uint32(1) - bit), "z", 1)

    parts = split(part)
    moved, first = barrier(([pick(parts, turned_place(by)) for by in STEPS], first))
    moved = [turned(p, by) for p, by in zip(moved, STEPS)]
    below = shifted(first, -1)
    part = sum(moved, pick(parts, turned_place()))

    moved = [rotated(part, "z", by) for by in (2, 4, 6)]
    (two, four, six), beside = barrier((moved, beside(below)))
    part = ((part + four) + (two + six)) * scale

    whole_part = jnp.zeros((4,) + part.shape, part.dtype)
    for by in range(4):
        whole_part = put(whole_part, turned(part, by) if by else part, turned_place(-by))
    part = whole_part.reshape(-1, part.shape[1])
    got = swapped(part, "z", 1)
    copies, outer = spread(bit.astype(jnp.int32).reshape(1), part, got, part.shape[0] - rows)
    copies, moved = barrier((exchange(copies, "y"), [rotated(outer, "x", by) for by in STEPS]))
    return [copies.reshape(-1, part.shape[1])], [outer] + moved, beside


def assemble_kernel(where_ref, *refs):
    inner, pieces, (conv_ref, expand_ref, joined) = refs[:2], refs[2:10], refs[10:]
    channels = conv_ref.shape[2]
    core = where_ref[0]
    for by in range(4):
        rows = pieces[by].shape[0]
        at = pl.multiple_of(((where_ref[1] + 4 - by) & 3) * rows, 8)
        joined[core, pl.ds(at, rows), :] = pieces[by][...]
        joined[1 - core, pl.ds(at, rows), :] = pieces[4 + by][...]
    for at, (row_tap, col_tap) in enumerate(INNER_TAPS):
        rows, tap = slice(at * LANES, (at + 1) * LANES), 3 * row_tap + col_tap
        conv_ref[tap, pl.ds(pl.multiple_of(core * LANES, LANES), LANES), :] = inner[0][rows, :]
        conv_ref[tap, pl.ds(pl.multiple_of((1 - core) * LANES, LANES), LANES), :] = inner[1][rows, :]
    for half in range(2):
        lanes = slice(half * LANES, (half + 1) * LANES)
        for at, (row_tap, col_tap) in enumerate(OUTER_TAPS):
            conv_ref[3 * row_tap + col_tap, lanes, :] = joined[half, at * LANES : (at + 1) * LANES, :]
        for n in range(expand_ref.shape[1] // channels):
            at = (len(OUTER_TAPS) + n) * LANES
            expand_ref[lanes, n * channels : (n + 1) * channels] = joined[half, at : at + LANES, :]


def assemble(where, groups, channels, deep):
    refs = [piece for group in groups for piece in group]
    return pl.pallas_call(
        assemble_kernel,
        out_shape=(
            jax.ShapeDtypeStruct((9, channels, channels), jnp.float32),
            jax.ShapeDtypeStruct((channels, deep), jnp.float32),
        ),
        in_specs=[scalars()] + [whole()] * len(refs),
        out_specs=(whole(), whole()),
        scratch_shapes=[pltpu.VMEM((2, 4 * groups[1][0].shape[0], channels), jnp.float32)],
        compiler_params=params(),
        cost_estimate=pl.CostEstimate(flops=0, bytes_accessed=7 * 10**6, transcendentals=0),
        name="assemble",
    )(where, *refs)


def body(stem_input, stem_preact, deep_cotangent, tissue_tiles, conv_weight, expand_weight):
    _, out_rows, out_cols, channels = stem_preact.shape
    _, all_rows, band, deep = deep_cotangent.shape
    devices = SIZES["x"] * SIZES["z"]
    preact = stem_preact[0]
    cotangent = deep_cotangent[0].reshape(all_rows * band, deep)
    share = tissue_tiles.astype(jnp.float32) / TILES
    core = lax.axis_index("core").astype(jnp.int32)
    where = jnp.stack([core, lax.axis_index("x")]).astype(jnp.int32)

    sent, weighted = build_sent(share, cotangent, expand_weight, preact, devices)
    blocks = prepare(stem_input[0])
    above = prepare(shifted(stem_input[0, -1:], 1))
    arrived = exchange(sent, SPACE)
    own_inner, other_inner, own_outer, other_outer, grad, first = terms(
        where[:1], arrived, preact, above, blocks, weighted
    )

    samples_all = stem_input.shape[0] * SIZES["y"] * SIZES["core"]
    scale = float(samples_all * all_rows * out_cols) ** (-0.5)
    inner = add(own_inner, swapped(other_inner, "core", 1))
    outer, *parts = combine(where, own_outer, swapped(other_outer, "core", 1))
    inner, outer, grad_input = total_sums(
        inner, outer, parts, scale, first, lambda b: input_grad(grad, b, conv_weight)
    )
    groups = [pieces + [swapped(piece, "core", 1) for piece in pieces] for pieces in (inner, outer)]
    grad_conv, grad_expand = assemble(where, groups, channels, deep)
    return (grad_input[None], grad_conv.reshape(3, 3, channels, channels), grad_expand)


def solution(mesh):
    fine = Mesh(
        mesh.devices.reshape(SIZES["x"], SIZES["z"], SIZES["y"], SIZES["core"]),
        ("x", "z", "y", "core"),
    )
    return jax.shard_map(
        body,
        mesh=fine,
        in_specs=(
            P(REP, SPACE, None, None),
            P(REP, SPACE, None, None),
            P(REP, None, SPACE, None),
            P(REP),
            P(),
            P(),
        ),
        out_specs=(P(REP, SPACE, None, None), P(), P()),
        check_vma=False,
    )
```
